32 devices in a mesh: dp: 8 (over z, x), tensor: 4 (over y, core).
Axes of the slice: x: 2, y: 2, z: 4, core: 2. Of those that a mesh axis runs over, the one named last changes fastest.
Arguments:
- input_rows: bfloat16 [32768, 768], P(('dp', 'tensor')), may hold values from -6 to 6
- time_embed: bfloat16 [8, 768], P('dp'), may hold values from -4 to 4
- parents: int32 [8, 13], P('dp'), may hold values from 0 to 11, as said below
- qkv_weight: bfloat16 [768, 3, 768], P('dp', None, 'tensor'), may hold values from -0.21875 to 0.21875
- qv_bias: bfloat16 [2, 768], P(None, 'tensor'), may hold values from -0.59765625 to 0.59765625
- out_weight: bfloat16 [768, 768], P('tensor', 'dp'), may hold values from -3.5 to 3.5
- out_bias: bfloat16 [768], replicated, may hold values from -1.796875 to 1.796875
- inner_weight: bfloat16 [768, 3072], P('dp', 'tensor'), may hold values from -0.21875 to 0.21875
- inner_bias: bfloat16 [3072], P('tensor'), may hold values from -1.796875 to 1.796875
- outer_weight: bfloat16 [3072, 768], P('tensor', 'dp'), may hold values from -0.109375 to 0.109375
- outer_bias: bfloat16 [768], replicated, may hold values from -1.796875 to 1.796875
- norm_gain: bfloat16 [2, 768], replicated, may hold values from 0.5 to 1.5
- norm_shift: bfloat16 [2, 768], replicated, may hold values from -1.796875 to 1.796875
- cotangent: bfloat16 [32768, 768], P(('dp', 'tensor')), may hold values from -6 to 6
Outputs:
- block_out: bfloat16 [32768, 768], P(('dp', 'tensor'))
- input_grad: bfloat16 [32768, 768], P(('dp', 'tensor'))
- qkv_weight_grad: float32 [768, 3, 768], P('dp', None, 'tensor')
- qv_bias_grad: float32 [2, 768], P(None, 'tensor')
- out_weight_grad: float32 [768, 768], P('tensor', 'dp')
- out_bias_grad: float32 [768], replicated
- inner_weight_grad: float32 [768, 3072], P('dp', 'tensor')
- inner_bias_grad: float32 [3072], P('tensor')
- outer_weight_grad: float32 [3072, 768], P('tensor', 'dp')
- outer_bias_grad: float32 [768], replicated
- norm_gain_grad: float32 [2, 768], replicated
- norm_shift_grad: float32 [2, 768], replicated
The draws below stay inside these ranges and needn't reach their ends.
Inputs may be any that keep to these rules, and one draw needn't show every extreme that they name: `parents`: segment 0 is the trunk, positions 0 to 1023 of a tree, and its entry is 0; segment s >= 1 is block 4 + s - 1, and its entry is smaller than s.
All inputs are finite; a program needn't handle non-finite values.
Results may differ from the reference program's by a relative error of at most 0.02.
Values may be sent and summed in bfloat16 or wider, within the bound.
A program may use at most 256 MiB of HBM per device.

```python
import math
import jax
import jax.numpy as jnp
from jax import lax

D = 768
HEADS = 12
HEAD_DIM = 64
FF = 3072
TRUNK_BLOCKS = 4
BLOCK = 256
QBLK = 512
SEGS = 13
SEQ = 4096
TREES = 8
TOKENS = 32768


def draw_parents(key, part):
    seg_ids = jnp.arange(SEGS, dtype=jnp.int32)
    raw_bits = jax.random.randint(key, (TREES, SEGS), 0, 1 << 20, dtype=jnp.int32)
    picks = raw_bits % jnp.maximum(seg_ids, 1)[None, :]
    return jnp.where(seg_ids[None, :] == SEGS - 1, SEGS - 2, picks).astype(jnp.int32)


def with_spikes(array, stream_key, source, target, blocks, factor):
    def block_of(position):
        return (jnp.arange(array.shape[position]) // (array.shape[position] // blocks)).reshape((-1,) + (1,) * (array.ndim - 1 - position))

    near = jax.random.permutation(stream_key, blocks)[block_of(target)]
    other_side = (block_of(target) + blocks // 2) % blocks
    return jnp.where((block_of(source) == near) | (block_of(source) == other_side), factor * array, array)


def level_of(rng, shape, cuts, least, largest):
    def one(dim, shards_of):
        steps = jax.random.uniform(jax.random.fold_in(jax.random.fold_in(rng, 6), dim), (shards_of,), jnp.float32, least / len(cuts), largest / len(cuts))
        return jnp.repeat(jnp.exp(steps), shape[dim] // shards_of).reshape((-1,) + (1,) * (len(shape) - dim - 1))

    level = one(*cuts[0])
    for cut in cuts[1:]:
        level = level * one(*cut)
    return level


def bell_draw(key, shape, width, bound, cuts=(), kind=jnp.bfloat16):
    values = jax.random.normal(key, shape, jnp.float32) * width
    if len(cuts) > 0:
        values = level_of(key, shape, cuts, -0.22, 0.18) * values
    return jnp.clip(values, min=-bound, max=bound).astype(kind)


def noise_with(own_key, extent, deviation, most, cuts, heavy, kind=jnp.bfloat16):
    values = deviation * jax.random.normal(own_key, extent, jnp.float32)
    if cuts:
        values = values * level_of(own_key, extent, cuts, -0.22, 0.18)
    return jnp.clip(with_spikes(values, jax.random.fold_in(own_key, 3), *heavy), -most, most).astype(kind)


def setup_inputs(seed: int = 0) -> dict:
    key_list = jax.random.split(jax.random.key(seed), 15)
    return {
        "input_rows": noise_with(key_list[0], (TOKENS, D), 1.0, 6.0, ((0, 32),), (0, 1, 32, 2.75)),
        "time_embed": bell_draw(key_list[1], (TREES, D), 0.5, 4.0, ((0, 8),)),
        "parents": draw_parents(jax.random.fold_in(key_list[14], 71), 0),
        "qkv_weight": bell_draw(key_list[3], (D, 3, D), D ** -0.5, 0.21875, ((0, 8), (2, 4))),
        "qv_bias": bell_draw(key_list[4], (2, D), 0.1, 0.59765625, ((1, 4),)),
        "out_weight": bell_draw(key_list[5], (D, D), (max(2, D // 256)) ** -0.5, 3.5, ((0, 4), (1, 8))),
        "out_bias": bell_draw(key_list[6], (D,), 0.3, 1.796875),
        "inner_weight": bell_draw(key_list[7], (D, FF), D ** -0.5, 0.21875, ((0, 8), (1, 4))),
        "inner_bias": bell_draw(key_list[8], (FF,), 0.3, 1.796875, ((0, 4),)),
        "outer_weight": bell_draw(key_list[9], (FF, D), FF ** -0.5, 0.109375, ((0, 4), (1, 8))),
        "outer_bias": bell_draw(key_list[10], (D,), 0.3, 1.796875),
        "norm_gain": jnp.clip(1.0 + 0.1 * jax.random.normal(key_list[11], (2, D), jnp.float32), 0.5, 1.5).astype(jnp.bfloat16),
        "norm_shift": bell_draw(key_list[12], (2, D), 0.3, 1.796875),
        "cotangent": noise_with(key_list[13], (TOKENS, D), 1.0, 6.0, ((0, 32),), (0, 1, 32, 2.75)),
    }


epsilon = 1e-05
root_half = 0.7071067811865476
far_below = -1e+30

@jax.custom_vjp
def low(v):
    return lax.optimization_barrier(v.astype(jnp.bfloat16)).astype(jnp.float32)

@jax.custom_vjp
def low_back(v):
    return v

def low_keep(v):
    return (low(v), None)

def low_pass(kept, grad):
    return (grad,)

def back_keep(v):
    return (v, None)

def back_low(kept, grad):
    return (low(grad),)
low.defvjp(low_keep, low_pass)
low_back.defvjp(back_keep, back_low)

def layer_norm(summed, gain_row, shift_row):
    centre = lax.optimization_barrier(jnp.mean(summed, axis=-1, keepdims=True))
    offset = summed - centre
    inv_std = lax.rsqrt(lax.optimization_barrier(jnp.mean(offset * offset, axis=-1, keepdims=True)) + epsilon)
    return offset * inv_std * gain_row + shift_row

def gelu_value(pre_act):
    return 0.5 * pre_act * (1.0 + lax.erf(pre_act * root_half))

def block_sight(parent_row):
    seg_ids = jnp.arange(SEGS, dtype=jnp.int32)
    step_up = parent_row[:, None] == seg_ids[None, :]
    identity_mat = seg_ids[:, None] == seg_ids[None, :]
    ancestry = identity_mat
    for repeat_step in range(SEGS):
        reached = jnp.any(jnp.logical_and(step_up[:, :, None], ancestry[None, :, :]), axis=1)
        ancestry = jnp.logical_or(identity_mat, reached)
    block_ids = jnp.arange(SEQ // BLOCK, dtype=jnp.int32)
    segment_of = jnp.maximum(block_ids - TRUNK_BLOCKS + 1, 0).astype(jnp.int32)
    row_pick = jnp.take(ancestry, segment_of, axis=0)
    return jnp.take(row_pick, segment_of, axis=1)

def attend_tree(queries, key_rows, value_rows, sight_map):
    scale_factor = 1.0 / math.sqrt(HEAD_DIM)
    span_count = QBLK // BLOCK

    def one_block(block_index):
        query_block = lax.dynamic_slice_in_dim(queries, block_index * QBLK, QBLK, 0)
        sight_rows = lax.dynamic_slice_in_dim(sight_map, block_index * span_count, span_count, 0)
        seen_mask = jnp.repeat(jnp.repeat(sight_rows, BLOCK, axis=0), BLOCK, axis=1)
        raw_scores = jnp.einsum('qhd,khd->hqk', query_block, key_rows, precision=lax.Precision.HIGHEST) * scale_factor
        scores = low_back(jnp.where(seen_mask[None], raw_scores, far_below))
        probs_low = low(jax.nn.softmax(scores, axis=-1))
        return jnp.einsum('hqk,khd->qhd', probs_low, value_rows, precision=lax.Precision.HIGHEST)
    blocks = lax.map(jax.checkpoint(one_block), jnp.arange(SEQ // QBLK, dtype=jnp.int32))
    return blocks.reshape(SEQ, HEADS * HEAD_DIM)

def reference(input_rows, time_embed, parents, qkv_weight, qv_bias, out_weight, out_bias, inner_weight, inner_bias, outer_weight, outer_bias, norm_gain, norm_shift, cotangent):
    sight_maps = lax.map(block_sight, parents)
    embed_rows = time_embed.astype(jnp.float32)

    def forward(rows_input, qkv_float, qv_float, out_float, out_shift, inner_float, inner_shift, outer_float, outer_shift, gain_rows, shift_rows):

        def one_tree(pieces):
            tree_rows, tree_embed, sight_map = pieces
            start_sum = tree_rows + tree_embed[None, :]
            start_low = low(start_sum)
            projected = jnp.einsum('sd,dcf->scf', start_low, qkv_float, precision=lax.Precision.HIGHEST)
            queries = low(low_back(projected[:, 0] + qv_float[0])).reshape(SEQ, HEADS, HEAD_DIM)
            key_rows = low(low_back(projected[:, 1])).reshape(SEQ, HEADS, HEAD_DIM)
            value_rows = low(low_back(projected[:, 2] + qv_float[1])).reshape(SEQ, HEADS, HEAD_DIM)
            mixed_heads = low(low_back(attend_tree(queries, key_rows, value_rows, sight_map)))
            attn_out = low_back(jnp.dot(mixed_heads, out_float, precision=lax.Precision.HIGHEST) + out_shift)
            hidden = layer_norm(start_sum + attn_out, gain_rows[0], shift_rows[0])
            hidden_low = low(hidden)
            pre_act = low_back(jnp.dot(hidden_low, inner_float, precision=lax.Precision.HIGHEST) + inner_shift)
            act_low = low(gelu_value(pre_act))
            mlp_out = low_back(jnp.dot(act_low, outer_float, precision=lax.Precision.HIGHEST) + outer_shift)
            return layer_norm(hidden + mlp_out, gain_rows[1], shift_rows[1])
        tree_out = lax.map(jax.checkpoint(one_tree), (rows_input.reshape(TREES, SEQ, D), embed_rows, sight_maps))
        return tree_out.reshape(TREES * SEQ, D)
    float_args = tuple((item.astype(jnp.float32) for item in (input_rows, qkv_weight, qv_bias, out_weight, out_bias, inner_weight, inner_bias, outer_weight, outer_bias, norm_gain, norm_shift)))
    result, pullback = jax.vjp(forward, *float_args)
    gradients = pullback(cotangent.astype(jnp.float32))
    return (result.astype(jnp.bfloat16), gradients[0].astype(jnp.bfloat16), gradients[1], gradients[2], gradients[3], gradients[4], gradients[5], gradients[6], gradients[7], gradients[8], gradients[9], gradients[10])
```

```python
import functools
import math

import jax
import jax.numpy as jnp
from jax import lax
from jax.experimental import pallas as pl
from jax.experimental.pallas import tpu as pltpu
from jax.sharding import PartitionSpec as P

bf=jnp.bfloat16; f32=jnp.float32
LOG2E=1.4426950408889634
BLK=256; TRUNK=1024; NB=16; HD=64; HN=3

def _masked(t, h):
    z=jnp.zeros((HD,t.shape[1]),t.dtype)
    if h==0: return jnp.concatenate([t,z],0)
    if h==1: return jnp.concatenate([z,t],0)
    return t
def _lanes(h): return slice(0,128) if h<2 else slice(128,192)

def fwd_kernel(path_ref, cnt_ref, qt_ref, k_ref, vt_ref, o_ref, lse_ref, m_s, acc_s):
    def qblock(i, _):
        qs=pl.ds(pl.multiple_of(i*BLK,BLK),BLK)
        qm=[_masked(qt_ref[h*HD:(h+1)*HD,qs],h) for h in range(HN)]
        for h in range(HN):
            s=jnp.dot(k_ref[0:TRUNK,_lanes(h)],qm[h],preferred_element_type=f32)*LOG2E
            m=jnp.max(s,axis=0,keepdims=True)
            p=jnp.exp2(s-m).astype(bf)
            acc_s[h]=jnp.dot(vt_ref[h,:,0:TRUNK],p,preferred_element_type=f32)
            m_s[h:h+1]=m
        def step(j,_):
            kb=path_ref[i,j]
            ks=pl.ds(pl.multiple_of(kb*BLK,BLK),BLK)
            for h in range(HN):
                s=jnp.dot(k_ref[ks,_lanes(h)],qm[h],preferred_element_type=f32)*LOG2E
                mo=m_s[h:h+1]
                m=jnp.maximum(mo,jnp.max(s,axis=0,keepdims=True))
                al=jnp.exp2(mo-m)
                p=jnp.exp2(s-m).astype(bf)
                acc_s[h]=acc_s[h]*al+jnp.dot(vt_ref[h,:,ks],p,preferred_element_type=f32)
                m_s[h:h+1]=m
            return 0
        lax.fori_loop(0,cnt_ref[i],step,0)
        for h in range(HN):
            l=acc_s[h,HD:HD+1,:]
            o_ref[h*HD:(h+1)*HD,qs]=acc_s[h,0:HD,:]/l
            lse_ref[h:h+1,qs]=m_s[h:h+1]+jnp.log2(l)
        return 0
    lax.fori_loop(0,NB,qblock,0)

def attn_fwd(path,cnt,qt,k,vt):
    S=qt.shape[1]
    vm=pl.BlockSpec(memory_space=pltpu.VMEM); sm=pl.BlockSpec(memory_space=pltpu.SMEM)
    return pl.pallas_call(fwd_kernel,
        out_shape=(jax.ShapeDtypeStruct((HN*HD,S),f32),jax.ShapeDtypeStruct((8,S),f32)),
        in_specs=[sm,sm,vm,vm,vm],out_specs=(vm,vm),
        scratch_shapes=[pltpu.VMEM((8,BLK),f32),pltpu.VMEM((HN,80,BLK),f32)],
        compiler_params=pltpu.CompilerParams(vmem_limit_bytes=48<<20),
        name="tree_attention",
    )(path,cnt,qt,k,vt)

def bwd_kernel(path_ref,cnt_ref,qt_ref,k_ref,v_ref,kt_ref,dot_ref,o_ref,lse_ref,dqt_ref,dk_ref,dv_ref,dq_s):
    nt=(((1,),(1,)),((),()))
    dk_ref[...]=jnp.zeros_like(dk_ref); dv_ref[...]=jnp.zeros_like(dv_ref)
    def qblock(i,_):
        qs=pl.ds(pl.multiple_of(i*BLK,BLK),BLK)
        qm=[_masked(qt_ref[h*HD:(h+1)*HD,qs],h) for h in range(HN)]
        dt=[dot_ref[h*HD:(h+1)*HD,qs] for h in range(HN)]
        dm=[_masked(dt[h],h) for h in range(HN)]
        delta=[jnp.sum(dt[h].astype(f32)*o_ref[h*HD:(h+1)*HD,qs],axis=0,keepdims=True) for h in range(HN)]
        lse=[lse_ref[h:h+1,qs] for h in range(HN)]
        def keys(ks,first):
            ps=[];ds=[]
            for h in range(HN):
                s=jnp.dot(k_ref[ks,_lanes(h)],qm[h],preferred_element_type=f32)*LOG2E
                p=jnp.exp2(s-lse[h])
                dp=jnp.dot(v_ref[ks,_lanes(h)],dm[h],preferred_element_type=f32)
                d=(p*(dp-delta[h])).astype(bf)
                ps.append(p.astype(bf)); ds.append(d)
                g=jnp.dot(kt_ref[h*HD:(h+1)*HD,ks],d,preferred_element_type=f32)
                if first: dq_s[h]=g
                else: dq_s[h]+=g
            dv_ref[ks,0:128]+=lax.dot_general(jnp.concatenate(ps[:2],1),jnp.concatenate(dm[:2],1),nt,preferred_element_type=f32)
            dk_ref[ks,0:128]+=lax.dot_general(jnp.concatenate(ds[:2],1),jnp.concatenate(qm[:2],1),nt,preferred_element_type=f32)
            dv_ref[ks,128:192]+=lax.dot_general(ps[2],dm[2],nt,preferred_element_type=f32)
            dk_ref[ks,128:192]+=lax.dot_general(ds[2],qm[2],nt,preferred_element_type=f32)
        for t in range(TRUNK//TCH):
            keys(slice(t*TCH,(t+1)*TCH),t==0)
        def step(j,_):
            kb=path_ref[i,j]
            keys(pl.ds(pl.multiple_of(kb*BLK,BLK),BLK),False)
            return 0
        lax.fori_loop(0,cnt_ref[i],step,0)
        for h in range(HN):
            dqt_ref[h*HD:(h+1)*HD,qs]=(dq_s[h]*0.125).astype(bf)
        return 0
    lax.fori_loop(0,NB,qblock,0)
TCH=512
def attn_bwd(path,cnt,qt,k,v,kt,dot,o,lse):
    S=qt.shape[1]
    vm=pl.BlockSpec(memory_space=pltpu.VMEM); sm=pl.BlockSpec(memory_space=pltpu.SMEM)
    return pl.pallas_call(bwd_kernel,
        out_shape=(jax.ShapeDtypeStruct((HN*HD,S),bf),jax.ShapeDtypeStruct((S,HN*HD),f32),jax.ShapeDtypeStruct((S,HN*HD),f32)),
        in_specs=[sm,sm]+[vm]*7,out_specs=(vm,vm,vm),
        scratch_shapes=[pltpu.VMEM((HN,HD,BLK),f32)],
        compiler_params=pltpu.CompilerParams(vmem_limit_bytes=56<<20),
        name="tree_attention_grad",
    )(path,cnt,qt,k,v,kt,dot,o,lse)

def path_tables(parent):
    segs=parent.shape[0]
    seg=jnp.maximum(jnp.arange(NB)-3,0).astype(jnp.int32)
    cols=[];cnt=jnp.zeros((NB,),jnp.int32);cur=seg
    for _ in range(segs-1):
        cols.append(jnp.maximum(cur+3,0)); cnt=cnt+(cur>0)
        nxt=jnp.sum(jnp.where(cur[:,None]==jnp.arange(segs)[None,:],parent[None,:],0),axis=1).astype(jnp.int32)
        cur=jnp.where(cur>0,nxt,0)
    return jnp.stack(cols,1),cnt


D = 768
SEQ = 4096
ROWS = SEQ // 4
QW = HN * HD
FQ = 768
epsilon = 1e-05
root_half = 0.7071067811865476
inv_root_tau = 0.3989422804014327


def layer_norm(summed, gain_row, shift_row):
    centre = jnp.mean(summed, axis=-1, keepdims=True)
    offset = summed - centre
    inv_std = lax.rsqrt(jnp.mean(offset * offset, axis=-1, keepdims=True) + epsilon)
    normed = offset * inv_std
    return normed * gain_row + shift_row, normed, inv_std


def norm_back(grad_out, normed, inv_std, gain_row):
    scaled = grad_out * gain_row
    return inv_std * (
        scaled
        - jnp.mean(scaled, axis=-1, keepdims=True)
        - normed * jnp.mean(scaled * normed, axis=-1, keepdims=True)
    )


def gelu_parts(u):
    half = 0.5 * (1.0 + lax.erf(u * root_half))
    return u * half, half + u * inv_root_tau * jnp.exp(-0.5 * u * u)


def partner(x, mask):
    return lax.ppermute(x, "tensor", [(i, i ^ mask) for i in range(4)])


def on_device(
    input_rows, time_embed, parents, qkv_weight, qv_bias, out_weight, out_bias, inner_weight,
    inner_bias, outer_weight, outer_bias, norm_gain, norm_shift, cotangent,
):
    rank = lax.axis_index("tensor")
    part = qkv_weight.shape[0]
    wide = dict(preferred_element_type=f32)

    start_sum = input_rows.astype(f32) + time_embed.astype(f32)
    start_low = start_sum.astype(bf)
    across = partner(start_low, 2)
    both = partner(jnp.stack([start_low, across]), 1)
    whole = jnp.zeros((SEQ, D), bf)
    for m, piece in ((0, start_low), (2, across), (1, both[0]), (3, both[1])):
        whole = lax.dynamic_update_slice_in_dim(whole, piece, (rank ^ m) * ROWS, 0)

    qkv_all = lax.all_gather(qkv_weight.reshape(part, 3 * QW), "dp", axis=0, tiled=True)
    packed = jnp.concatenate([inner_weight, outer_weight.T, out_weight.T], axis=1)
    packed = lax.all_gather(packed, "dp", axis=0, tiled=True)
    packed = lax.all_gather(packed, "tensor", axis=0, tiled=False)

    bias = qv_bias.astype(f32)
    wq, wk, wv = (qkv_all[:, i * QW:(i + 1) * QW] for i in range(3))
    tr = lambda w: lax.dot_general(w, whole, (((0,), (1,)), ((), ())), **wide)
    qt = ((tr(wq) + bias[0][:, None]).astype(bf).astype(f32) * 0.125).astype(bf)
    k = jnp.dot(whole, wk, **wide).astype(bf)
    v = (jnp.dot(whole, wv, **wide) + bias[1]).astype(bf)
    kt, vt = k.T, v.T
    vt_ext = jnp.concatenate(
        [vt.reshape(HN, HD, SEQ), jnp.ones((HN, 1, SEQ), bf), jnp.zeros((HN, 15, SEQ), bf)], 1)
    path, cnt = path_tables(parents[0])
    ot, lse = attn_fwd(path, cnt, qt, k, vt_ext)
    mix_low = ot.astype(bf)

    def to_tokens(x):
        out = jnp.zeros((D, ROWS), bf)
        for m in range(4):
            piece = lax.dynamic_slice_in_dim(x, (rank ^ m) * ROWS, ROWS, 1)
            piece = partner(piece, m) if m else piece
            out = lax.dynamic_update_slice_in_dim(out, piece, (rank ^ m) * QW, 0)
        return out

    def to_heads(x):
        out = jnp.zeros((QW, SEQ), bf)
        for m in range(4):
            piece = lax.dynamic_slice_in_dim(x, (rank ^ m) * QW, QW, 0)
            piece = partner(piece, m) if m else piece
            out = lax.dynamic_update_slice_in_dim(out, piece, (rank ^ m) * ROWS, 1)
        return out

    mixed = to_tokens(mix_low)
    inner = [packed[t, :, :FQ] for t in range(4)]
    outer_t = [packed[t, :, FQ:2 * FQ] for t in range(4)]
    out_t = jnp.concatenate([packed[t, :, 2 * FQ:] for t in range(4)], axis=1)
    bias_in = lax.all_gather(inner_bias, "tensor", axis=0, tiled=False).astype(f32)
    gain, shift = norm_gain.astype(f32), norm_shift.astype(f32)

    attn_out = lax.dot_general(mixed, out_t, (((0,), (1,)), ((), ())), **wide) + out_bias.astype(f32)
    hidden, normed1, inv1 = layer_norm(start_sum + attn_out, gain[0], shift[0])
    hidden_low = hidden.astype(bf)
    acts, slopes = [], []
    mlp = outer_bias.astype(f32)
    for t in range(4):
        u = jnp.dot(hidden_low, inner[t], **wide) + bias_in[t]
        value, slope = gelu_parts(u)
        acts.append(value.astype(bf))
        slopes.append(slope)
        mlp = mlp + jnp.einsum("tf,df->td", acts[t], outer_t[t], **wide)
    final, normed2, inv2 = layer_norm(hidden + mlp, gain[1], shift[1])
    block_out = final.astype(bf)

    grad_final = cotangent.astype(f32)
    gain2 = jnp.sum(grad_final * normed2, axis=0)
    shift2 = jnp.sum(grad_final, axis=0)
    grad2 = norm_back(grad_final, normed2, inv2, gain[1])
    gm = grad2.astype(bf)
    outer_bias_sum = jnp.sum(gm, axis=0, dtype=f32)
    gin = grad2
    inner_sums, grads = [], []
    for t in range(4):
        gp = (jnp.dot(gm, outer_t[t], **wide) * slopes[t]).astype(bf)
        inner_sums.append(jnp.sum(gp, axis=0, dtype=f32))
        gin = gin + jnp.einsum("tf,df->td", gp, inner[t], **wide)
        dinner = jnp.einsum("td,tf->df", hidden_low, gp, **wide)
        douter = jnp.einsum("td,tf->df", gm, acts[t], **wide)
        grads.append([dinner.astype(bf), douter.astype(bf)])
    gain1 = jnp.sum(gin * normed1, axis=0)
    shift1 = jnp.sum(gin, axis=0)
    grad1 = norm_back(gin, normed1, inv1, gain[0])
    ga = grad1.astype(bf)
    out_bias_sum = jnp.sum(ga, axis=0, dtype=f32)
    dout = jnp.einsum("td,ct->dc", ga, mixed, **wide).astype(bf)
    for t in range(4):
        grads[t] = jnp.concatenate(grads[t] + [dout[:, t * QW:(t + 1) * QW]], axis=1)
    share = lax.psum_scatter(jnp.stack(grads), "tensor", scatter_dimension=0, tiled=False)
    share = lax.psum_scatter(share, "dp", scatter_dimension=0, tiled=True).astype(f32)

    do_t = to_heads(jnp.einsum("dc,td->ct", out_t, ga, **wide).astype(bf))
    dqt, dk, dv = attn_bwd(path, cnt, qt, k, v, kt, do_t, ot, lse)
    dq = dqt.T
    dk, dv = dk.astype(bf), dv.astype(bf)
    grad_proj = jnp.concatenate([dq, dk, dv], axis=1)
    dqkv = jnp.einsum("td,tf->df", whole, grad_proj, **wide).astype(bf)
    qkv_share = lax.psum_scatter(dqkv, "dp", scatter_dimension=0, tiled=True).astype(f32)
    partial = jnp.einsum("tf,df->td", grad_proj, qkv_all, **wide).astype(bf).reshape(4, ROWS, D)
    take = lambda i: lax.dynamic_index_in_dim(partial, i, 0, keepdims=False)
    got = partner(jnp.stack([take(rank ^ 1), take(rank ^ 3)]), 1).astype(f32)
    far = partner((take(rank ^ 2).astype(f32) + got[1]).astype(bf), 2).astype(f32)
    input_grad = (take(rank).astype(f32) + got[0] + far + grad1).astype(bf)

    pair = jnp.stack([jnp.sum(dq, axis=0, dtype=f32), jnp.sum(dv, axis=0, dtype=f32)])
    pair = lax.dynamic_update_slice_in_dim(jnp.zeros((2, D), f32), pair, rank * QW, 1)
    sums = lax.psum(
        jnp.concatenate(
            [pair, jnp.stack(inner_sums), jnp.stack([out_bias_sum, outer_bias_sum, gain1, gain2, shift1, shift2])]),
        ("dp", "tensor"))
    return (
        block_out,
        input_grad,
        qkv_share.reshape(part, 3, QW),
        lax.dynamic_slice_in_dim(sums[:2], rank * QW, QW, 1),
        share[:, 2 * FQ:].T,
        sums[6],
        share[:, :FQ],
        lax.dynamic_index_in_dim(sums[2:6], rank, 0, keepdims=False),
        share[:, FQ:2 * FQ].T,
        sums[7],
        sums[8:10],
        sums[10:12],
    )


def solution(mesh):
    both = P(("dp", "tensor"), None)
    return jax.shard_map(
        on_device,
        mesh=mesh,
        in_specs=(
            both, P("dp", None), P("dp", None), P("dp", None, "tensor"), P(None, "tensor"),
            P("tensor", "dp"), P(), P("dp", "tensor"), P("tensor"), P("tensor", "dp"), P(), P(), P(), both,
        ),
        out_specs=(
            both, both, P("dp", None, "tensor"), P(None, "tensor"), P("tensor", "dp"), P(),
            P("dp", "tensor"), P("tensor"), P("tensor", "dp"), P(), P(), P(),
        ),
        check_vma=False,
    )
```

```python
import functools
import jax, jax.numpy as jnp
from jax import lax
from jax.experimental import pallas as pl
from jax.experimental.pallas import tpu as pltpu
from jax.sharding import PartitionSpec as P
bf = jnp.bfloat16
f32 = jnp.float32
BLK = 256
TRUNK = 1024
NB = 16
HD = 64
HN = 3
SEGS = 13
PAD = 4
LIST = 192
TQ = 512
TK = 1024
FP = 4
BP = 4
BTQ = 1024
BTK = 256
VM = pl.BlockSpec(memory_space=pltpu.VMEM)
SM = pl.BlockSpec(memory_space=pltpu.SMEM)
HB = pl.BlockSpec(memory_space=pltpu.HBM)
NT = (((1,), (1,)), ((), ()))


def mm(a, b, dims=(((1,), (0,)), ((), ()))):
    return lax.dot_general(a, b, dims, preferred_element_type=f32)


def aligned(i, n):
    return pl.ds(pl.multiple_of(i * n, n), n)


def list_pairs(parents, cur, pairs):
    for s in range(1, SEGS):
        cur[s] = jnp.int32(s)

    def level(_, n):
        for s in range(1, SEGS):
            c = cur[s]
            pairs[0, n] = jnp.int32(s + 3)
            pairs[1, n] = c + 3
            cur[s] = jnp.where(c > 0, parents[c], 0)
            n = n + jnp.where(c > 0, 1, 0)
        for i in range(PAD - 1):
            pairs[0, n + i] = jnp.int32(NB)
            pairs[1, n + i] = jnp.int32(NB)
        return (n + PAD - 1) // PAD * PAD

    pairs[2, 0] = lax.fori_loop(0, SEGS - 1, level, jnp.int32(0))


PR = 1024


def fwd_kernel(parents, tab, x_hbm, w_hbm, b_ref, qt_hbm, kv_hbm, kt_hbm, o_hbm, mix_hbm, lse_ref, pairs,
               cur, m_s, acc_s, xs, w_s, wt_s, wr_s, br_s, qt_ref, kv_ref, kt_ref, vt_ref, o_ref, mix_ref, sem):
    def fetch(i, slot):
        return pltpu.make_async_copy(x_hbm.at[i], xs.at[slot], sem.at[slot])

    load_w = pltpu.make_async_copy(w_hbm, w_s, sem.at[2])
    load_w.start()
    fetch(0, 0).start()
    list_pairs(parents, cur, pairs)
    load_w.wait()
    bias = b_ref[...]
    w = w_s[...].reshape(w_s.shape[0] * w_s.shape[1], w_s.shape[2])
    wt_s[...] = w.T
    for h in range(HN):
        for c in (1, 2):
            to = slice(h * 128 + (c - 1) * HD, h * 128 + c * HD)
            wr_s[:, to] = w[:, c * HN * HD + h * HD:c * HN * HD + (h + 1) * HD]
            part = bias[:, HN * HD + h * HD:HN * HD + (h + 1) * HD] if c == 2 else jnp.zeros((1, HD), f32)
            br_s[:, to] = jnp.broadcast_to(part, (8, HD))
    bias_col = jnp.transpose(jnp.broadcast_to(bias, (8, 2 * HN * HD)))
    ones = (lax.broadcasted_iota(jnp.int32, (16, PR), 0) == 0).astype(f32).astype(bf)

    def rows(i, _):
        slot = lax.rem(i, 2)

        @pl.when(i + 1 < NB * BLK // PR)
        def _():
            fetch(i + 1, 1 - slot).start()

        fetch(i, slot).wait()
        cols = aligned(i, PR)
        x = xs[slot]
        up = mm(wt_s[...], x, NT)
        q = (up[:HN * HD] + bias_col[:HN * HD, 0:1]).astype(bf)
        qt_ref[:, cols] = (q.astype(f32) * 0.125).astype(bf)
        kt_ref[:, cols] = up[HN * HD:2 * HN * HD].astype(bf)
        vt = (up[2 * HN * HD:] + bias_col[HN * HD:, 0:1]).astype(bf)
        for h in range(HN):
            vt_ref[h, :HD, cols] = vt[h * HD:(h + 1) * HD]
            vt_ref[h, HD:, cols] = ones
        kv_ref[cols] = (mm(x, wr_s[...]) + br_s[0:1]).astype(bf)
        return 0

    lax.fori_loop(0, NB * BLK // PR, rows, 0)
    saves = [pltpu.make_async_copy(a, b, sem.at[3 + n])
             for n, (a, b) in enumerate(((qt_ref, qt_hbm), (kv_ref, kv_hbm), (kt_ref, kt_hbm)))]
    for c in saves:
        c.start()
    zero = jnp.zeros((HD, TQ), bf)

    def tile(i, _):
        qz = [jnp.concatenate([qt_ref[h * HD:(h + 1) * HD, aligned(i, TQ)], zero], 0) for h in range(HN)]
        m, acc = [None] * HN, [None] * HN
        for c in range(TRUNK // TK):
            ks = slice(c * TK, (c + 1) * TK)
            s = [mm(kv_ref[ks, h * 128:(h + 1) * 128], qz[h]) for h in range(HN)]
            new = [jnp.max(x, axis=0, keepdims=True) for x in s]
            if c:
                new = [jnp.maximum(x, y) for x, y in zip(m, new)]
            p = [jnp.exp(x - y).astype(bf) for x, y in zip(s, new)]
            a = [mm(vt_ref[h, :, ks], p[h]) for h in range(HN)]
            if c:
                a = [x * jnp.exp(y - z) + w for x, y, z, w in zip(acc, m, new, a)]
            m, acc = new, a
        for h in range(HN):
            for j in range(TQ // BLK):
                acc_s[i * (TQ // BLK) + j, h] = acc[h][:, j * BLK:(j + 1) * BLK]
                m_s[i * (TQ // BLK) + j, h:h + 1] = m[h][:, j * BLK:(j + 1) * BLK]
        return 0

    lax.fori_loop(0, NB * BLK // TQ, tile, 0)

    def step(g, _):
        work = []
        for p in range(FP):
            q, kb = pairs[0, g * FP + p], jnp.minimum(pairs[1, g * FP + p], NB - 1)
            work += [(q, aligned(jnp.minimum(q, NB - 1), BLK), aligned(kb, BLK), h) for h in range(HN)]
        s = [mm(kv_ref[ks, h * 128:(h + 1) * 128],
                jnp.concatenate([qt_ref[h * HD:(h + 1) * HD, qs], zero[:, :BLK]], 0)) for q, qs, ks, h in work]
        m = [m_s[q, h:h + 1] for q, qs, ks, h in work]
        new = [jnp.maximum(y, jnp.max(x, axis=0, keepdims=True)) for x, y in zip(s, m)]
        p = [jnp.exp(x - y).astype(bf) for x, y in zip(s, new)]
        a = [mm(vt_ref[h, :, ks], x) for x, (q, qs, ks, h) in zip(p, work)]
        a = [acc_s[q, h] * jnp.exp(x - y) + z for x, y, z, (q, qs, ks, h) in zip(m, new, a, work)]
        for x, y, (q, qs, ks, h) in zip(new, a, work):
            m_s[q, h:h + 1] = x
            acc_s[q, h] = y
        return 0

    lax.fori_loop(0, pairs[2, 0] // FP, step, 0)

    def finish(i, _):
        qs = aligned(i, BLK)
        for h in range(HN):
            total = acc_s[i, h, HD:HD + 1, :]
            out = acc_s[i, h, 0:HD, :] / total
            o_ref[h * HD:(h + 1) * HD, qs] = out
            mix_ref[tab[i // 4], h * HD:(h + 1) * HD, aligned(lax.rem(i, 4), BLK)] = out.astype(bf)
            lse_ref[h:h + 1, qs] = m_s[i, h:h + 1] + jnp.log(total)
        return 0

    lax.fori_loop(0, NB, finish, 0)
    saves += [pltpu.make_async_copy(mix_ref, mix_hbm, sem.at[6]), pltpu.make_async_copy(o_ref, o_hbm, sem.at[7])]
    for c in saves[3:]:
        c.start()
    for c in saves:
        c.wait()


def attn_fwd(parents, tab, whole, w, bias):
    S = NB * BLK
    sd = jax.ShapeDtypeStruct
    vm = pltpu.VMEM
    n = HN * HD
    d = whole.shape[2]
    return pl.pallas_call(
        fwd_kernel,
        out_shape=(sd((n, S), bf), sd((S, 2 * n), bf), sd((n, S), bf), sd((n, S), f32), sd((4, n, S // 4), bf),
                   sd((8, S), f32), sd((3, LIST), jnp.int32)),
        in_specs=[SM, SM, HB, HB, VM], out_specs=(HB,) * 5 + (VM, SM),
        scratch_shapes=[pltpu.SMEM((16,), jnp.int32), vm((NB + 1, 8, BLK), f32), vm((NB + 1, HN, 80, BLK), f32),
                        vm((2, PR, d), bf), vm(w.shape, bf), vm((3 * n, d), bf), vm((d, 2 * n), bf), vm((8, 2 * n), f32),
                        vm((n, S), bf), vm((S, 2 * n), bf), vm((n, S), bf), vm((HN, 80, S), bf),
                        vm((n, S), f32), vm((4, n, S // 4), bf), pltpu.SemaphoreType.DMA((8,))],
        compiler_params=pltpu.CompilerParams(vmem_limit_bytes=60 << 20),
        cost_estimate=pl.CostEstimate(flops=40_000_000_000, bytes_accessed=12_000_000, transcendentals=18_000_000),
        name="tree_attention",
    )(parents, tab, whole, w, bias)


def bwd_kernel(heads, pairs, tab, qt_hbm, kv_hbm, kt_hbm, dots_hbm, o_hbm, lse_ref, dqt_hbm, dkv_hbm,
               dkv_s, dq_s, st_s, dot_ref, qt_ref, kv_ref, kt_ref, dots, o_ref, dqt_ref, dkv_ref, sem):
    loads = [pltpu.make_async_copy(a, b, sem.at[n]) for n, (a, b) in enumerate((
        (dots_hbm, dots), (o_hbm, o_ref), (qt_hbm, qt_ref), (kv_hbm, kv_ref), (kt_hbm, kt_ref)))]
    for c in loads:
        c.start()
    dkv_s[...] = jnp.zeros_like(dkv_s)
    dq_s[...] = jnp.zeros_like(dq_s)
    loads[0].wait()
    for m in range(4):
        dot_ref[:, aligned(tab[m], NB * BLK // 4)] = dots[m]
    loads[1].wait()

    def stats(i, _):
        qs = aligned(i, BLK)
        for n, h in enumerate(heads):
            rows = slice(h * HD, (h + 1) * HD)
            st_s[i, n:n + 1] = jnp.sum(dot_ref[rows, qs].astype(f32) * o_ref[rows, qs], axis=0, keepdims=True)
            st_s[i, 4 + n:5 + n] = lse_ref[h:h + 1, qs]
        return 0

    lax.fori_loop(0, NB, stats, 0)
    for c in loads[2:]:
        c.wait()

    def chains(work, width):
        zero = jnp.zeros((HD, width), bf)
        rows = lambda h: slice(h * HD, (h + 1) * HD)
        qz = [jnp.concatenate([qt_ref[rows(h), qs], zero], 0) for h, qs, ks, lse, delta in work]
        dz = [jnp.concatenate([zero, dot_ref[rows(h), qs]], 0) for h, qs, ks, lse, delta in work]
        kv = [kv_ref[ks, h * 128:(h + 1) * 128] for h, qs, ks, lse, delta in work]
        p = [jnp.exp(mm(x, y) - w[3]) for x, y, w in zip(kv, qz, work)]
        ds = [(x * (mm(y, z) - w[4])).astype(bf) for x, y, z, w in zip(p, kv, dz, work)]
        g = [mm(jnp.concatenate([x, y.astype(bf)], 1), jnp.concatenate([z, u], 1), NT)
             for x, y, z, u in zip(ds, p, qz, dz)]
        return g, [mm(kt_ref[rows(h), ks], x) for x, (h, qs, ks, lse, delta) in zip(ds, work)]

    per = BTQ // BLK

    def tile(i, _):
        row = lambda k: jnp.concatenate([st_s[i * per + j, k:k + 1] for j in range(per)], 1)
        dq = [None] * len(heads)
        for c in range(TRUNK // BTK):
            ks = slice(c * BTK, (c + 1) * BTK)
            g, d = chains([(h, aligned(i, BTQ), ks, row(4 + n), row(n)) for n, h in enumerate(heads)], BTQ)
            for n in range(len(heads)):
                dkv_s[ks, n * 128:(n + 1) * 128] += g[n]
                dq[n] = d[n] if c == 0 else dq[n] + d[n]
        for n in range(len(heads)):
            for j in range(per):
                dq_s[i * per + j, n] += dq[n][:, j * BLK:(j + 1) * BLK]
        return 0

    lax.fori_loop(0, NB * BLK // BTQ, tile, 0)

    def step(s, _):
        work, where = [], []
        for p in range(BP):
            q, kb = pairs[0, s * BP + p], pairs[1, s * BP + p]
            qr = jnp.minimum(q, NB - 1)
            for n, h in enumerate(heads):
                work.append((h, aligned(qr, BLK), aligned(jnp.minimum(kb, NB - 1), BLK),
                             st_s[qr, 4 + n:5 + n], st_s[qr, n:n + 1]))
                where.append((q, kb, n))
        for g, d, (q, kb, n) in zip(*chains(work, BLK), where):
            dkv_s[aligned(kb, BLK), n * 128:(n + 1) * 128] += g
            dq_s[q, n] += d
        return 0

    lax.fori_loop(0, pairs[2, 0] // BP, step, 0)

    def finish(i, _):
        for n in range(len(heads)):
            dqt_ref[n * HD:(n + 1) * HD, aligned(i, BLK)] = (dq_s[i, n] * 0.125).astype(bf)
        dkv_ref[aligned(i, BLK)] = dkv_s[aligned(i, BLK)].astype(bf)
        return 0

    lax.fori_loop(0, NB, finish, 0)
    saves = [pltpu.make_async_copy(dqt_ref, dqt_hbm, sem.at[5]), pltpu.make_async_copy(dkv_ref, dkv_hbm, sem.at[6])]
    for c in saves:
        c.start()
    for c in saves:
        c.wait()


def attn_bwd(heads, pairs, tab, qt, kv, kt, dots, o, lse):
    S = qt.shape[1]
    sd = jax.ShapeDtypeStruct
    n = len(heads)
    return pl.pallas_call(
        functools.partial(bwd_kernel, heads),
        out_shape=(sd((n * HD, S), bf), sd((S, n * 128), bf)),
        in_specs=[SM, SM] + [HB] * 5 + [VM], out_specs=(HB, HB),
        scratch_shapes=[pltpu.VMEM((S + BLK, n * 128), f32), pltpu.VMEM((NB + 1, n, HD, BLK), f32),
                        pltpu.VMEM((NB, 8, BLK), f32), pltpu.VMEM((HN * HD, S), bf)]
        + [pltpu.VMEM(a.shape, a.dtype) for a in (qt, kv, kt, dots, o)]
        + [pltpu.VMEM((n * HD, S), bf), pltpu.VMEM((S, n * 128), bf), pltpu.SemaphoreType.DMA((7,))],
        compiler_params=pltpu.CompilerParams(vmem_limit_bytes=60 << 20),
        cost_estimate=pl.CostEstimate(flops=20_000_000_000 * n, bytes_accessed=8_000_000 * n, transcendentals=6_000_000 * n),
        name="tree_attention_grad",
    )(pairs, tab, qt, kv, kt, dots, o, lse)


D = 768
SEQ = 4096
ROWS = SEQ // 4
QW = HN * HD
FQ = 768
PK = 1792
MESH = pl.DeviceIdType.MESH
HBM = pl.BlockSpec(memory_space=pl.ANY)
TN = (((0,), (0,)), ((), ()))
epsilon = 1e-05
root_half = 0.7071067811865476
inv_root_tau = 0.3989422804014327


def layer_norm(summed, gain_row, shift_row):
    centre = jnp.mean(summed, axis=-1, keepdims=True)
    offset = summed - centre
    inv_std = lax.rsqrt(jnp.mean(offset * offset, axis=-1, keepdims=True) + epsilon)
    normed = offset * inv_std
    return normed * gain_row + shift_row, normed, inv_std


def norm_back(grad_out, normed, inv_std, gain_row):
    scaled = grad_out * gain_row
    return inv_std * (
        scaled
        - jnp.mean(scaled, axis=-1, keepdims=True)
        - normed * jnp.mean(scaled * normed, axis=-1, keepdims=True)
    )


def gelu_parts(u):
    half = 0.5 * (1.0 + lax.erf(u * root_half))
    return u * half, half + u * inv_root_tau * jnp.exp(-0.5 * u * u)


def partner(x, mask):
    return lax.ppermute(x, "tensor", [(i, i ^ mask) for i in range(4)])


def across_x(x):
    return lax.ppermute(x, "dp", [(i, i ^ 1) for i in range(8)])


def flip1(r):
    return r + 1 - 2 * lax.rem(r, 2)


CH = 4
CROWS = ROWS // CH


def remote(src, dst, s, q, dev):
    return pltpu.make_async_remote_copy(
        src_ref=src, dst_ref=dst, send_sem=s, recv_sem=q, device_id=dev, device_id_type=MESH)


def meet(targets, meanwhile=None):
    barrier = pltpu.get_barrier_semaphore()
    for t in targets:
        pl.semaphore_signal(barrier, inc=1, device_id=t, device_id_type=MESH)
    if meanwhile is not None:
        meanwhile()
    pl.semaphore_wait(barrier, len(targets))


class Sends:
    def __init__(self):
        self.started = []

    def go(self, *args):
        c = remote(*args)
        c.start()
        self.started.append(c)
        return c

    def drain(self):
        for c in self.started:
            c.wait_send()


def gather_kernel(with_w, *refs):
    if with_w:
        (inp, te, wq, w1, w2, w3, bias, whole_hbm, wqg_hbm, gz_hbm, gx_hbm, whole, wqg, gz, gx, bcol,
         ysend, yrecv, csend, crecv, out, zsend, zrecv, xsend, xrecv) = refs
    else:
        inp, te, whole_hbm, whole, ysend, yrecv, csend, crecv, out = refs
    r = lax.axis_index("tensor")
    d = lax.axis_index("dp")
    rc, ry = flip1(r), lax.rem(r + 2, 4)
    core, yy = {"tensor": rc}, {"tensor": ry}
    targets = [core, yy]
    if with_w:
        z, x = d // 2, lax.rem(d, 2)
        xx = {"dp": flip1(d)}
        up, down = {"dp": lax.rem(z + 1, 4) * 2 + x}, {"dp": lax.rem(z + 3, 4) * 2 + x}
        targets += [xx, up, down]

    def prepare():
        shift = te[...].astype(f32)
        whole[r] = (inp[...].astype(f32) + shift).astype(bf)
        if with_w:
            for c in range(3):
                wqg[d, :, c * QW:(c + 1) * QW] = wq[c]

    meet(targets, prepare)
    sends = Sends()
    if with_w:

        def line(a, s, slot, way):
            ref = wqg.at[slot * 2 + x] if a == 0 else gz.at[slot]
            k = 2 * (s - 1) + way
            return remote(ref, ref, zsend.at[a, k], zrecv.at[a, k], (up, down)[way])

        def side(a, i, slot):
            src = wqg.at[slot * 2 + x] if a == 0 else gz.at[slot]
            dst = src if a == 0 else gx.at[slot]
            return remote(src, dst, xsend.at[a, i], xrecv.at[a, i], xx)

        def can_send(s, way):
            return jnp.logical_and(z < 3, z - s + 1 >= 0) if way == 0 else jnp.logical_and(z > 0, z + s - 1 <= 3)

        def can_recv(s, way):
            return z - s >= 0 if way == 0 else z + s <= 3

        def own(a):
            for way in (0, 1):
                @pl.when(can_send(1, way))
                def _():
                    line(a, 1, z, way).start()
            side(a, 0, z).start()

        own(0)
    rows = [pl.ds(i * CROWS, CROWS) for i in range(CH)]
    yc = []
    for i in range(CH):
        mine = whole.at[r, rows[i]]
        yc.append(sends.go(mine, mine, ysend.at[i], yrecv.at[i], yy))
    c0 = sends.go(whole.at[r], whole.at[r], csend.at[CH], crecv.at[CH], core)
    if with_w:
        part = wqg.shape[1]
        gz[z, :, 0:FQ] = w1[...]
        gz[z, :, FQ:2 * FQ] = w2[...]
        bcol[...] = jnp.transpose(jnp.broadcast_to(bias[...].astype(f32), (8, D)))
        fill = PK - 2 * FQ - QW
        column = bcol[pl.ds(pl.multiple_of(d * part, 32), part), 0:1]
        column = jnp.where(lax.broadcasted_iota(jnp.int32, (part, fill), 1) == 0, column, 0.0)
        gz[z, :, 2 * FQ:] = jnp.concatenate([w3[...].astype(f32).T, column], 1).astype(bf)
        own(1)
        for s in (1, 2, 3):
            for way in (0, 1):
                slot = z - s if way == 0 else z + s

                @pl.when(can_recv(s, way))
                def _():
                    for a in (0, 1):
                        line(a, s, slot, way).wait_recv()
                        if s < 3:
                            @pl.when(can_send(s + 1, way))
                            def _():
                                line(a, s + 1, slot, way).start()
                        side(a, slot_sem(s, way), slot).start()
    keeps = []

    def keep(src, dst):
        c = pltpu.make_async_copy(src, dst, out.at[len(keeps)])
        c.start()
        keeps.append(c)

    keep(whole.at[r], whole_hbm.at[r])
    cc = []
    for i in range(CH):
        yc[i].wait_recv()
        part = whole.at[ry, rows[i]]
        cc.append(sends.go(part, part, csend.at[i], crecv.at[i], core))
    keep(whole.at[ry], whole_hbm.at[ry])
    c0.wait_recv()
    keep(whole.at[rc], whole_hbm.at[rc])
    for c in cc:
        c.wait_recv()
    rd = 3 - r
    keep(whole.at[rd], whole_hbm.at[rd])
    if with_w:
        keep(gz, gz_hbm)
        for a in (0, 1):
            side(a, 0, z).wait()
        for s in (1, 2, 3):
            for way in (0, 1):
                slot = z - s if way == 0 else z + s

                @pl.when(can_recv(s, way))
                def _():
                    for a in (0, 1):
                        side(a, slot_sem(s, way), slot).wait()

                @pl.when(can_send(s, way))
                def _():
                    for a in (0, 1):
                        line(a, s, slot_of_send(z, s, way), way).wait_send()
        keep(gx, gx_hbm)
        keep(wqg, wqg_hbm)
    for c in keeps:
        c.wait()
    sends.drain()


def slot_of_send(z, s, way):
    return z - s + 1 if way == 0 else z + s - 1


def slot_sem(s, way):
    return 2 * s - 1 + way


def gather_start(inp, te, *weights):
    with_w = len(weights) > 0
    dma = pltpu.SemaphoreType.DMA
    shapes = [jax.ShapeDtypeStruct((4, ROWS, D), bf)]
    args = [inp, te, *weights]
    scratch = []
    sems = [dma((CH,)), dma((CH,)), dma((CH + 1,)), dma((CH + 1,)), dma((7,))]
    if with_w:
        part = weights[0].shape[1]
        line = jax.ShapeDtypeStruct((4, part, PK), bf)
        shapes += [jax.ShapeDtypeStruct((8, part, 3 * QW), bf), line, line]
        scratch = [pltpu.VMEM((D, 8), f32)]
        sems += [dma((2, 6)), dma((2, 6)), dma((2, 7)), dma((2, 7))]
    return pl.pallas_call(
        functools.partial(gather_kernel, with_w),
        out_shape=shapes, in_specs=[VM] * len(args), out_specs=[HB] * len(shapes),
        scratch_shapes=[pltpu.VMEM(a.shape, bf) for a in shapes] + scratch + sems,
        compiler_params=pltpu.CompilerParams(collective_id=0, has_side_effects=True, vmem_limit_bytes=60 << 20),
        name="gather_start",
    )(*args)


RB = 512
NR = ROWS // RB


def middle_kernel(with_w, *refs):
    if with_w:
        wa, wb, wc, wd = refs[:4]
        xsend, xrecv, wsend, wrecv = refs[-4:]
        refs = refs[4:-4]
    else:
        wfull, refs = refs[0], refs[1:]
    (mix_hbm, inp, te, cot, vec, block_out, grad1_o, dots_hbm, p00, p01, p10, p11, sums_o,
     w, wt_s, mix, mixr, gmix, dots, both, ht, gmt, gat, act, gp, slope_s,
     loc, asend, arecv, bsend, brecv, gsend, grecv) = refs
    r = lax.axis_index("tensor")
    d = lax.axis_index("dp")
    x = lax.rem(d, 2)
    ranks = [r, flip1(r), lax.rem(r + 2, 4), 3 - r]
    devices = [{"tensor": k} for k in ranks]
    xx = {"dp": flip1(d)}
    load = pltpu.make_async_copy(mix_hbm, mix, loc.at[5])
    load.start()
    meet(devices[1:] + ([xx] if with_w else []))
    sends = Sends()
    core = devices[1]
    load.wait()

    def heads_in(b, m):
        cols = pl.ds(b * RB, RB)
        return remote(mix.at[m, :, cols], mixr.at[m, :, cols], asend.at[b, m], arecv.at[b, m], devices[m])

    def heads_out(b, m):
        cols = aligned(b, RB)
        return remote(gmix.at[m, :, cols], dots.at[m, :, cols], bsend.at[b, m], brecv.at[b, m], devices[m])

    heads = [[heads_in(b, m) for m in (3, 2, 1)] for b in range(NR)]
    for c in heads[0]:
        c.start()
    fills, arrivals = [pltpu.make_async_copy(mix.at[0], mixr.at[0], loc.at[0])], []
    if with_w:
        ry = ranks[2]
        four, two, end = pl.ds(0, 4), pl.ds(0, 2), pl.ds(2, 2)
        own = ((wa, r, four, x), (wb, r, four, 1 - x), (wc, ry, four, x), (wd, ry, two, 1 - x))
        relay = sends.go(wc.at[end], w.at[ry, end, x], xsend.at[0], xrecv.at[0], xx)
        for i, (ref, t, zs, side) in enumerate(own):
            arrivals.append(sends.go(ref, w.at[t, zs, side], wsend.at[i], wrecv.at[i], core))
            fills.append(pltpu.make_async_copy(ref, w.at[t, zs, side], loc.at[1 + i]))
    else:
        fills.append(pltpu.make_async_copy(wfull, w, loc.at[1]))
    for c in fills:
        c.start()
    for part in heads[1:]:
        for c in part:
            c.start()
    sums_o[...] = jnp.zeros_like(sums_o)
    vecs = vec[...]
    out_bias, outer_bias = vecs[0:1], vecs[1:2]
    gain1, gain2, shift1, shift2 = vecs[2:3], vecs[3:4], vecs[4:5], vecs[5:6]
    if with_w:
        relay.wait_recv()
        tail = w.at[ry, end, 1 - x]
        onward = remote(tail, tail, wsend.at[4], wrecv.at[4], core)
        onward.start()
        arrivals.append(onward)
    for c in fills:
        c.wait()
    for c in arrivals:
        c.wait_recv()
    for t in range(4):
        wt_s[t] = jnp.transpose(w[t, :, :, :, 2 * FQ:].reshape(D, PK - 2 * FQ))
    bias_in = [wt_s[t, QW:QW + 16].astype(f32)[0:1] for t in range(4)]
    w_in = lambda t: w[t, :, :, :, 0:FQ].reshape(D, FQ)
    w_ou = lambda t: w[t, :, :, :, FQ:2 * FQ].reshape(D, FQ)

    def add_sum(i, rows):
        sums_o[i:i + 1] += jnp.sum(rows, axis=0, keepdims=True)

    def block(b, _):
        for i in range(NR):
            @pl.when(b == i)
            def _():
                for c in heads[i]:
                    c.wait_recv()
        rows = aligned(b, RB)
        start = inp[rows].astype(f32) + te[...].astype(f32)
        attn = out_bias
        for m in range(4):
            attn = attn + mm(mixr[m, :, rows], wt_s[ranks[m], :QW], TN)
        hidden, normed1, inv1 = layer_norm(start + attn, gain1, shift1)
        low = hidden.astype(bf)
        ht[:, rows] = low.T
        mlp = outer_bias
        for t in range(4):
            u = mm(low, w_in(t)) + bias_in[t]
            value, slope = gelu_parts(u)
            value = value.astype(bf)
            act[t, rows] = value
            slope_s[t] = slope.astype(bf)
            mlp = mlp + mm(value, w_ou(t), NT)
        final, normed2, inv2 = layer_norm(hidden + mlp, gain2, shift2)
        block_out[rows] = final.astype(bf)
        e = cot[rows].astype(f32)
        add_sum(0, e * normed2)
        add_sum(1, e)
        grad2 = norm_back(e, normed2, inv2, gain2)
        gm = grad2.astype(bf)
        gmt[:, rows] = gm.T
        add_sum(2, gm.astype(f32))
        gin = grad2
        for t in range(4):
            g = (mm(gm, w_ou(t)) * slope_s[t].astype(f32)).astype(bf)
            gp[t, rows] = g
            add_sum(6 + t, g.astype(f32))
            gin = gin + mm(g, w_in(t), NT)
        add_sum(3, gin * normed1)
        add_sum(4, gin)
        grad1 = norm_back(gin, normed1, inv1, gain1)
        grad1_o[rows] = grad1
        ga = grad1.astype(bf)
        gat_rows = ga.T
        gat[:, rows] = gat_rows
        add_sum(5, ga.astype(f32))
        for m in (3, 2, 1):
            gmix[m, :, rows] = mm(wt_s[ranks[m], :QW], gat_rows).astype(bf)
            heads_out(b, m).start()
        dots[0, :, rows] = mm(wt_s[r, :QW], gat_rows).astype(bf)
        return 0

    lax.fori_loop(0, NR, block, 0)

    if with_w:
        onward.wait_send()

    def grads(t, m):
        return (lambda: mm(ht[...], gp[t]), lambda: mm(gmt[...], act[t]), lambda: mm(gat[...], mixr[m], NT))

    cols = (slice(0, FQ), slice(FQ, 2 * FQ), slice(2 * FQ, 2 * FQ + QW))
    blank = jnp.zeros((4, 2, 96, PK - 2 * FQ - QW), bf)
    cut = lambda g: g.reshape(4, 2, 96, g.shape[1])

    def handing(q):
        return remote(w.at[q], both.at[q], gsend.at[q], grecv.at[q], core)

    for q in (1, 0):
        for c, g in zip(cols, grads(ranks[2 * q + 1], 2 * q + 1)):
            w[q, :, :, :, c] = cut(g().astype(bf))
        w[q, :, :, :, 2 * FQ + QW:] = blank
        handing(q).start()
    saves = []
    for q in (1, 0):
        mine = grads(ranks[2 * q], 2 * q)
        handing(q).wait_recv()
        for c, g in zip(cols, mine):
            both[q, :, :, :, c] = (both[q, :, :, :, c].astype(f32) + cut(g())).astype(bf)
        for n, side in ((0, x), (1, 1 - x)):
            to = ((p00, p01), (p10, p11))[q][n]
            saves.append(pltpu.make_async_copy(both.at[q, :, side], to, loc.at[6 + 2 * q + n]))
            saves[-1].start()
    for b in range(NR):
        for m in (1, 2, 3):
            heads_out(b, m).wait()
        for c in heads[b]:
            c.wait_send()
    saves.append(pltpu.make_async_copy(dots, dots_hbm, loc.at[10]))
    saves[-1].start()
    for c in saves:
        c.wait()
    for q in range(2):
        handing(q).wait_send()
    sends.drain()


def middle(weights, mix, inp, te, cot, vec):
    sd = jax.ShapeDtypeStruct
    dma = pltpu.SemaphoreType.DMA
    with_w = len(weights) > 1
    vm = pltpu.VMEM
    tokens = (D, ROWS)
    extra = [dma((1,)), dma((1,)), dma((5,)), dma((5,))] if with_w else []
    return pl.pallas_call(
        functools.partial(middle_kernel, with_w),
        out_shape=(sd((ROWS, D), bf), sd((ROWS, D), f32), sd((4, QW, ROWS), bf),
                   *([sd((4, 96, PK), bf)] * 4), sd((16, D), f32)),
        in_specs=[HB] * len(weights) + [HB] + [VM] * 4, out_specs=(VM, VM, HB, HB, HB, HB, HB, VM),
        scratch_shapes=[vm((4, 4, 2, 96, PK), bf), vm((4, PK - 2 * FQ, D), bf), vm((4, QW, ROWS), bf),
                        vm((4, QW, ROWS), bf), vm((4, QW, ROWS), bf), vm((4, QW, ROWS), bf),
                        vm((2, 4, 2, 96, PK), bf), vm(tokens, bf), vm(tokens, bf), vm(tokens, bf),
                        vm((4, ROWS, FQ), bf), vm((4, ROWS, FQ), bf), vm((4, RB, FQ), bf),
                        dma((11,)), dma((NR, 4)), dma((NR, 4)), dma((NR, 4)), dma((NR, 4)), dma((2,)), dma((2,))] + extra,
        compiler_params=pltpu.CompilerParams(collective_id=2, has_side_effects=True, vmem_limit_bytes=63 << 20),
        cost_estimate=pl.CostEstimate(flops=33_000_000_000, bytes_accessed=50_000_000, transcendentals=9_000_000),
        name="middle",
    )(*weights, mix, inp, te, cot, vec)


def final_kernel(with_w, *refs):
    if with_w:
        (x_hbm, w_hbm, dqt_hbm, dkv_hbm, g1_hbm, m0_hbm, m1_hbm, m2_hbm, m3_hbm, small, out, pair, qo, mo, tot,
         x_s, w_s, wr_s, dqt, dkv, grad1, part, crv, ysd, yrv, m0, m1, m2, m3, zsm, zrm, dwq, xrq, zsq, zrq,
         prv, psd, prs, loc, csend, crecv, ysend, yrecv, xsend, xrecv, zsend, zrecv) = refs
    else:
        (x_hbm, w_hbm, dqt_hbm, dkv_hbm, g1_hbm, out, pair, dw,
         x_s, w_s, wr_s, dqt, dkv, grad1, part, crv, ysd, yrv, loc, csend, crecv, ysend, yrecv) = refs
    pulls = [(w_hbm, w_s), (dqt_hbm, dqt), (dkv_hbm, dkv)]
    pulls += [(m0_hbm, m0), (m1_hbm, m1), (m2_hbm, m2), (m3_hbm, m3)] if with_w else []
    pulls += [(x_hbm, x_s), (g1_hbm, grad1)]
    loads = [pltpu.make_async_copy(a, b, loc.at[n]) for n, (a, b) in enumerate(pulls)]
    for c in loads:
        c.start()
    r = lax.axis_index("tensor")
    d = lax.axis_index("dp")
    rc, ry = flip1(r), lax.rem(r + 2, 4)
    rd = 3 - r
    core, yy = {"tensor": rc}, {"tensor": ry}
    targets = [core, yy]
    if with_w:
        z, x = d // 2, lax.rem(d, 2)
        xo = 1 - x
        zs = [lax.rem(z + k, 4) for k in range(4)]
        xx = {"dp": flip1(d)}
        zdev = [{"dp": zs[k] * 2 + x} for k in range(4)]
        targets += [xx] + zdev[1:]
    meet(targets)
    sends = Sends()
    go = sends.go
    wait = lambda *which: [loads[n].wait() for n in which]
    rows = [pl.ds(i * CROWS, CROWS) for i in range(CH)]
    if with_w:
        wait(3, 4, 5, 6)
        zm = []
        for k in (1, 2, 3, 0):
            at = zs[k]
            zsm[k] = ((m0[at].astype(f32) + m1[at].astype(f32)) + (m2[at].astype(f32) + m3[at].astype(f32))).astype(bf)
            if k:
                zm.append(go(zsm.at[k], zrm.at[k - 1], zsend.at[1, k - 1], zrecv.at[1, k - 1], zdev[k]))
    wait(0, 1, 2)
    w = w_s[...].reshape(D, 3 * QW)
    for h in range(HN):
        for c in (1, 2):
            wr_s[:, h * 128 + (c - 1) * HD:h * 128 + c * HD] = w[:, c * QW + h * HD:c * QW + (h + 1) * HD]
    wqs = w[:, :QW]

    def project_back(t, i):
        at = pl.ds(pl.multiple_of(t * ROWS + i * CROWS, CROWS), CROWS)
        part[t, rows[i]] = (mm(dqt[:, at], wqs, (((0,), (1,)), ((), ()))) + mm(dkv[at], wr_s[...], NT)).astype(bf)

    first, second, third = [], [], []
    for i in range(CH):
        project_back(rd, i)
        second.append(go(part.at[rd, rows[i]], crv.at[1, rows[i]], csend.at[1, i], crecv.at[1, i], core))
        project_back(ry, i)
        if i:
            second[i - 1].wait_recv()
            prev = rows[i - 1]
            ysd[prev] = (part[ry, prev].astype(f32) + crv[1, prev].astype(f32)).astype(bf)
            third.append(go(ysd.at[prev], yrv.at[prev], ysend.at[i - 1], yrecv.at[i - 1], yy))
    prev = rows[CH - 1]
    second[CH - 1].wait_recv()
    ysd[prev] = (part[ry, prev].astype(f32) + crv[1, prev].astype(f32)).astype(bf)
    third.append(go(ysd.at[prev], yrv.at[prev], ysend.at[CH - 1], yrecv.at[CH - 1], yy))

    wait(len(loads) - 2)
    whole = x_s[...].reshape(SEQ, D)
    aq = mm(dqt[...], whole)
    akv = mm(dkv[...], whole, TN)
    blocks = [aq]
    for c in (0, 1):
        blocks += [akv[h * 128 + c * HD:h * 128 + (c + 1) * HD] for h in range(HN)]
    dwt = jnp.concatenate(blocks, 0).T.astype(bf)
    sum_q = jnp.sum(dqt[...].astype(f32), axis=1, keepdims=True)
    sum_q = jnp.transpose(jnp.broadcast_to(sum_q, (QW, 8)))
    sum_kv = jnp.sum(dkv[...].astype(f32), axis=0, keepdims=True)
    sum_v = jnp.concatenate([sum_kv[:, h * 128 + HD:(h + 1) * 128] for h in range(HN)], 1)
    pairs = jnp.concatenate([sum_q[0:1], sum_v, jnp.zeros((6, QW), f32)], 0)
    if with_w:
        dwq[...] = dwt.reshape(dwq.shape)
        xq = go(dwq.at[:, xo], xrq, xsend.at[0], xrecv.at[0], xx)
        prs[...] = pairs
        px = go(prs, prv, xsend.at[1], xrecv.at[1], xx)
    for i in range(CH):
        project_back(rc, i)
        first.append(go(part.at[rc, rows[i]], crv.at[0, rows[i]], csend.at[0, i], crecv.at[0, i], core))
        project_back(r, i)
    if with_w:
        tot[...] = jnp.sum(small[...], axis=0)
        px.wait_recv()
        psd[z] = prs[...] + prv[...]
        zp = [go(psd.at[z], psd.at[z], zsend.at[2, k - 1], zrecv.at[2, k - 1], zdev[k]) for k in (1, 2, 3)]
        xq.wait_recv()
        for k in range(4):
            zsq[k] = (dwq[zs[k], x].astype(f32) + xrq[zs[k]].astype(f32)).astype(bf)
        zq = [go(zsq.at[k], zrq.at[k - 1], zsend.at[0, k - 1], zrecv.at[0, k - 1], zdev[k]) for k in (1, 2, 3)]
    else:
        dw[...] = dwt
        pair[...] = pairs
    wait(len(loads) - 1)
    for i in range(CH):
        first[i].wait_recv()
        third[i].wait_recv()
        out[rows[i]] = (part[r, rows[i]].astype(f32) + crv[0, rows[i]].astype(f32)
                        + yrv[rows[i]].astype(f32) + grad1[rows[i]]).astype(bf)
    if with_w:
        for c in zq:
            c.wait_recv()
        whole_q = (zsq[0].astype(f32) + zrq[0].astype(f32)) + (zrq[1].astype(f32) + zrq[2].astype(f32))
        qo[...] = whole_q
        for c in zp:
            c.wait_recv()
        pair[...] = ((psd[0] + psd[1]) + psd[2]) + psd[3]
        for c in zm:
            c.wait_recv()
        mo[...] = (zsm[0].astype(f32) + zrm[0].astype(f32)) + (zrm[1].astype(f32) + zrm[2].astype(f32))
    sends.drain()


def final(whole, w, dqt, dkv, grad1, *more):
    with_w = len(more) > 0
    dma = pltpu.SemaphoreType.DMA
    sd = jax.ShapeDtypeStruct
    vm = pltpu.VMEM
    rows = (ROWS, D)
    like = lambda a: vm(a.shape, a.dtype)
    shapes = [sd(rows, bf), sd((8, QW), f32)]
    args = [whole, w, dqt, dkv, grad1, *more]
    scratch = [like(whole), like(w), vm((D, 2 * QW), bf), like(dqt), like(dkv), like(grad1), vm((4,) + rows, bf),
               vm((2,) + rows, bf), vm(rows, bf), vm(rows, bf)]
    sems = [dma((9,)), dma((2, CH)), dma((2, CH)), dma((CH,)), dma((CH,))]
    if with_w:
        n = w.shape[1]
        shapes += [sd((n, 3 * QW), f32), sd((n, PK), f32), sd(more[4].shape[1:], f32)]
        scratch += [like(m) for m in more[:4]] + [vm((4, n, PK), bf), vm((3, n, PK), bf),
                    vm((4, 2, n, 3 * QW), bf), vm((4, n, 3 * QW), bf), vm((4, n, 3 * QW), bf), vm((3, n, 3 * QW), bf),
                    vm((8, QW), f32), vm((4, 8, QW), f32), vm((8, QW), f32)]
        sems += [dma((2,)), dma((2,)), dma((3, 3)), dma((3, 3))]
    else:
        shapes += [sd((D, 3 * QW), bf)]
    return pl.pallas_call(
        functools.partial(final_kernel, with_w),
        out_shape=shapes,
        in_specs=[HB] * (len(args) - 1) + [VM if with_w else HB], out_specs=[VM] * len(shapes),
        scratch_shapes=scratch + sems,
        compiler_params=pltpu.CompilerParams(
            collective_id=1, has_side_effects=True, vmem_limit_bytes=60 << 20),
        name="final",
    )(*args)


def emit_kernel(rank, *refs):
    sources, outs, kept, sem = refs[:6], refs[6:18], refs[18:24], refs[24]
    loads = [pltpu.make_async_copy(a, b, sem.at[n]) for n, (a, b) in enumerate(zip(sources, kept))]
    for c in loads:
        c.start()
    block_out, input_grad, qkv_o, pair_o, out_o, out_b, inner_o, inner_b, outer_o, outer_b, gain_o, shift_o = outs
    saves = [pltpu.make_async_copy(kept[n], to, sem.at[6 + n]) for n, to in enumerate((block_out, input_grad))]
    for n in range(2):
        loads[n].wait()
        saves[n].start()
    for c in loads[2:]:
        c.wait()
    pair, qkv, share, sums = kept[2:]
    for c in range(3):
        qkv_o[c] = qkv[:, c * QW:(c + 1) * QW]
    pair_o[...] = pair[0:2]
    inner_o[...] = share[:, 0:FQ]
    outer_o[...] = share[:, FQ:2 * FQ]
    out_o[...] = share[:, 2 * FQ:].T[:QW]
    out_b[...] = sums[5]
    inner_b[...] = sums[6 + rank[0]]
    outer_b[...] = sums[2]
    gain_o[...] = jnp.concatenate([sums[3:4], sums[0:1]], 0)
    shift_o[...] = jnp.concatenate([sums[4:5], sums[1:2]], 0)
    for c in saves:
        c.wait()


def emit(rank, *arrays):
    sd = jax.ShapeDtypeStruct
    n = arrays[4].shape[0]
    rows = sd((ROWS, D), bf)
    vec = sd((D,), f32)
    shapes = (rows, rows, sd((3, n, QW), f32), sd((2, QW), f32), sd((QW, n), f32), vec, sd((n, FQ), f32), vec,
              sd((n, FQ), f32), vec, sd((2, D), f32), sd((2, D), f32))
    return pl.pallas_call(
        emit_kernel, out_shape=shapes, in_specs=[SM] + [HB] * 6, out_specs=(HB, HB) + (VM,) * 10,
        scratch_shapes=[pltpu.VMEM(a.shape, a.dtype) for a in arrays] + [pltpu.SemaphoreType.DMA((8,))],
        compiler_params=pltpu.CompilerParams(vmem_limit_bytes=60 << 20),
        name="emit",
    )(rank.reshape(1), *arrays)


def add_low(a, b):
    return (a.astype(f32) + b.astype(f32)).astype(bf)


def on_device(
    ring, input_rows, time_embed, parents, qkv_weight, qv_bias, out_weight, out_bias, inner_weight,
    inner_bias, outer_weight, outer_bias, norm_gain, norm_shift, cotangent,
):
    rank = lax.axis_index("tensor")
    dpos = lax.axis_index("dp")
    part = qkv_weight.shape[0]
    own_ring = ring == 8
    order = jnp.stack([rank, rank ^ 1, rank ^ 2, rank ^ 3]).astype(jnp.int32)

    bias = qv_bias.astype(f32).reshape(1, 2 * QW)
    if own_ring:
        whole, w_all, gz, gx = gather_start(
            input_rows, time_embed, jnp.transpose(qkv_weight, (1, 0, 2)), inner_weight, outer_weight.T, out_weight,
            inner_bias[None])
        weights = [gz, gx, partner(gz, 2), partner(gx[:2], 2)]
    else:
        whole = gather_start(input_rows, time_embed)[0]
        w_all = lax.all_gather(qkv_weight.reshape(part, 3 * QW), "dp", axis=0, tiled=True).reshape(8, 96, 3 * QW)
        bias_part = lax.dynamic_slice_in_dim(inner_bias, dpos * part, part, 0)
        packed = jnp.concatenate([inner_weight, outer_weight.T, out_weight.T, bias_part[:, None],
                                  jnp.zeros((part, PK - 2 * FQ - QW - 1), bf)], axis=1)
        packed = lax.all_gather(packed, "dp", axis=0, tiled=True)
        weights = [lax.all_gather(packed, "tensor", axis=0, tiled=False).reshape(4, 4, 2, 96, PK)]

    qt, kv, kt, ot, mix, lse, pairs = attn_fwd(parents[0], order, whole, w_all, bias)
    vec = jnp.concatenate(
        [out_bias[None], outer_bias[None], norm_gain, norm_shift, jnp.zeros((2, D), bf)], axis=0).astype(f32)
    block_out, grad1, dots, *parts, sums = middle(weights, mix, input_rows, time_embed, cotangent, vec)
    sums = lax.all_gather(sums, ("dp", "tensor"), axis=0, tiled=False)
    if own_ring:
        diagonal = [(i * 4 + j, (i ^ 1) * 4 + (j ^ 2)) for i in range(8) for j in range(4)]
        parts = [parts[0], across_x(parts[1]), partner(parts[2], 2), lax.ppermute(parts[3], ("dp", "tensor"), diagonal)]
    else:
        far = [partner(parts[2], 2), partner(parts[3], 2)]
    dqt, dkv = attn_bwd((0, 1, 2), pairs, order, qt, kv, kt, dots, ot, lse)
    if own_ring:
        input_grad, pair, qkv_share, share, sums = final(whole, w_all, dqt, dkv, grad1, *parts, sums)
        (block_out, input_grad, qkv_share, pair, out_share, out_sum, inner_share, inner_sum, outer_share, outer_sum,
         gains, shifts) = emit(rank, block_out, input_grad, pair, qkv_share, share, sums)
        return (block_out, input_grad, jnp.transpose(qkv_share, (1, 0, 2)), pair, out_share, out_sum,
                inner_share, inner_sum, outer_share.T, outer_sum, gains, shifts)
    else:
        input_grad, pair, dwq = final(whole, w_all, dqt, dkv, grad1)
        own, other = add_low(parts[0], far[0]), add_low(parts[1], far[1])
        even = dpos % 2 == 0
        mine = jnp.stack([jnp.where(even, own, other), jnp.where(even, other, own)], axis=1).reshape(D, PK)
        share = lax.psum_scatter(mine, "dp", scatter_dimension=0, tiled=True).astype(f32)
        qkv_share = lax.psum_scatter(dwq, "dp", scatter_dimension=0, tiled=True).astype(f32).reshape(part, 3, QW)
        pair = lax.psum(pair, "dp")
        sums = jnp.sum(sums, axis=0)
    return (
        block_out,
        input_grad,
        qkv_share,
        pair[:2],
        share[:, 2 * FQ:2 * FQ + QW].T,
        sums[5],
        share[:, :FQ],
        lax.dynamic_index_in_dim(sums[6:10], rank, 0, keepdims=False),
        share[:, FQ:2 * FQ].T,
        sums[2],
        jnp.stack([sums[3], sums[0]]),
        jnp.stack([sums[4], sums[1]]),
    )


def solution(mesh):
    both = P(("dp", "tensor"), None)
    return jax.shard_map(
        functools.partial(on_device, mesh.shape["dp"]),
        mesh=mesh,
        in_specs=(
            both, P("dp", None), P("dp", None), P("dp", None, "tensor"), P(None, "tensor"),
            P("tensor", "dp"), P(), P("dp", "tensor"), P("tensor"), P("tensor", "dp"), P(), P(), P(), both,
        ),
        out_specs=(
            both, both, P("dp", None, "tensor"), P(None, "tensor"), P("tensor", "dp"), P(),
            P("dp", "tensor"), P("tensor"), P("tensor", "dp"), P(), P(), P(),
        ),
        check_vma=False,
    )
```

```python
import functools
import jax, jax.numpy as jnp
from jax import lax
from jax.experimental import pallas as pl
from jax.experimental.pallas import tpu as pltpu
from jax.sharding import PartitionSpec as P
bf = jnp.bfloat16
f32 = jnp.float32
BLK = 256
TRUNK = 1024
NB = 16
HD = 64
HN = 3
SEGS = 13
PAD = 4
LIST = 192
TQ = 512
TK = 1024
FP = 4
BP = 4
BTQ = 1024
BTK = 256
VM = pl.BlockSpec(memory_space=pltpu.VMEM)
SM = pl.BlockSpec(memory_space=pltpu.SMEM)
HB = pl.BlockSpec(memory_space=pltpu.HBM)
NT = (((1,), (1,)), ((), ()))


def mm(a, b, dims=(((1,), (0,)), ((), ()))):
    return lax.dot_general(a, b, dims, preferred_element_type=f32)


def aligned(i, n):
    return pl.ds(pl.multiple_of(i * n, n), n)


def list_pairs(parents, cur, pairs):
    for s in range(1, SEGS):
        cur[s] = jnp.int32(s)

    def level(_, n):
        for s in range(1, SEGS):
            c = cur[s]
            pairs[0, n] = jnp.int32(s + 3)
            pairs[1, n] = c + 3
            cur[s] = jnp.where(c > 0, parents[0, c], 0)
            n = n + jnp.where(c > 0, 1, 0)
        for i in range(PAD - 1):
            pairs[0, n + i] = jnp.int32(NB)
            pairs[1, n + i] = jnp.int32(NB)
        return (n + PAD - 1) // PAD * PAD

    pairs[2, 0] = lax.fori_loop(0, SEGS - 1, level, jnp.int32(0))


PR = 1024


def fwd_kernel(parents, x_hbm, w_hbm, b_ref, qt_hbm, kv_hbm, kt_hbm, o_hbm, mix_hbm, lse_ref, pairs,
               cur, m_s, acc_s, xs, w_s, wt_s, wr_s, br_s, qt_ref, kv_ref, kt_ref, vt_ref, o_ref, mix_ref, sem):
    def fetch(i, slot):
        return pltpu.make_async_copy(x_hbm.at[i], xs.at[slot], sem.at[slot])

    load_w = pltpu.make_async_copy(w_hbm, w_s, sem.at[2])
    load_w.start()
    fetch(0, 0).start()
    list_pairs(parents, cur, pairs)
    load_w.wait()
    bias = b_ref[...].astype(f32)
    bias = jnp.concatenate([bias[0:1], bias[1:2]], 1)
    w = w_s[...].reshape(w_s.shape[0] * w_s.shape[1], w_s.shape[2])
    wt_s[...] = w.T
    for h in range(HN):
        for c in (1, 2):
            to = slice(h * 128 + (c - 1) * HD, h * 128 + c * HD)
            wr_s[:, to] = w[:, c * HN * HD + h * HD:c * HN * HD + (h + 1) * HD]
            part = bias[:, HN * HD + h * HD:HN * HD + (h + 1) * HD] if c == 2 else jnp.zeros((1, HD), f32)
            br_s[:, to] = jnp.broadcast_to(part, (8, HD))
    bias_col = jnp.transpose(jnp.broadcast_to(bias, (8, 2 * HN * HD)))
    ones = (lax.broadcasted_iota(jnp.int32, (16, PR), 0) == 0).astype(f32).astype(bf)

    def rows(i, _):
        slot = lax.rem(i, 2)

        @pl.when(i + 1 < NB * BLK // PR)
        def _():
            fetch(i + 1, 1 - slot).start()

        fetch(i, slot).wait()
        cols = aligned(i, PR)
        x = xs[slot]
        up = mm(wt_s[...], x, NT)
        q = (up[:HN * HD] + bias_col[:HN * HD, 0:1]).astype(bf)
        qt_ref[:, cols] = (q.astype(f32) * 0.125).astype(bf)
        kt_ref[:, cols] = up[HN * HD:2 * HN * HD].astype(bf)
        vt = (up[2 * HN * HD:] + bias_col[HN * HD:, 0:1]).astype(bf)
        for h in range(HN):
            vt_ref[h, :HD, cols] = vt[h * HD:(h + 1) * HD]
            vt_ref[h, HD:, cols] = ones
        kv_ref[cols] = (mm(x, wr_s[...]) + br_s[0:1]).astype(bf)
        return 0

    lax.fori_loop(0, NB * BLK // PR, rows, 0)
    saves = [pltpu.make_async_copy(a, b, sem.at[3 + n])
             for n, (a, b) in enumerate(((qt_ref, qt_hbm), (kv_ref, kv_hbm), (kt_ref, kt_hbm)))]
    for c in saves:
        c.start()
    zero = jnp.zeros((HD, TQ), bf)

    def tile(i, _):
        qz = [jnp.concatenate([qt_ref[h * HD:(h + 1) * HD, aligned(i, TQ)], zero], 0) for h in range(HN)]
        m, acc = [None] * HN, [None] * HN
        for c in range(TRUNK // TK):
            ks = slice(c * TK, (c + 1) * TK)
            s = [mm(kv_ref[ks, h * 128:(h + 1) * 128], qz[h]) for h in range(HN)]
            new = [jnp.max(x, axis=0, keepdims=True) for x in s]
            if c:
                new = [jnp.maximum(x, y) for x, y in zip(m, new)]
            p = [jnp.exp(x - y).astype(bf) for x, y in zip(s, new)]
            a = [mm(vt_ref[h, :, ks], p[h]) for h in range(HN)]
            if c:
                a = [x * jnp.exp(y - z) + w for x, y, z, w in zip(acc, m, new, a)]
            m, acc = new, a
        for h in range(HN):
            for j in range(TQ // BLK):
                acc_s[i * (TQ // BLK) + j, h] = acc[h][:, j * BLK:(j + 1) * BLK]
                m_s[i * (TQ // BLK) + j, h:h + 1] = m[h][:, j * BLK:(j + 1) * BLK]
        return 0

    lax.fori_loop(0, NB * BLK // TQ, tile, 0)

    def step(g, _):
        work = []
        for p in range(FP):
            q, kb = pairs[0, g * FP + p], jnp.minimum(pairs[1, g * FP + p], NB - 1)
            work += [(q, aligned(jnp.minimum(q, NB - 1), BLK), aligned(kb, BLK), h) for h in range(HN)]
        s = [mm(kv_ref[ks, h * 128:(h + 1) * 128],
                jnp.concatenate([qt_ref[h * HD:(h + 1) * HD, qs], zero[:, :BLK]], 0)) for q, qs, ks, h in work]
        m = [m_s[q, h:h + 1] for q, qs, ks, h in work]
        new = [jnp.maximum(y, jnp.max(x, axis=0, keepdims=True)) for x, y in zip(s, m)]
        p = [jnp.exp(x - y).astype(bf) for x, y in zip(s, new)]
        a = [mm(vt_ref[h, :, ks], x) for x, (q, qs, ks, h) in zip(p, work)]
        a = [acc_s[q, h] * jnp.exp(x - y) + z for x, y, z, (q, qs, ks, h) in zip(m, new, a, work)]
        for x, y, (q, qs, ks, h) in zip(new, a, work):
            m_s[q, h:h + 1] = x
            acc_s[q, h] = y
        return 0

    lax.fori_loop(0, pairs[2, 0] // FP, step, 0)

    rank = lax.axis_index("tensor")

    def finish(i, _):
        qs = aligned(i, BLK)
        slot = jnp.bitwise_xor(rank, i // 4)
        for h in range(HN):
            total = acc_s[i, h, HD:HD + 1, :]
            out = acc_s[i, h, 0:HD, :] / total
            o_ref[h * HD:(h + 1) * HD, qs] = out
            mix_ref[slot, h * HD:(h + 1) * HD, aligned(lax.rem(i, 4), BLK)] = out.astype(bf)
            lse_ref[h:h + 1, qs] = m_s[i, h:h + 1] + jnp.log(total)
        return 0

    lax.fori_loop(0, NB, finish, 0)
    saves += [pltpu.make_async_copy(mix_ref, mix_hbm, sem.at[6]), pltpu.make_async_copy(o_ref, o_hbm, sem.at[7])]
    for c in saves[3:]:
        c.start()
    for c in saves:
        c.wait()


def attn_fwd(parents, whole, w, bias):
    S = NB * BLK
    sd = jax.ShapeDtypeStruct
    vm = pltpu.VMEM
    n = HN * HD
    d = whole.shape[2]
    return pl.pallas_call(
        fwd_kernel,
        out_shape=(sd((n, S), bf), sd((S, 2 * n), bf), sd((n, S), bf), sd((n, S), f32), sd((4, n, S // 4), bf),
                   sd((8, S), f32), sd((3, LIST), jnp.int32)),
        in_specs=[SM, HB, HB, VM], out_specs=(HB,) * 5 + (VM, SM),
        scratch_shapes=[pltpu.SMEM((16,), jnp.int32), vm((NB + 1, 8, BLK), f32), vm((NB + 1, HN, 80, BLK), f32),
                        vm((2, PR, d), bf), vm(w.shape, bf), vm((3 * n, d), bf), vm((d, 2 * n), bf), vm((8, 2 * n), f32),
                        vm((n, S), bf), vm((S, 2 * n), bf), vm((n, S), bf), vm((HN, 80, S), bf),
                        vm((n, S), f32), vm((4, n, S // 4), bf), pltpu.SemaphoreType.DMA((8,))],
        compiler_params=pltpu.CompilerParams(vmem_limit_bytes=60 << 20),
        cost_estimate=pl.CostEstimate(flops=40_000_000_000, bytes_accessed=12_000_000, transcendentals=18_000_000),
        name="tree_attention",
    )(parents, whole, w, bias)


def bwd_kernel(heads, pairs, qt_hbm, kv_hbm, kt_hbm, dots_hbm, o_hbm, lse_ref, dqt_hbm, dkv_hbm,
               dkv_s, dq_s, st_s, dot_ref, qt_ref, kv_ref, kt_ref, dots, o_ref, dqt_ref, dkv_ref, sem):
    loads = [pltpu.make_async_copy(a, b, sem.at[n]) for n, (a, b) in enumerate((
        (dots_hbm, dots), (o_hbm, o_ref), (qt_hbm, qt_ref), (kv_hbm, kv_ref), (kt_hbm, kt_ref)))]
    for c in loads:
        c.start()
    dkv_s[...] = jnp.zeros_like(dkv_s)
    dq_s[...] = jnp.zeros_like(dq_s)
    rank = lax.axis_index("tensor")
    loads[0].wait()
    for m in range(4):
        dot_ref[:, aligned(jnp.bitwise_xor(rank, m), NB * BLK // 4)] = dots[m]
    loads[1].wait()

    def stats(i, _):
        qs = aligned(i, BLK)
        for n, h in enumerate(heads):
            rows = slice(h * HD, (h + 1) * HD)
            st_s[i, n:n + 1] = jnp.sum(dot_ref[rows, qs].astype(f32) * o_ref[rows, qs], axis=0, keepdims=True)
            st_s[i, 4 + n:5 + n] = lse_ref[h:h + 1, qs]
        return 0

    lax.fori_loop(0, NB, stats, 0)
    for c in loads[2:]:
        c.wait()

    def chains(work, width):
        zero = jnp.zeros((HD, width), bf)
        rows = lambda h: slice(h * HD, (h + 1) * HD)
        qz = [jnp.concatenate([qt_ref[rows(h), qs], zero], 0) for h, qs, ks, lse, delta in work]
        dz = [jnp.concatenate([zero, dot_ref[rows(h), qs]], 0) for h, qs, ks, lse, delta in work]
        kv = [kv_ref[ks, h * 128:(h + 1) * 128] for h, qs, ks, lse, delta in work]
        p = [jnp.exp(mm(x, y) - w[3]) for x, y, w in zip(kv, qz, work)]
        ds = [(x * (mm(y, z) - w[4])).astype(bf) for x, y, z, w in zip(p, kv, dz, work)]
        g = [mm(jnp.concatenate([x, y.astype(bf)], 1), jnp.concatenate([z, u], 1), NT)
             for x, y, z, u in zip(ds, p, qz, dz)]
        return g, [mm(kt_ref[rows(h), ks], x) for x, (h, qs, ks, lse, delta) in zip(ds, work)]

    per = BTQ // BLK

    def tile(i, _):
        row = lambda k: jnp.concatenate([st_s[i * per + j, k:k + 1] for j in range(per)], 1)
        dq = [None] * len(heads)
        for c in range(TRUNK // BTK):
            ks = slice(c * BTK, (c + 1) * BTK)
            g, d = chains([(h, aligned(i, BTQ), ks, row(4 + n), row(n)) for n, h in enumerate(heads)], BTQ)
            for n in range(len(heads)):
                dkv_s[ks, n * 128:(n + 1) * 128] += g[n]
                dq[n] = d[n] if c == 0 else dq[n] + d[n]
        for n in range(len(heads)):
            for j in range(per):
                dq_s[i * per + j, n] += dq[n][:, j * BLK:(j + 1) * BLK]
        return 0

    lax.fori_loop(0, NB * BLK // BTQ, tile, 0)

    def step(s, _):
        work, where = [], []
        for p in range(BP):
            q, kb = pairs[0, s * BP + p], pairs[1, s * BP + p]
            qr = jnp.minimum(q, NB - 1)
            for n, h in enumerate(heads):
                work.append((h, aligned(qr, BLK), aligned(jnp.minimum(kb, NB - 1), BLK),
                             st_s[qr, 4 + n:5 + n], st_s[qr, n:n + 1]))
                where.append((q, kb, n))
        for g, d, (q, kb, n) in zip(*chains(work, BLK), where):
            dkv_s[aligned(kb, BLK), n * 128:(n + 1) * 128] += g
            dq_s[q, n] += d
        return 0

    lax.fori_loop(0, pairs[2, 0] // BP, step, 0)

    def finish(i, _):
        for n in range(len(heads)):
            dqt_ref[n * HD:(n + 1) * HD, aligned(i, BLK)] = (dq_s[i, n] * 0.125).astype(bf)
        dkv_ref[aligned(i, BLK)] = dkv_s[aligned(i, BLK)].astype(bf)
        return 0

    lax.fori_loop(0, NB, finish, 0)
    saves = [pltpu.make_async_copy(dqt_ref, dqt_hbm, sem.at[5]), pltpu.make_async_copy(dkv_ref, dkv_hbm, sem.at[6])]
    for c in saves:
        c.start()
    for c in saves:
        c.wait()


def attn_bwd(heads, pairs, qt, kv, kt, dots, o, lse):
    S = qt.shape[1]
    sd = jax.ShapeDtypeStruct
    n = len(heads)
    return pl.pallas_call(
        functools.partial(bwd_kernel, heads),
        out_shape=(sd((n * HD, S), bf), sd((S, n * 128), bf)),
        in_specs=[SM] + [HB] * 5 + [VM], out_specs=(HB, HB),
        scratch_shapes=[pltpu.VMEM((S + BLK, n * 128), f32), pltpu.VMEM((NB + 1, n, HD, BLK), f32),
                        pltpu.VMEM((NB, 8, BLK), f32), pltpu.VMEM((HN * HD, S), bf)]
        + [pltpu.VMEM(a.shape, a.dtype) for a in (qt, kv, kt, dots, o)]
        + [pltpu.VMEM((n * HD, S), bf), pltpu.VMEM((S, n * 128), bf), pltpu.SemaphoreType.DMA((7,))],
        compiler_params=pltpu.CompilerParams(vmem_limit_bytes=60 << 20),
        cost_estimate=pl.CostEstimate(flops=20_000_000_000 * n, bytes_accessed=8_000_000 * n, transcendentals=6_000_000 * n),
        name="tree_attention_grad",
    )(pairs, qt, kv, kt, dots, o, lse)


D = 768
SEQ = 4096
ROWS = SEQ // 4
QW = HN * HD
FQ = 768
AT = FQ
OU = FQ + 256
PK = OU + FQ
MESH = pl.DeviceIdType.MESH
HBM = pl.BlockSpec(memory_space=pl.ANY)
TN = (((0,), (0,)), ((), ()))
epsilon = 1e-05
root_half = 0.7071067811865476
inv_root_tau = 0.3989422804014327


def layer_norm(summed, gain_row, shift_row):
    centre = jnp.mean(summed, axis=-1, keepdims=True)
    offset = summed - centre
    inv_std = lax.rsqrt(jnp.mean(offset * offset, axis=-1, keepdims=True) + epsilon)
    normed = offset * inv_std
    return normed * gain_row + shift_row, normed, inv_std


def norm_back(grad_out, normed, inv_std, gain_row):
    scaled = grad_out * gain_row
    return inv_std * (
        scaled
        - jnp.mean(scaled, axis=-1, keepdims=True)
        - normed * jnp.mean(scaled * normed, axis=-1, keepdims=True)
    )


def gelu_parts(u):
    half = 0.5 * (1.0 + lax.erf(u * root_half))
    return u * half, half + u * inv_root_tau * jnp.exp(-0.5 * u * u)


def partner(x, mask):
    return lax.ppermute(x, "tensor", [(i, i ^ mask) for i in range(4)])


def across_x(x):
    return lax.ppermute(x, "dp", [(i, i ^ 1) for i in range(8)])


def flip1(r):
    return r + 1 - 2 * lax.rem(r, 2)


CH = 4
CROWS = ROWS // CH


def remote(src, dst, s, q, dev):
    return pltpu.make_async_remote_copy(
        src_ref=src, dst_ref=dst, send_sem=s, recv_sem=q, device_id=dev, device_id_type=MESH)


def meet(targets, meanwhile=None):
    barrier = pltpu.get_barrier_semaphore()
    for t in targets:
        pl.semaphore_signal(barrier, inc=1, device_id=t, device_id_type=MESH)
    if meanwhile is not None:
        meanwhile()
    pl.semaphore_wait(barrier, len(targets))


class Sends:
    def __init__(self):
        self.started = []

    def go(self, *args):
        c = remote(*args)
        c.start()
        self.started.append(c)
        return c

    def drain(self):
        for c in self.started:
            c.wait_send()


def gather_kernel(with_w, *refs):
    if with_w:
        (inp, te, wq, w1, w2, w3, bias, whole_hbm, wqg_hbm, gz_hbm, gl_hbm, whole, wqg, gz, bcol,
         ysend, yrecv, csend, crecv, out, zsend, zrecv, xsend, xrecv) = refs
    else:
        inp, te, whole_hbm, whole, ysend, yrecv, csend, crecv, out = refs
    r = lax.axis_index("tensor")
    d = lax.axis_index("dp")
    rc, ry = flip1(r), lax.rem(r + 2, 4)
    core, yy = {"tensor": rc}, {"tensor": ry}
    targets = [core, yy]
    if with_w:
        z, x = d // 2, lax.rem(d, 2)
        xx = {"dp": flip1(d)}
        up, down = {"dp": lax.rem(z + 1, 4) * 2 + x}, {"dp": lax.rem(z + 3, 4) * 2 + x}
        targets += [xx, up, down]

    def prepare():
        shift = te[...].astype(f32)
        whole[r] = (inp[...].astype(f32) + shift).astype(bf)
        if with_w:
            for c in range(3):
                wqg[d, :, c * QW:(c + 1) * QW] = wq[c]

    meet(targets, prepare)
    sends = Sends()
    if with_w:

        def line(a, s, slot, way):
            ref = wqg.at[slot * 2 + x] if a == 0 else gz.at[slot]
            k = 2 * (s - 1) + way
            return remote(ref, ref, zsend.at[a, k], zrecv.at[a, k], (up, down)[way])

        def side(i, slot):
            ref = wqg.at[slot * 2 + x]
            return remote(ref, ref, xsend.at[i], xrecv.at[i], xx)

        def can_send(s, way):
            return jnp.logical_and(z < 3, z - s + 1 >= 0) if way == 0 else jnp.logical_and(z > 0, z + s - 1 <= 3)

        def can_recv(s, way):
            return z - s >= 0 if way == 0 else z + s <= 3

        def own(a):
            for way in (0, 1):
                @pl.when(can_send(1, way))
                def _():
                    line(a, 1, z, way).start()

        own(0)
        side(0, z).start()
    rows = [pl.ds(i * CROWS, CROWS) for i in range(CH)]
    yc = []
    for i in range(CH):
        mine = whole.at[r, rows[i]]
        yc.append(sends.go(mine, mine, ysend.at[i], yrecv.at[i], yy))
    c0 = sends.go(whole.at[r], whole.at[r], csend.at[CH], crecv.at[CH], core)
    if with_w:
        part = wqg.shape[1]
        gz[z, :, 0:FQ] = w1[...]
        gz[z, :, OU:] = w2[...]
        bcol[...] = jnp.transpose(jnp.broadcast_to(bias[...].astype(f32).reshape(1, D), (8, D)))
        fill = OU - AT - QW
        column = bcol[pl.ds(pl.multiple_of(d * part, 32), part), 0:1]
        column = jnp.where(lax.broadcasted_iota(jnp.int32, (part, fill), 1) == 0, column, 0.0)
        gz[z, :, AT:OU] = jnp.concatenate([w3[...].astype(f32).T, column], 1).astype(bf)
        own(1)
        for s in (1, 2, 3):
            for way in (0, 1):
                slot = z - s if way == 0 else z + s

                @pl.when(can_recv(s, way))
                def _():
                    for a in (0, 1):
                        line(a, s, slot, way).wait_recv()
                        if s < 3:
                            @pl.when(can_send(s + 1, way))
                            def _():
                                line(a, s + 1, slot, way).start()
                        if a == 0:
                            side(slot_sem(s, way), slot).start()
    keeps = []

    def keep(src, dst):
        c = pltpu.make_async_copy(src, dst, out.at[len(keeps)])
        c.start()
        keeps.append(c)

    keep(whole.at[r], whole_hbm.at[r])
    cc = []
    for i in range(CH):
        yc[i].wait_recv()
        part = whole.at[ry, rows[i]]
        cc.append(sends.go(part, part, csend.at[i], crecv.at[i], core))
    keep(whole.at[ry], whole_hbm.at[ry])
    c0.wait_recv()
    keep(whole.at[rc], whole_hbm.at[rc])
    for c in cc:
        c.wait_recv()
    rd = 3 - r
    keep(whole.at[rd], whole_hbm.at[rd])
    if with_w:
        keep(gz, gz_hbm)
        keep(gz.at[pl.ds(0, 2)], gl_hbm)
        side(0, z).wait()
        for s in (1, 2, 3):
            for way in (0, 1):
                slot = z - s if way == 0 else z + s

                @pl.when(can_recv(s, way))
                def _():
                    side(slot_sem(s, way), slot).wait()

                @pl.when(can_send(s, way))
                def _():
                    for a in (0, 1):
                        line(a, s, slot_of_send(z, s, way), way).wait_send()
        keep(wqg, wqg_hbm)
    for c in keeps:
        c.wait()
    sends.drain()


def slot_of_send(z, s, way):
    return z - s + 1 if way == 0 else z + s - 1


def slot_sem(s, way):
    return 2 * s - 1 + way


def gather_start(inp, te, *weights):
    with_w = len(weights) > 0
    dma = pltpu.SemaphoreType.DMA
    shapes = [jax.ShapeDtypeStruct((4, ROWS, D), bf)]
    args = [inp, te, *weights]
    scratch = []
    sems = [dma((CH,)), dma((CH,)), dma((CH + 1,)), dma((CH + 1,)), dma((8,))]
    if with_w:
        part = weights[0].shape[1]
        line = jax.ShapeDtypeStruct((4, part, PK), bf)
        shapes += [jax.ShapeDtypeStruct((8, part, 3 * QW), bf), line, jax.ShapeDtypeStruct((2, part, PK), bf)]
        scratch = [pltpu.VMEM((D, 8), f32)]
        sems += [dma((2, 6)), dma((2, 6)), dma((7,)), dma((7,))]
    return pl.pallas_call(
        functools.partial(gather_kernel, with_w),
        out_shape=shapes, in_specs=[VM] * len(args), out_specs=[HB] * len(shapes),
        scratch_shapes=[pltpu.VMEM(a.shape, bf) for a in shapes[:3]] + scratch + sems,
        compiler_params=pltpu.CompilerParams(collective_id=0, has_side_effects=True, vmem_limit_bytes=60 << 20),
        name="gather_start",
    )(*args)


RB = 512
NR = ROWS // RB


def middle_kernel(with_w, *refs):
    if with_w:
        wa, wb, wc, wd = refs[:4]
        step, line_s, xsend, xrecv, wsend, wrecv, ssend, srecv = refs[-8:]
        refs = refs[4:-8]
    else:
        wfull, refs = refs[0], refs[1:]
    (mix_hbm, inp, te, cot, ob, fb, ng, ns, block_out, grad1_o, dots_hbm, p00, p01, p10, p11, sums_o,
     w, wt_s, mix, mixr, gmix, dots, both, ht, gmt, gat, act, gp, slope_s,
     loc, asend, arecv, bsend, brecv, gsend, grecv) = refs
    r = lax.axis_index("tensor")
    d = lax.axis_index("dp")
    x = lax.rem(d, 2)
    ranks = [r, flip1(r), lax.rem(r + 2, 4), 3 - r]
    devices = [{"tensor": k} for k in ranks]
    xx = {"dp": flip1(d)}
    load = pltpu.make_async_copy(mix_hbm, mix, loc.at[5])
    load.start()
    if with_w:
        z = d // 2
        zdev = [{"dp": lax.rem(z + k, 4) * 2 + x} for k in range(4)]
        meet(devices[1:] + [xx] + zdev[1:])
    else:
        meet(devices[1:])
    sends = Sends()
    core = devices[1]
    load.wait()

    def heads_in(b, m):
        cols = pl.ds(b * RB, RB)
        return remote(mix.at[m, :, cols], mixr.at[m, :, cols], asend.at[b, m], arecv.at[b, m], devices[m])

    def heads_out(b, m):
        cols = aligned(b, RB)
        return remote(gmix.at[m, :, cols], dots.at[m, :, cols], bsend.at[b, m], brecv.at[b, m], devices[m])

    heads = [[heads_in(b, m) for m in (3, 2, 1)] for b in range(NR)]
    for c in heads[0]:
        c.start()
    fill = pltpu.make_async_copy(mix.at[0], mixr.at[0], loc.at[0])
    fill.start()

    def weight_moves(j, relay, hand, place):
        rank, side = lax.axis_index("tensor"), lax.rem(lax.axis_index("dp"), 2)
        span = (pl.ds(0, OU), pl.ds(OU, FQ))[j]
        other = lax.rem(rank + 2, 4)
        four, two, end = pl.ds(0, 4), pl.ds(0, 2), pl.ds(2, 2)
        near = {"tensor": flip1(rank)}
        relay(remote(wc.at[end, :, span], w.at[other, end, side, :, span], xsend.at[j], xrecv.at[j],
                     {"dp": flip1(lax.axis_index("dp"))}))
        pieces = ((wa, rank, four, side), (wb, rank, four, 1 - side), (wc, other, four, side), (wd, other, two, 1 - side))
        for i, (ref, t, zz, at) in enumerate(pieces):
            src, dst = ref.at[:, :, span], w.at[t, zz, at, :, span]
            hand(remote(src, dst, wsend.at[j, i], wrecv.at[j, i], near))
            if place is not None:
                place(pltpu.make_async_copy(src, dst, loc.at[11 + 4 * j + i]))

    def whole_fill(j):
        span = (pl.ds(0, OU), pl.ds(OU, FQ))[j]
        return pltpu.make_async_copy(wfull.at[:, :, :, :, span], w.at[:, :, :, :, span], loc.at[1 + j])

    def weight_tail(j):
        rank, side = lax.axis_index("tensor"), lax.rem(lax.axis_index("dp"), 2)
        tail = w.at[lax.rem(rank + 2, 4), pl.ds(2, 2), 1 - side, :, (pl.ds(0, OU), pl.ds(OU, FQ))[j]]
        return remote(tail, tail, wsend.at[j, 4], wrecv.at[j, 4], {"tensor": flip1(rank)})

    if with_w:
        for j in (0, 1):
            weight_moves(j, lambda c: c.start(), lambda c: c.start(), lambda c: c.start())
    else:
        for j in (0, 1):
            whole_fill(j).start()
    for part in heads[1:]:
        for c in part:
            c.start()
    sums_o[...] = jnp.zeros_like(sums_o)
    out_bias, outer_bias = (v[...].astype(f32).reshape(1, D) for v in (ob, fb))
    gains, shifts = ng[...].astype(f32), ns[...].astype(f32)
    gain1, gain2, shift1, shift2 = gains[0:1], gains[1:2], shifts[0:1], shifts[1:2]
    def weights_here(j):
        if with_w:
            def arrived(c):
                c.wait_recv()
                weight_tail(j).start()

            weight_moves(j, arrived, lambda c: c.wait_recv(), lambda c: c.wait())
            weight_tail(j).wait_recv()
        else:
            whole_fill(j).wait()

    weights_here(0)
    fill.wait()
    for t in range(4):
        wt_s[t] = jnp.transpose(w[t, :, :, :, AT:OU].reshape(D, OU - AT))
    bias_in = [wt_s[t, QW:QW + 16].astype(f32)[0:1] for t in range(4)]
    w_in = lambda t: w[t, :, :, :, 0:FQ].reshape(D, FQ)
    w_ou = lambda t: w[t, :, :, :, OU:].reshape(D, FQ)

    def add_sum(i, rows):
        sums_o[i:i + 1] += jnp.sum(rows, axis=0, keepdims=True)

    def block(b, _):
        for i in range(NR):
            @pl.when(b == i)
            def _():
                for c in heads[i]:
                    c.wait_recv()
        rows = aligned(b, RB)
        start = inp[rows].astype(f32) + te[...].astype(f32)
        attn = out_bias
        for m in range(4):
            attn = attn + mm(mixr[m, :, rows], wt_s[ranks[m], :QW], TN)
        hidden, normed1, inv1 = layer_norm(start + attn, gain1, shift1)
        low = hidden.astype(bf)
        ht[:, rows] = low.T
        for t in range(4):
            u = mm(low, w_in(t)) + bias_in[t]
            value, slope = gelu_parts(u)
            act[t, rows] = value.astype(bf)
            slope_s[t] = slope.astype(bf)

        @pl.when(b == 0)
        def _():
            weights_here(1)

        mlp = outer_bias
        for t in range(4):
            mlp = mlp + mm(act[t, rows], w_ou(t), NT)
        final, normed2, inv2 = layer_norm(hidden + mlp, gain2, shift2)
        block_out[rows] = final.astype(bf)
        e = cot[rows].astype(f32)
        add_sum(0, e * normed2)
        add_sum(1, e)
        grad2 = norm_back(e, normed2, inv2, gain2)
        gm = grad2.astype(bf)
        gmt[:, rows] = gm.T
        add_sum(2, gm.astype(f32))
        gin = grad2
        for t in range(4):
            g = (mm(gm, w_ou(t)) * slope_s[t].astype(f32)).astype(bf)
            gp[t, rows] = g
            add_sum(6 + t, g.astype(f32))
            gin = gin + mm(g, w_in(t), NT)
        add_sum(3, gin * normed1)
        add_sum(4, gin)
        grad1 = norm_back(gin, normed1, inv1, gain1)
        grad1_o[rows] = grad1
        ga = grad1.astype(bf)
        gat_rows = ga.T
        gat[:, rows] = gat_rows
        add_sum(5, ga.astype(f32))
        for m in (3, 2, 1):
            gmix[m, :, rows] = mm(wt_s[ranks[m], :QW], gat_rows).astype(bf)
            heads_out(b, m).start()
        dots[0, :, rows] = mm(wt_s[r, :QW], gat_rows).astype(bf)
        return 0

    lax.fori_loop(0, NR, block, 0)

    if with_w:
        for j in (0, 1):
            weight_moves(j, lambda c: c.wait_send(), lambda c: c.wait_send(), None)
            weight_tail(j).wait_send()

    def grads(t, m):
        return (lambda: mm(ht[...], gp[t]), lambda: mm(gmt[...], act[t]), lambda: mm(gat[...], mixr[m], NT))

    cols = (slice(0, FQ), slice(OU, PK), slice(AT, AT + QW))
    blank = jnp.zeros((4, 2, 96, OU - AT - QW), bf)
    cut = lambda g: g.reshape(4, 2, 96, g.shape[1])

    def handing(q):
        return remote(w.at[q], both.at[q], gsend.at[q], grecv.at[q], core)

    hops = []

    def hop(n):
        if not with_w:
            return
        if n:
            hops[-1].wait_recv()
        step[n] = step[n - 1] + step[n + 3] if n else sums_o[...]
        hops.append(sends.go(step.at[n], step.at[n + 4], ssend.at[n], srecv.at[n], (core, devices[2], xx)[n]))

    hop(0)
    for q in (1, 0):
        for c, g in zip(cols, grads(ranks[2 * q + 1], 2 * q + 1)):
            w[q, :, :, :, c] = cut(g().astype(bf))
        w[q, :, :, :, AT + QW:OU] = blank
        handing(q).start()
        hop(2 - q)
    saves = []
    for q in (1, 0):
        mine = grads(ranks[2 * q], 2 * q)
        handing(q).wait_recv()
        for c, g in zip(cols, mine):
            both[q, :, :, :, c] = (both[q, :, :, :, c].astype(f32) + cut(g())).astype(bf)
        for n, side in ((0, x), (1, 1 - x)):
            to = ((p00, p01), (p10, p11))[q][n]
            saves.append(pltpu.make_async_copy(both.at[q, :, side], to, loc.at[6 + 2 * q + n]))
            saves[-1].start()
        if with_w and q:
            hops[-1].wait_recv()
            line_s[z] = step[2] + step[6]
            ends = [sends.go(line_s.at[z], line_s.at[z], ssend.at[2 + k], srecv.at[2 + k], zdev[k]) for k in (1, 2, 3)]
    if with_w:
        for c in ends:
            c.wait_recv()
        sums_o[...] = ((line_s[0] + line_s[1]) + line_s[2]) + line_s[3]
    for b in range(NR):
        for m in (1, 2, 3):
            heads_out(b, m).wait()
        for c in heads[b]:
            c.wait_send()
    saves.append(pltpu.make_async_copy(dots, dots_hbm, loc.at[10]))
    saves[-1].start()
    for c in saves:
        c.wait()
    for q in range(2):
        handing(q).wait_send()
    sends.drain()


def middle(weights, mix, *rest):
    sd = jax.ShapeDtypeStruct
    dma = pltpu.SemaphoreType.DMA
    with_w = len(weights) > 1
    vm = pltpu.VMEM
    tokens = (D, ROWS)
    extra = [vm((7, 16, D), f32), vm((4, 16, D), f32), dma((2,)), dma((2,)), dma((2, 5)), dma((2, 5)),
             dma((6,)), dma((6,))] if with_w else []
    return pl.pallas_call(
        functools.partial(middle_kernel, with_w),
        out_shape=(sd((ROWS, D), bf), sd((ROWS, D), f32), sd((4, QW, ROWS), bf),
                   *([sd((4, 96, PK), bf)] * 4), sd((16, D), f32)),
        in_specs=[HB] * len(weights) + [HB] + [VM] * 7, out_specs=(VM, VM, HB, HB, HB, HB, HB, VM),
        scratch_shapes=[vm((4, 4, 2, 96, PK), bf), vm((4, OU - AT, D), bf), vm((4, QW, ROWS), bf),
                        vm((4, QW, ROWS), bf), vm((4, QW, ROWS), bf), vm((4, QW, ROWS), bf),
                        vm((2, 4, 2, 96, PK), bf), vm(tokens, bf), vm(tokens, bf), vm(tokens, bf),
                        vm((4, ROWS, FQ), bf), vm((4, ROWS, FQ), bf), vm((4, RB, FQ), bf),
                        dma((19,)), dma((NR, 4)), dma((NR, 4)), dma((NR, 4)), dma((NR, 4)), dma((2,)), dma((2,))] + extra,
        compiler_params=pltpu.CompilerParams(collective_id=2, has_side_effects=True, vmem_limit_bytes=63 << 20),
        cost_estimate=pl.CostEstimate(flops=33_000_000_000, bytes_accessed=50_000_000, transcendentals=9_000_000),
        name="middle",
    )(*weights, mix, *rest)


def final_kernel(with_w, *refs):
    if with_w:
        (x_hbm, w_hbm, dqt_hbm, dkv_hbm, g1_hbm, m0_hbm, m1_hbm, m2_hbm, m3_hbm, out, pair, qo, mo,
         x_s, w_s, wr_s, dqt, dkv, grad1, part, crv, ysd, yrv, m0, m1, m2, m3, zsm, zrm, dwq, xrq, zsq, zrq,
         prv, psd, prs, loc, csend, crecv, ysend, yrecv, xsend, xrecv, zsend, zrecv) = refs
    else:
        (x_hbm, w_hbm, dqt_hbm, dkv_hbm, g1_hbm, out, pair, dw,
         x_s, w_s, wr_s, dqt, dkv, grad1, part, crv, ysd, yrv, loc, csend, crecv, ysend, yrecv) = refs
    pulls = [(w_hbm, w_s), (dqt_hbm, dqt), (dkv_hbm, dkv)]
    pulls += [(m0_hbm, m0), (m1_hbm, m1), (m2_hbm, m2), (m3_hbm, m3)] if with_w else []
    pulls += [(x_hbm, x_s), (g1_hbm, grad1)]
    loads = [pltpu.make_async_copy(a, b, loc.at[n]) for n, (a, b) in enumerate(pulls)]
    for c in loads:
        c.start()
    r = lax.axis_index("tensor")
    d = lax.axis_index("dp")
    rc, ry = flip1(r), lax.rem(r + 2, 4)
    rd = 3 - r
    core, yy = {"tensor": rc}, {"tensor": ry}
    targets = [core, yy]
    if with_w:
        z, x = d // 2, lax.rem(d, 2)
        xo = 1 - x
        zs = [lax.rem(z + k, 4) for k in range(4)]
        xx = {"dp": flip1(d)}
        zdev = [{"dp": zs[k] * 2 + x} for k in range(4)]
        targets += [xx] + zdev[1:]
    meet(targets)
    sends = Sends()
    go = sends.go
    wait = lambda *which: [loads[n].wait() for n in which]
    rows = [pl.ds(i * CROWS, CROWS) for i in range(CH)]
    if with_w:
        wait(3, 4, 5, 6)
        zm = []
        for k in (1, 2, 3, 0):
            at = zs[k]
            zsm[k] = ((m0[at].astype(f32) + m1[at].astype(f32)) + (m2[at].astype(f32) + m3[at].astype(f32))).astype(bf)
            if k:
                zm.append(go(zsm.at[k], zrm.at[k - 1], zsend.at[1, k - 1], zrecv.at[1, k - 1], zdev[k]))
    wait(0, 1, 2)
    w = w_s[...].reshape(D, 3 * QW)
    for h in range(HN):
        for c in (1, 2):
            wr_s[:, h * 128 + (c - 1) * HD:h * 128 + c * HD] = w[:, c * QW + h * HD:c * QW + (h + 1) * HD]
    wqs = w[:, :QW]

    def project_back(t, i):
        at = pl.ds(pl.multiple_of(t * ROWS + i * CROWS, CROWS), CROWS)
        part[t, rows[i]] = (mm(dqt[:, at], wqs, (((0,), (1,)), ((), ()))) + mm(dkv[at], wr_s[...], NT)).astype(bf)

    first, second, third = [], [], []
    for i in range(CH):
        project_back(rd, i)
        second.append(go(part.at[rd, rows[i]], crv.at[1, rows[i]], csend.at[1, i], crecv.at[1, i], core))
        project_back(ry, i)
        if i:
            second[i - 1].wait_recv()
            prev = rows[i - 1]
            ysd[prev] = (part[ry, prev].astype(f32) + crv[1, prev].astype(f32)).astype(bf)
            third.append(go(ysd.at[prev], yrv.at[prev], ysend.at[i - 1], yrecv.at[i - 1], yy))
    prev = rows[CH - 1]
    second[CH - 1].wait_recv()
    ysd[prev] = (part[ry, prev].astype(f32) + crv[1, prev].astype(f32)).astype(bf)
    third.append(go(ysd.at[prev], yrv.at[prev], ysend.at[CH - 1], yrecv.at[CH - 1], yy))

    wait(len(loads) - 2)
    whole = x_s[...].reshape(SEQ, D)
    aq = mm(dqt[...], whole)
    akv = mm(dkv[...], whole, TN)
    blocks = [aq]
    for c in (0, 1):
        blocks += [akv[h * 128 + c * HD:h * 128 + (c + 1) * HD] for h in range(HN)]
    dwt = jnp.concatenate(blocks, 0).T.astype(bf)
    sum_q = jnp.sum(dqt[...].astype(f32), axis=1, keepdims=True)
    sum_q = jnp.transpose(jnp.broadcast_to(sum_q, (QW, 8)))
    sum_kv = jnp.sum(dkv[...].astype(f32), axis=0, keepdims=True)
    sum_v = jnp.concatenate([sum_kv[:, h * 128 + HD:(h + 1) * 128] for h in range(HN)], 1)
    pairs = jnp.concatenate([sum_q[0:1], sum_v, jnp.zeros((6, QW), f32)], 0)
    if with_w:
        dwq[...] = dwt.reshape(dwq.shape)
        xq = go(dwq.at[:, xo], xrq, xsend.at[0], xrecv.at[0], xx)
        prs[...] = pairs
        px = go(prs, prv, xsend.at[1], xrecv.at[1], xx)
    for i in range(CH):
        project_back(rc, i)
        first.append(go(part.at[rc, rows[i]], crv.at[0, rows[i]], csend.at[0, i], crecv.at[0, i], core))
        project_back(r, i)
    if with_w:
        px.wait_recv()
        psd[z] = prs[...] + prv[...]
        zp = [go(psd.at[z], psd.at[z], zsend.at[2, k - 1], zrecv.at[2, k - 1], zdev[k]) for k in (1, 2, 3)]
        xq.wait_recv()
        for k in range(4):
            zsq[k] = (dwq[zs[k], x].astype(f32) + xrq[zs[k]].astype(f32)).astype(bf)
        zq = [go(zsq.at[k], zrq.at[k - 1], zsend.at[0, k - 1], zrecv.at[0, k - 1], zdev[k]) for k in (1, 2, 3)]
    else:
        dw[...] = dwt
        pair[...] = pairs
    wait(len(loads) - 1)
    for i in range(CH):
        first[i].wait_recv()
        third[i].wait_recv()
        out[rows[i]] = (part[r, rows[i]].astype(f32) + crv[0, rows[i]].astype(f32)
                        + yrv[rows[i]].astype(f32) + grad1[rows[i]]).astype(bf)
    if with_w:
        for c in zq:
            c.wait_recv()
        whole_q = (zsq[0].astype(f32) + zrq[0].astype(f32)) + (zrq[1].astype(f32) + zrq[2].astype(f32))
        qo[...] = whole_q
        for c in zp:
            c.wait_recv()
        pair[...] = ((psd[0] + psd[1]) + psd[2]) + psd[3]
        for c in zm:
            c.wait_recv()
        mo[...] = (zsm[0].astype(f32) + zrm[0].astype(f32)) + (zrm[1].astype(f32) + zrm[2].astype(f32))
    sends.drain()


def final(whole, w, dqt, dkv, grad1, *more):
    with_w = len(more) > 0
    dma = pltpu.SemaphoreType.DMA
    sd = jax.ShapeDtypeStruct
    vm = pltpu.VMEM
    rows = (ROWS, D)
    like = lambda a: vm(a.shape, a.dtype)
    shapes = [sd(rows, bf), sd((8, QW), f32)]
    args = [whole, w, dqt, dkv, grad1, *more]
    scratch = [like(whole), like(w), vm((D, 2 * QW), bf), like(dqt), like(dkv), like(grad1), vm((4,) + rows, bf),
               vm((2,) + rows, bf), vm(rows, bf), vm(rows, bf)]
    sems = [dma((9,)), dma((2, CH)), dma((2, CH)), dma((CH,)), dma((CH,))]
    if with_w:
        n = w.shape[1]
        shapes += [sd((n, 3 * QW), f32), sd((n, PK), f32)]
        scratch += [like(m) for m in more] + [vm((4, n, PK), bf), vm((3, n, PK), bf),
                    vm((4, 2, n, 3 * QW), bf), vm((4, n, 3 * QW), bf), vm((4, n, 3 * QW), bf), vm((3, n, 3 * QW), bf),
                    vm((8, QW), f32), vm((4, 8, QW), f32), vm((8, QW), f32)]
        sems += [dma((2,)), dma((2,)), dma((3, 3)), dma((3, 3))]
    else:
        shapes += [sd((D, 3 * QW), bf)]
    return pl.pallas_call(
        functools.partial(final_kernel, with_w),
        out_shape=shapes,
        in_specs=[HB] * len(args), out_specs=[VM] * len(shapes),
        scratch_shapes=scratch + sems,
        compiler_params=pltpu.CompilerParams(
            collective_id=1, has_side_effects=True, vmem_limit_bytes=60 << 20),
        name="final",
    )(*args)


def emit_kernel(*refs):
    sources, outs, kept, sem = refs[:6], refs[6:18], refs[18:24], refs[24]
    loads = [pltpu.make_async_copy(a, b, sem.at[n]) for n, (a, b) in enumerate(zip(sources, kept))]
    for c in loads:
        c.start()
    block_out, input_grad, qkv_o, pair_o, out_o, out_b, inner_o, inner_b, outer_o, outer_b, gain_o, shift_o = outs
    saves = [pltpu.make_async_copy(kept[n], to, sem.at[6 + n]) for n, to in enumerate((block_out, input_grad))]
    for n in range(2):
        loads[n].wait()
        saves[n].start()
    for c in loads[2:]:
        c.wait()
    pair, qkv, share, sums = kept[2:]
    for c in range(3):
        qkv_o[c] = qkv[:, c * QW:(c + 1) * QW]
    pair_o[...] = pair[0:2]
    inner_o[...] = share[:, 0:FQ]
    outer_o[...] = share[:, OU:]
    out_o[...] = share[:, AT:OU].T[:QW]
    out_b[...] = sums[5]
    inner_b[...] = sums[6 + lax.axis_index("tensor")]
    outer_b[...] = sums[2]
    gain_o[...] = jnp.concatenate([sums[3:4], sums[0:1]], 0)
    shift_o[...] = jnp.concatenate([sums[4:5], sums[1:2]], 0)
    for c in saves:
        c.wait()


def emit(*arrays):
    sd = jax.ShapeDtypeStruct
    n = arrays[4].shape[0]
    rows = sd((ROWS, D), bf)
    vec = sd((D,), f32)
    shapes = (rows, rows, sd((3, n, QW), f32), sd((2, QW), f32), sd((QW, n), f32), vec, sd((n, FQ), f32), vec,
              sd((n, FQ), f32), vec, sd((2, D), f32), sd((2, D), f32))
    return pl.pallas_call(
        emit_kernel, out_shape=shapes, in_specs=[HB] * 6, out_specs=(HB, HB) + (VM,) * 10,
        scratch_shapes=[pltpu.VMEM(a.shape, a.dtype) for a in arrays] + [pltpu.SemaphoreType.DMA((8,))],
        compiler_params=pltpu.CompilerParams(vmem_limit_bytes=60 << 20),
        name="emit",
    )(*arrays)


def add_low(a, b):
    return (a.astype(f32) + b.astype(f32)).astype(bf)


def on_device(
    ring, input_rows, time_embed, parents, qkv_weight, qv_bias, out_weight, out_bias, inner_weight,
    inner_bias, outer_weight, outer_bias, norm_gain, norm_shift, cotangent,
):
    rank = lax.axis_index("tensor")
    dpos = lax.axis_index("dp")
    part = qkv_weight.shape[0]
    own_ring = ring == 8

    if own_ring:
        whole, w_all, gz, half = gather_start(
            input_rows, time_embed, jnp.transpose(qkv_weight, (1, 0, 2)), inner_weight, outer_weight.T, out_weight,
            inner_bias)
        diagonal = [(i * 4 + j, (i ^ 1) * 4 + (j ^ 2)) for i in range(8) for j in range(4)]
        cross = lambda a: lax.ppermute(a, ("dp", "tensor"), diagonal)
        weights = [gz, across_x(gz), partner(gz, 2), cross(half)]
    else:
        whole = gather_start(input_rows, time_embed)[0]
        w_all = lax.all_gather(qkv_weight.reshape(part, 3 * QW), "dp", axis=0, tiled=True).reshape(8, 96, 3 * QW)
        bias_part = lax.dynamic_slice_in_dim(inner_bias, dpos * part, part, 0)
        packed = jnp.concatenate([inner_weight, out_weight.T, bias_part[:, None],
                                  jnp.zeros((part, OU - AT - QW - 1), bf), outer_weight.T], axis=1)
        packed = lax.all_gather(packed, "dp", axis=0, tiled=True)
        weights = [lax.all_gather(packed, "tensor", axis=0, tiled=False).reshape(4, 4, 2, 96, PK)]

    qt, kv, kt, ot, mix, lse, pairs = attn_fwd(parents, whole, w_all, qv_bias)
    block_out, grad1, dots, *parts, sums = middle(
        weights, mix, input_rows, time_embed, cotangent, out_bias, outer_bias, norm_gain, norm_shift)
    if own_ring:
        parts = [parts[0], across_x(parts[1]), partner(parts[2], 2), cross(parts[3])]
    else:
        far = [partner(parts[2], 2), partner(parts[3], 2)]
    dqt, dkv = attn_bwd((0, 1, 2), pairs, qt, kv, kt, dots, ot, lse)
    if own_ring:
        input_grad, pair, qkv_share, share = final(whole, w_all, dqt, dkv, grad1, *parts)
        (block_out, input_grad, qkv_share, pair, out_share, out_sum, inner_share, inner_sum, outer_share, outer_sum,
         gains, shifts) = emit(block_out, input_grad, pair, qkv_share, share, sums)
        return (block_out, input_grad, jnp.transpose(qkv_share, (1, 0, 2)), pair, out_share, out_sum,
                inner_share, inner_sum, outer_share.T, outer_sum, gains, shifts)
    else:
        input_grad, pair, dwq = final(whole, w_all, dqt, dkv, grad1)
        own, other = add_low(parts[0], far[0]), add_low(parts[1], far[1])
        even = dpos % 2 == 0
        mine = jnp.stack([jnp.where(even, own, other), jnp.where(even, other, own)], axis=1).reshape(D, PK)
        share = lax.psum_scatter(mine, "dp", scatter_dimension=0, tiled=True).astype(f32)
        qkv_share = lax.psum_scatter(dwq, "dp", scatter_dimension=0, tiled=True).astype(f32).reshape(part, 3, QW)
        pair = lax.psum(pair, "dp")
        sums = jnp.sum(lax.all_gather(sums, ("dp", "tensor"), axis=0, tiled=False), axis=0)
    return (
        block_out,
        input_grad,
        qkv_share,
        pair[:2],
        share[:, AT:AT + QW].T,
        sums[5],
        share[:, :FQ],
        lax.dynamic_index_in_dim(sums[6:10], rank, 0, keepdims=False),
        share[:, OU:].T,
        sums[2],
        jnp.stack([sums[3], sums[0]]),
        jnp.stack([sums[4], sums[1]]),
    )


def solution(mesh):
    both = P(("dp", "tensor"), None)
    return jax.shard_map(
        functools.partial(on_device, mesh.shape["dp"]),
        mesh=mesh,
        in_specs=(
            both, P("dp", None), P("dp", None), P("dp", None, "tensor"), P(None, "tensor"),
            P("tensor", "dp"), P(), P("dp", "tensor"), P("tensor"), P("tensor", "dp"), P(), P(), P(), both,
        ),
        out_specs=(
            both, both, P("dp", None, "tensor"), P(None, "tensor"), P("tensor", "dp"), P(),
            P("dp", "tensor"), P("tensor"), P("tensor", "dp"), P(), P(), P(),
        ),
        check_vma=False,
    )
```

```python
import functools
import jax, jax.numpy as jnp
from jax import lax
from jax.experimental import pallas as pl
from jax.experimental.pallas import tpu as pltpu
from jax.sharding import PartitionSpec as P
bf = jnp.bfloat16
f32 = jnp.float32
BLK = 256
TRUNK = 1024
NB = 16
HD = 64
HN = 3
SEGS = 13
PAD = 4
LIST = 192
TQ = 512
TK = 1024
FP = 4
BP = 4
BTQ = 1024
BTK = 256
VM = pl.BlockSpec(memory_space=pltpu.VMEM)
SM = pl.BlockSpec(memory_space=pltpu.SMEM)
HB = pl.BlockSpec(memory_space=pltpu.HBM)
NT = (((1,), (1,)), ((), ()))


def mm(a, b, dims=(((1,), (0,)), ((), ()))):
    return lax.dot_general(a, b, dims, preferred_element_type=f32)


def aligned(i, n):
    return pl.ds(pl.multiple_of(i * n, n), n)


def list_pairs(parents, cur, pairs):
    for s in range(1, SEGS):
        cur[s] = jnp.int32(s)

    def level(_, n):
        for s in range(1, SEGS):
            c = cur[s]
            pairs[0, n] = jnp.int32(s + 3)
            pairs[1, n] = c + 3
            cur[s] = jnp.where(c > 0, parents[0, c], 0)
            n = n + jnp.where(c > 0, 1, 0)
        for i in range(PAD - 1):
            pairs[0, n + i] = jnp.int32(NB)
            pairs[1, n + i] = jnp.int32(NB)
        return (n + PAD - 1) // PAD * PAD

    pairs[2, 0] = lax.fori_loop(0, SEGS - 1, level, jnp.int32(0))


PR = 1024


def fwd_kernel(parents, x_hbm, w_hbm, b_ref, qt_hbm, kv_hbm, kt_hbm, o_hbm, mix_hbm, lse_ref, pairs,
               cur, m_s, acc_s, xs, w_s, wt_s, wr_s, br_s, qt_ref, kv_ref, kt_ref, vt_ref, o_ref, mix_ref, sem):
    def fetch(i, slot):
        return pltpu.make_async_copy(x_hbm.at[i], xs.at[slot], sem.at[slot])

    load_w = pltpu.make_async_copy(w_hbm, w_s, sem.at[2])
    load_w.start()
    fetch(0, 0).start()
    list_pairs(parents, cur, pairs)
    load_w.wait()
    bias = b_ref[...].astype(f32)
    bias = jnp.concatenate([bias[0:1], bias[1:2]], 1)
    w = w_s[...].reshape(w_s.shape[0] * w_s.shape[1], w_s.shape[2])
    wt_s[...] = w[:, :HN * HD].T
    for h in range(HN):
        for c in (1, 2):
            to = slice(h * 128 + (c - 1) * HD, h * 128 + c * HD)
            wr_s[:, to] = w[:, c * HN * HD + h * HD:c * HN * HD + (h + 1) * HD]
            part = bias[:, HN * HD + h * HD:HN * HD + (h + 1) * HD] if c == 2 else jnp.zeros((1, HD), f32)
            br_s[:, to] = jnp.broadcast_to(part, (8, HD))
    bias_col = jnp.transpose(jnp.broadcast_to(bias[:, :HN * HD], (8, HN * HD)))
    ones = (lax.broadcasted_iota(jnp.int32, (16, PR), 0) == 0).astype(f32).astype(bf)

    def rows(i, _):
        slot = lax.rem(i, 2)

        @pl.when(i + 1 < NB * BLK // PR)
        def _():
            fetch(i + 1, 1 - slot).start()

        fetch(i, slot).wait()
        cols = aligned(i, PR)
        x = xs[slot]
        kv = (mm(x, wr_s[...]) + br_s[0:1]).astype(bf)
        kv_ref[cols] = kv
        q = (mm(wt_s[...], x, NT) + bias_col[:, 0:1]).astype(bf)
        qt_ref[:, cols] = (q.astype(f32) * 0.125).astype(bf)
        turned = kv.T
        for h in range(HN):
            kt_ref[h * HD:(h + 1) * HD, cols] = turned[h * 128:h * 128 + HD]
            vt_ref[h, :HD, cols] = turned[h * 128 + HD:(h + 1) * 128]
            vt_ref[h, HD:, cols] = ones
        return 0

    lax.fori_loop(0, NB * BLK // PR, rows, 0)
    saves = [pltpu.make_async_copy(a, b, sem.at[3 + n])
             for n, (a, b) in enumerate(((qt_ref, qt_hbm), (kv_ref, kv_hbm), (kt_ref, kt_hbm)))]
    for c in saves:
        c.start()
    zero = jnp.zeros((HD, TQ), bf)

    def tile(i, _):
        qz = [jnp.concatenate([qt_ref[h * HD:(h + 1) * HD, aligned(i, TQ)], zero], 0) for h in range(HN)]
        m, acc = [None] * HN, [None] * HN
        for c in range(TRUNK // TK):
            ks = slice(c * TK, (c + 1) * TK)
            s = [mm(kv_ref[ks, h * 128:(h + 1) * 128], qz[h]) for h in range(HN)]
            new = [jnp.max(x, axis=0, keepdims=True) for x in s]
            if c:
                new = [jnp.maximum(x, y) for x, y in zip(m, new)]
            p = [jnp.exp(x - y).astype(bf) for x, y in zip(s, new)]
            a = [mm(vt_ref[h, :, ks], p[h]) for h in range(HN)]
            if c:
                a = [x * jnp.exp(y - z) + w for x, y, z, w in zip(acc, m, new, a)]
            m, acc = new, a
        for h in range(HN):
            for j in range(TQ // BLK):
                acc_s[i * (TQ // BLK) + j, h] = acc[h][:, j * BLK:(j + 1) * BLK]
                m_s[i * (TQ // BLK) + j, h:h + 1] = m[h][:, j * BLK:(j + 1) * BLK]
        return 0

    lax.fori_loop(0, NB * BLK // TQ, tile, 0)

    def step(g, _):
        work = []
        for p in range(FP):
            q, kb = pairs[0, g * FP + p], jnp.minimum(pairs[1, g * FP + p], NB - 1)
            work += [(q, aligned(jnp.minimum(q, NB - 1), BLK), aligned(kb, BLK), h) for h in range(HN)]
        s = [mm(kv_ref[ks, h * 128:(h + 1) * 128],
                jnp.concatenate([qt_ref[h * HD:(h + 1) * HD, qs], zero[:, :BLK]], 0)) for q, qs, ks, h in work]
        m = [m_s[q, h:h + 1] for q, qs, ks, h in work]
        new = [jnp.maximum(y, jnp.max(x, axis=0, keepdims=True)) for x, y in zip(s, m)]
        p = [jnp.exp(x - y).astype(bf) for x, y in zip(s, new)]
        a = [mm(vt_ref[h, :, ks], x) for x, (q, qs, ks, h) in zip(p, work)]
        a = [acc_s[q, h] * jnp.exp(x - y) + z for x, y, z, (q, qs, ks, h) in zip(m, new, a, work)]
        for x, y, (q, qs, ks, h) in zip(new, a, work):
            m_s[q, h:h + 1] = x
            acc_s[q, h] = y
        return 0

    lax.fori_loop(0, pairs[2, 0] // FP, step, 0)

    rank = lax.axis_index("tensor")

    def finish(i, _):
        qs = aligned(i, BLK)
        slot = jnp.bitwise_xor(rank, i // 4)
        for h in range(HN):
            total = acc_s[i, h, HD:HD + 1, :]
            out = acc_s[i, h, 0:HD, :] / total
            o_ref[h * HD:(h + 1) * HD, qs] = out
            mix_ref[slot, h * HD:(h + 1) * HD, aligned(lax.rem(i, 4), BLK)] = out.astype(bf)
            lse_ref[h:h + 1, qs] = m_s[i, h:h + 1] + jnp.log(total)
        return 0

    lax.fori_loop(0, NB, finish, 0)
    saves += [pltpu.make_async_copy(mix_ref, mix_hbm, sem.at[6]), pltpu.make_async_copy(o_ref, o_hbm, sem.at[7])]
    for c in saves[3:]:
        c.start()
    for c in saves:
        c.wait()


def attn_fwd(parents, whole, w, bias):
    S = NB * BLK
    sd = jax.ShapeDtypeStruct
    vm = pltpu.VMEM
    n = HN * HD
    d = whole.shape[2]
    return pl.pallas_call(
        fwd_kernel,
        out_shape=(sd((n, S), bf), sd((S, 2 * n), bf), sd((n, S), bf), sd((n, S), f32), sd((4, n, S // 4), bf),
                   sd((8, S), f32), sd((3, LIST), jnp.int32)),
        in_specs=[SM, HB, HB, VM], out_specs=(HB,) * 5 + (VM, SM),
        scratch_shapes=[pltpu.SMEM((16,), jnp.int32), vm((NB + 1, 8, BLK), f32), vm((NB + 1, HN, 80, BLK), f32),
                        vm((2, PR, d), bf), vm(w.shape, bf), vm((n, d), bf), vm((d, 2 * n), bf), vm((8, 2 * n), f32),
                        vm((n, S), bf), vm((S, 2 * n), bf), vm((n, S), bf), vm((HN, 80, S), bf),
                        vm((n, S), f32), vm((4, n, S // 4), bf), pltpu.SemaphoreType.DMA((8,))],
        compiler_params=pltpu.CompilerParams(vmem_limit_bytes=63 << 20),
        cost_estimate=pl.CostEstimate(flops=40_000_000_000, bytes_accessed=12_000_000, transcendentals=18_000_000),
        name="tree_attention",
    )(parents, whole, w, bias)


def bwd_kernel(heads, pairs, qt_hbm, kv_hbm, kt_hbm, dots_hbm, o_hbm, lse_ref, rows_in, dqt_hbm, dkv_hbm, rows_out,
               rows_s, dkv_s, dq_s, st_s, dot_ref, qt_ref, kv_ref, kt_ref, dots, o_ref, dqt_ref, dkv_ref, sem):
    loads = [pltpu.make_async_copy(a, b, sem.at[n]) for n, (a, b) in enumerate((
        (dots_hbm, dots), (o_hbm, o_ref), (qt_hbm, qt_ref), (kv_hbm, kv_ref), (kt_hbm, kt_ref)))]
    for c in loads:
        c.start()
    through = [pltpu.make_async_copy(rows_in, rows_s, sem.at[7]), pltpu.make_async_copy(rows_s, rows_out, sem.at[8])]
    through[0].start()
    dkv_s[...] = jnp.zeros_like(dkv_s)
    dq_s[...] = jnp.zeros_like(dq_s)
    rank = lax.axis_index("tensor")
    loads[0].wait()
    for m in range(4):
        dot_ref[:, aligned(jnp.bitwise_xor(rank, m), NB * BLK // 4)] = dots[m]
    loads[1].wait()

    def stats(i, _):
        qs = aligned(i, BLK)
        for n, h in enumerate(heads):
            rows = slice(h * HD, (h + 1) * HD)
            st_s[i, n:n + 1] = jnp.sum(dot_ref[rows, qs].astype(f32) * o_ref[rows, qs], axis=0, keepdims=True)
            st_s[i, 4 + n:5 + n] = lse_ref[h:h + 1, qs]
        return 0

    lax.fori_loop(0, NB, stats, 0)
    for c in loads[2:]:
        c.wait()
    through[0].wait()
    through[1].start()

    def chains(work, width):
        zero = jnp.zeros((HD, width), bf)
        rows = lambda h: slice(h * HD, (h + 1) * HD)
        qz = [jnp.concatenate([qt_ref[rows(h), qs], zero], 0) for h, qs, ks, lse, delta in work]
        dz = [jnp.concatenate([zero, dot_ref[rows(h), qs]], 0) for h, qs, ks, lse, delta in work]
        kv = [kv_ref[ks, h * 128:(h + 1) * 128] for h, qs, ks, lse, delta in work]
        p = [jnp.exp(mm(x, y) - w[3]) for x, y, w in zip(kv, qz, work)]
        ds = [(x * (mm(y, z) - w[4])).astype(bf) for x, y, z, w in zip(p, kv, dz, work)]
        g = [mm(jnp.concatenate([x, y.astype(bf)], 1), jnp.concatenate([z, u], 1), NT)
             for x, y, z, u in zip(ds, p, qz, dz)]
        return g, [mm(kt_ref[rows(h), ks], x) for x, (h, qs, ks, lse, delta) in zip(ds, work)]

    per = BTQ // BLK

    def tile(i, _):
        row = lambda k: jnp.concatenate([st_s[i * per + j, k:k + 1] for j in range(per)], 1)
        dq = [None] * len(heads)
        for c in range(TRUNK // BTK):
            ks = slice(c * BTK, (c + 1) * BTK)
            g, d = chains([(h, aligned(i, BTQ), ks, row(4 + n), row(n)) for n, h in enumerate(heads)], BTQ)
            for n in range(len(heads)):
                dkv_s[ks, n * 128:(n + 1) * 128] += g[n]
                dq[n] = d[n] if c == 0 else dq[n] + d[n]
        for n in range(len(heads)):
            for j in range(per):
                dq_s[i * per + j, n] += dq[n][:, j * BLK:(j + 1) * BLK]
        return 0

    lax.fori_loop(0, NB * BLK // BTQ, tile, 0)

    def step(s, _):
        work, where = [], []
        for p in range(BP):
            q, kb = pairs[0, s * BP + p], pairs[1, s * BP + p]
            qr = jnp.minimum(q, NB - 1)
            for n, h in enumerate(heads):
                work.append((h, aligned(qr, BLK), aligned(jnp.minimum(kb, NB - 1), BLK),
                             st_s[qr, 4 + n:5 + n], st_s[qr, n:n + 1]))
                where.append((q, kb, n))
        for g, d, (q, kb, n) in zip(*chains(work, BLK), where):
            dkv_s[aligned(kb, BLK), n * 128:(n + 1) * 128] += g
            dq_s[q, n] += d
        return 0

    lax.fori_loop(0, pairs[2, 0] // BP, step, 0)

    def finish(i, _):
        for n in range(len(heads)):
            dqt_ref[n * HD:(n + 1) * HD, aligned(i, BLK)] = (dq_s[i, n] * 0.125).astype(bf)
        dkv_ref[aligned(i, BLK)] = dkv_s[aligned(i, BLK)].astype(bf)
        save(i).start()
        return 0

    def save(i):
        return pltpu.make_async_copy(dkv_ref.at[aligned(i, BLK)], dkv_hbm.at[aligned(i, BLK)], sem.at[9 + i])

    lax.fori_loop(0, NB, finish, 0)
    last = pltpu.make_async_copy(dqt_ref, dqt_hbm, sem.at[5])
    last.start()
    for i in range(NB):
        save(i).wait()
    last.wait()
    through[1].wait()


def attn_bwd(heads, pairs, qt, kv, kt, dots, o, lse, rows):
    S = qt.shape[1]
    sd = jax.ShapeDtypeStruct
    n = len(heads)
    return pl.pallas_call(
        functools.partial(bwd_kernel, heads),
        out_shape=(sd((n * HD, S), bf), sd((S, n * 128), bf), sd(rows.shape, rows.dtype)),
        in_specs=[SM] + [HB] * 5 + [VM, HB], out_specs=(HB, HB, HB),
        scratch_shapes=[pltpu.VMEM(rows.shape, rows.dtype), pltpu.VMEM((S + BLK, n * 128), f32), pltpu.VMEM((NB + 1, n, HD, BLK), f32),
                        pltpu.VMEM((NB, 8, BLK), f32), pltpu.VMEM((HN * HD, S), bf)]
        + [pltpu.VMEM(a.shape, a.dtype) for a in (qt, kv, kt, dots, o)]
        + [pltpu.VMEM((n * HD, S), bf), pltpu.VMEM((S, n * 128), bf), pltpu.SemaphoreType.DMA((9 + NB,))],
        compiler_params=pltpu.CompilerParams(vmem_limit_bytes=63 << 20),
        cost_estimate=pl.CostEstimate(flops=20_000_000_000 * n, bytes_accessed=8_000_000 * n, transcendentals=6_000_000 * n),
        name="tree_attention_grad",
    )(pairs, qt, kv, kt, dots, o, lse, rows)


D = 768
SEQ = 4096
ROWS = SEQ // 4
QW = HN * HD
FQ = 768
AT = FQ
OU = FQ + 256
PK = OU + FQ
MESH = pl.DeviceIdType.MESH
HBM = pl.BlockSpec(memory_space=pl.ANY)
TN = (((0,), (0,)), ((), ()))
epsilon = 1e-05
root_half = 0.7071067811865476
inv_root_tau = 0.3989422804014327


def layer_norm(summed, gain_row, shift_row):
    centre = jnp.mean(summed, axis=-1, keepdims=True)
    offset = summed - centre
    inv_std = lax.rsqrt(jnp.mean(offset * offset, axis=-1, keepdims=True) + epsilon)
    normed = offset * inv_std
    return normed * gain_row + shift_row, normed, inv_std


def norm_back(grad_out, normed, inv_std, gain_row):
    scaled = grad_out * gain_row
    return inv_std * (
        scaled
        - jnp.mean(scaled, axis=-1, keepdims=True)
        - normed * jnp.mean(scaled * normed, axis=-1, keepdims=True)
    )


def gelu_parts(u):
    half = 0.5 * (1.0 + lax.erf(u * root_half))
    return u * half, half + u * inv_root_tau * jnp.exp(-0.5 * u * u)


def partner(x, mask):
    return lax.ppermute(x, "tensor", [(i, i ^ mask) for i in range(4)])


def across_x(x):
    return lax.ppermute(x, "dp", [(i, i ^ 1) for i in range(8)])


def flip1(r):
    return r + 1 - 2 * lax.rem(r, 2)


CH = 4
CROWS = ROWS // CH


def remote(src, dst, s, q, dev):
    return pltpu.make_async_remote_copy(
        src_ref=src, dst_ref=dst, send_sem=s, recv_sem=q, device_id=dev, device_id_type=MESH)


def meet(targets, meanwhile=None):
    barrier = pltpu.get_barrier_semaphore()
    for t in targets:
        pl.semaphore_signal(barrier, inc=1, device_id=t, device_id_type=MESH)
    if meanwhile is not None:
        meanwhile()
    pl.semaphore_wait(barrier, len(targets))


class Sends:
    def __init__(self):
        self.started = []

    def go(self, *args):
        c = remote(*args)
        c.start()
        self.started.append(c)
        return c

    def drain(self):
        for c in self.started:
            c.wait_send()


def gather_kernel(with_w, *refs):
    if with_w:
        (inp, te, wq, w1, w2, w3, bias, whole_hbm, wqg_hbm, gz_hbm, gl_hbm, whole, wqg, gz, bcol,
         ysend, yrecv, csend, crecv, out, zsend, zrecv, xsend, xrecv) = refs
    else:
        inp, te, whole_hbm, whole, ysend, yrecv, csend, crecv, out = refs
    r = lax.axis_index("tensor")
    d = lax.axis_index("dp")
    rc, ry = flip1(r), lax.rem(r + 2, 4)
    core, yy = {"tensor": rc}, {"tensor": ry}
    targets = [core, yy]
    if with_w:
        z, x = d // 2, lax.rem(d, 2)
        xx = {"dp": flip1(d)}
        up, down = {"dp": lax.rem(z + 1, 4) * 2 + x}, {"dp": lax.rem(z + 3, 4) * 2 + x}
        targets += [xx, up, down]

    def prepare():
        shift = te[...].astype(f32)
        whole[r] = (inp[...].astype(f32) + shift).astype(bf)
        if with_w:
            for c in range(3):
                wqg[d, :, c * QW:(c + 1) * QW] = wq[c]

    meet(targets, prepare)
    sends = Sends()
    if with_w:

        def line(a, s, slot, way):
            ref = wqg.at[slot * 2 + x] if a == 0 else gz.at[slot]
            k = 2 * (s - 1) + way
            return remote(ref, ref, zsend.at[a, k], zrecv.at[a, k], (up, down)[way])

        def side(i, slot):
            ref = wqg.at[slot * 2 + x]
            return remote(ref, ref, xsend.at[i], xrecv.at[i], xx)

        def can_send(s, way):
            return jnp.logical_and(z < 3, z - s + 1 >= 0) if way == 0 else jnp.logical_and(z > 0, z + s - 1 <= 3)

        def can_recv(s, way):
            return z - s >= 0 if way == 0 else z + s <= 3

        def own(a):
            for way in (0, 1):
                @pl.when(can_send(1, way))
                def _():
                    line(a, 1, z, way).start()

        own(0)
        side(0, z).start()
    rows = [pl.ds(i * CROWS, CROWS) for i in range(CH)]
    yc = []
    for i in range(CH):
        mine = whole.at[r, rows[i]]
        yc.append(sends.go(mine, mine, ysend.at[i], yrecv.at[i], yy))
    c0 = sends.go(whole.at[r], whole.at[r], csend.at[CH], crecv.at[CH], core)
    if with_w:
        part = wqg.shape[1]
        gz[z, :, 0:FQ] = w1[...]
        gz[z, :, OU:] = w2[...]
        bcol[...] = jnp.transpose(jnp.broadcast_to(bias[...].astype(f32).reshape(1, D), (8, D)))
        fill = OU - AT - QW
        column = bcol[pl.ds(pl.multiple_of(d * part, 32), part), 0:1]
        column = jnp.where(lax.broadcasted_iota(jnp.int32, (part, fill), 1) == 0, column, 0.0)
        gz[z, :, AT:OU] = jnp.concatenate([w3[...].astype(f32).T, column], 1).astype(bf)
        own(1)
        for s in (1, 2, 3):
            for way in (0, 1):
                slot = z - s if way == 0 else z + s

                @pl.when(can_recv(s, way))
                def _():
                    for a in (0, 1):
                        line(a, s, slot, way).wait_recv()
                        if s < 3:
                            @pl.when(can_send(s + 1, way))
                            def _():
                                line(a, s + 1, slot, way).start()
                        if a == 0:
                            side(slot_sem(s, way), slot).start()
    keeps = []

    def keep(src, dst):
        c = pltpu.make_async_copy(src, dst, out.at[len(keeps)])
        c.start()
        keeps.append(c)

    keep(whole.at[r], whole_hbm.at[r])
    cc = []
    for i in range(CH):
        yc[i].wait_recv()
        part = whole.at[ry, rows[i]]
        cc.append(sends.go(part, part, csend.at[i], crecv.at[i], core))
    keep(whole.at[ry], whole_hbm.at[ry])
    c0.wait_recv()
    keep(whole.at[rc], whole_hbm.at[rc])
    for c in cc:
        c.wait_recv()
    rd = 3 - r
    keep(whole.at[rd], whole_hbm.at[rd])
    if with_w:
        keep(gz, gz_hbm)
        keep(gz.at[pl.ds(0, 2)], gl_hbm)
        side(0, z).wait()
        for s in (1, 2, 3):
            for way in (0, 1):
                slot = z - s if way == 0 else z + s

                @pl.when(can_recv(s, way))
                def _():
                    side(slot_sem(s, way), slot).wait()

                @pl.when(can_send(s, way))
                def _():
                    for a in (0, 1):
                        line(a, s, slot_of_send(z, s, way), way).wait_send()
        keep(wqg, wqg_hbm)
    for c in keeps:
        c.wait()
    sends.drain()


def slot_of_send(z, s, way):
    return z - s + 1 if way == 0 else z + s - 1


def slot_sem(s, way):
    return 2 * s - 1 + way


def gather_start(inp, te, *weights):
    with_w = len(weights) > 0
    dma = pltpu.SemaphoreType.DMA
    shapes = [jax.ShapeDtypeStruct((4, ROWS, D), bf)]
    args = [inp, te, *weights]
    scratch = []
    sems = [dma((CH,)), dma((CH,)), dma((CH + 1,)), dma((CH + 1,)), dma((8,))]
    if with_w:
        part = weights[0].shape[1]
        line = jax.ShapeDtypeStruct((4, part, PK), bf)
        shapes += [jax.ShapeDtypeStruct((8, part, 3 * QW), bf), line, jax.ShapeDtypeStruct((2, part, PK), bf)]
        scratch = [pltpu.VMEM((D, 8), f32)]
        sems += [dma((2, 6)), dma((2, 6)), dma((7,)), dma((7,))]
    return pl.pallas_call(
        functools.partial(gather_kernel, with_w),
        out_shape=shapes, in_specs=[VM] * len(args), out_specs=[HB] * len(shapes),
        scratch_shapes=[pltpu.VMEM(a.shape, bf) for a in shapes[:3]] + scratch + sems,
        compiler_params=pltpu.CompilerParams(collective_id=0, has_side_effects=True, vmem_limit_bytes=60 << 20),
        name="gather_start",
    )(*args)


RB = 512
NR = ROWS // RB


def middle_kernel(with_w, *refs):
    if with_w:
        wa, wb, wc, wd = refs[:4]
        step, line_s, xsend, xrecv, wsend, wrecv, ssend, srecv = refs[-8:]
        refs = refs[4:-8]
    else:
        wfull, refs = refs[0], refs[1:]
    (mix_hbm, inp_hbm, te, cot_hbm, ob, fb, ng, ns, block_hbm, grad1_hbm, dots_hbm, p00, p01, p10, p11, sums_o,
     inp, cot, block_out, grad1_o, w, wt_s, mix, mixr, gmix, dots, both, ht, gmt, gat, act, gp, slope_s,
     loc, asend, arecv, bsend, brecv, gsend, grecv) = refs
    r = lax.axis_index("tensor")
    d = lax.axis_index("dp")
    x = lax.rem(d, 2)
    ranks = [r, flip1(r), lax.rem(r + 2, 4), 3 - r]
    devices = [{"tensor": k} for k in ranks]
    xx = {"dp": flip1(d)}
    load = pltpu.make_async_copy(mix_hbm, mix, loc.at[5])
    load.start()
    rows_in = [pltpu.make_async_copy(inp_hbm, inp, loc.at[19]), pltpu.make_async_copy(cot_hbm, cot, loc.at[20])]
    for c in rows_in:
        c.start()
    if with_w:
        z = d // 2
        zdev = [{"dp": lax.rem(z + k, 4) * 2 + x} for k in range(4)]
        meet(devices[1:] + [xx] + zdev[1:])
    else:
        meet(devices[1:])
    sends = Sends()
    core = devices[1]
    load.wait()

    def heads_in(b, m):
        cols = pl.ds(b * RB, RB)
        return remote(mix.at[m, :, cols], mixr.at[m, :, cols], asend.at[b, m], arecv.at[b, m], devices[m])

    def heads_out(b, m):
        cols = aligned(b, RB)
        return remote(gmix.at[m, :, cols], dots.at[m, :, cols], bsend.at[b, m], brecv.at[b, m], devices[m])

    heads = [[heads_in(b, m) for m in (3, 2, 1)] for b in range(NR)]
    for c in heads[0]:
        c.start()
    fill = pltpu.make_async_copy(mix.at[0], mixr.at[0], loc.at[0])
    fill.start()

    def weight_moves(j, relay, hand, place):
        rank, side = lax.axis_index("tensor"), lax.rem(lax.axis_index("dp"), 2)
        span = (pl.ds(0, OU), pl.ds(OU, FQ))[j]
        other = lax.rem(rank + 2, 4)
        four, two, end = pl.ds(0, 4), pl.ds(0, 2), pl.ds(2, 2)
        near = {"tensor": flip1(rank)}
        relay(remote(wc.at[end, :, span], w.at[other, end, side, :, span], xsend.at[j], xrecv.at[j],
                     {"dp": flip1(lax.axis_index("dp"))}))
        pieces = ((wa, rank, four, side), (wb, rank, four, 1 - side), (wc, other, four, side), (wd, other, two, 1 - side))
        for i, (ref, t, zz, at) in enumerate(pieces):
            src, dst = ref.at[:, :, span], w.at[t, zz, at, :, span]
            hand(remote(src, dst, wsend.at[j, i], wrecv.at[j, i], near))
            if place is not None:
                place(pltpu.make_async_copy(src, dst, loc.at[11 + 4 * j + i]))

    def whole_fill(j):
        span = (pl.ds(0, OU), pl.ds(OU, FQ))[j]
        return pltpu.make_async_copy(wfull.at[:, :, :, :, span], w.at[:, :, :, :, span], loc.at[1 + j])

    def weight_tail(j):
        rank, side = lax.axis_index("tensor"), lax.rem(lax.axis_index("dp"), 2)
        tail = w.at[lax.rem(rank + 2, 4), pl.ds(2, 2), 1 - side, :, (pl.ds(0, OU), pl.ds(OU, FQ))[j]]
        return remote(tail, tail, wsend.at[j, 4], wrecv.at[j, 4], {"tensor": flip1(rank)})

    if with_w:
        for j in (0, 1):
            weight_moves(j, lambda c: c.start(), lambda c: c.start(), lambda c: c.start())
    else:
        for j in (0, 1):
            whole_fill(j).start()
    for part in heads[1:]:
        for c in part:
            c.start()
    sums_o[...] = jnp.zeros_like(sums_o)
    out_bias, outer_bias = (v[...].astype(f32).reshape(1, D) for v in (ob, fb))
    gains, shifts = ng[...].astype(f32), ns[...].astype(f32)
    gain1, gain2, shift1, shift2 = gains[0:1], gains[1:2], shifts[0:1], shifts[1:2]
    def weights_here(j):
        if with_w:
            def arrived(c):
                c.wait_recv()
                weight_tail(j).start()

            weight_moves(j, arrived, lambda c: c.wait_recv(), lambda c: c.wait())
            weight_tail(j).wait_recv()
        else:
            whole_fill(j).wait()

    weights_here(0)
    fill.wait()
    for c in rows_in:
        c.wait()
    for t in range(4):
        wt_s[t] = jnp.transpose(w[t, :, :, :, AT:OU].reshape(D, OU - AT))
    bias_in = [wt_s[t, QW:QW + 16].astype(f32)[0:1] for t in range(4)]
    w_in = lambda t: w[t, :, :, :, 0:FQ].reshape(D, FQ)
    w_ou = lambda t: w[t, :, :, :, OU:].reshape(D, FQ)

    def add_sum(i, rows):
        sums_o[i:i + 1] += jnp.sum(rows, axis=0, keepdims=True)

    def block(b, _):
        for i in range(NR):
            @pl.when(b == i)
            def _():
                for c in heads[i]:
                    c.wait_recv()
        rows = aligned(b, RB)
        start = inp[rows].astype(f32) + te[...].astype(f32)
        attn = out_bias
        for m in range(4):
            attn = attn + mm(mixr[m, :, rows], wt_s[ranks[m], :QW], TN)
        hidden, normed1, inv1 = layer_norm(start + attn, gain1, shift1)
        low = hidden.astype(bf)
        ht[:, rows] = low.T
        for t in range(4):
            u = mm(low, w_in(t)) + bias_in[t]
            value, slope = gelu_parts(u)
            act[t, rows] = value.astype(bf)
            slope_s[t] = slope.astype(bf)

        @pl.when(b == 0)
        def _():
            weights_here(1)

        mlp = outer_bias
        for t in range(4):
            mlp = mlp + mm(act[t, rows], w_ou(t), NT)
        final, normed2, inv2 = layer_norm(hidden + mlp, gain2, shift2)
        block_out[rows] = final.astype(bf)
        e = cot[rows].astype(f32)
        add_sum(0, e * normed2)
        add_sum(1, e)
        grad2 = norm_back(e, normed2, inv2, gain2)
        gm = grad2.astype(bf)
        gmt[:, rows] = gm.T
        add_sum(2, gm.astype(f32))
        gin = grad2
        for t in range(4):
            g = (mm(gm, w_ou(t)) * slope_s[t].astype(f32)).astype(bf)
            gp[t, rows] = g
            add_sum(6 + t, g.astype(f32))
            gin = gin + mm(g, w_in(t), NT)
        add_sum(3, gin * normed1)
        add_sum(4, gin)
        grad1 = norm_back(gin, normed1, inv1, gain1)
        grad1_o[rows] = grad1
        ga = grad1.astype(bf)
        gat_rows = ga.T
        gat[:, rows] = gat_rows
        add_sum(5, ga.astype(f32))
        for m in (3, 2, 1):
            gmix[m, :, rows] = mm(wt_s[ranks[m], :QW], gat_rows).astype(bf)
            heads_out(b, m).start()
        dots[0, :, rows] = mm(wt_s[r, :QW], gat_rows).astype(bf)
        return 0

    lax.fori_loop(0, NR, block, 0)

    if with_w:
        for j in (0, 1):
            weight_moves(j, lambda c: c.wait_send(), lambda c: c.wait_send(), None)
            weight_tail(j).wait_send()

    def grads(t, m):
        return (lambda: mm(ht[...], gp[t]), lambda: mm(gmt[...], act[t]), lambda: mm(gat[...], mixr[m], NT))

    cols = (slice(0, FQ), slice(OU, PK), slice(AT, AT + QW))
    blank = jnp.zeros((4, 2, 96, OU - AT - QW), bf)
    cut = lambda g: g.reshape(4, 2, 96, g.shape[1])

    def handing(q):
        return remote(w.at[q], both.at[q], gsend.at[q], grecv.at[q], core)

    hops = []

    def hop(n):
        if not with_w:
            return
        if n:
            hops[-1].wait_recv()
        step[n] = step[n - 1] + step[n + 3] if n else sums_o[...]
        hops.append(sends.go(step.at[n], step.at[n + 4], ssend.at[n], srecv.at[n], (core, devices[2], xx)[n]))

    hop(0)
    saves = [pltpu.make_async_copy(grad1_o, grad1_hbm, loc.at[21]), pltpu.make_async_copy(block_out, block_hbm, loc.at[22])]
    for c in saves:
        c.start()
    for q in (1, 0):
        for c, g in zip(cols, grads(ranks[2 * q + 1], 2 * q + 1)):
            w[q, :, :, :, c] = cut(g().astype(bf))
        w[q, :, :, :, AT + QW:OU] = blank
        handing(q).start()
        hop(2 - q)
    for q in (1, 0):
        mine = grads(ranks[2 * q], 2 * q)
        handing(q).wait_recv()
        for c, g in zip(cols, mine):
            both[q, :, :, :, c] = (both[q, :, :, :, c].astype(f32) + cut(g())).astype(bf)
        for n, side in ((0, x), (1, 1 - x)):
            to = ((p00, p01), (p10, p11))[q][n]
            saves.append(pltpu.make_async_copy(both.at[q, :, side], to, loc.at[6 + 2 * q + n]))
            saves[-1].start()
        if with_w and q:
            hops[-1].wait_recv()
            line_s[z] = step[2] + step[6]
            ends = [sends.go(line_s.at[z], line_s.at[z], ssend.at[2 + k], srecv.at[2 + k], zdev[k]) for k in (1, 2, 3)]
    if with_w:
        for c in ends:
            c.wait_recv()
        sums_o[...] = ((line_s[0] + line_s[1]) + line_s[2]) + line_s[3]
    for b in range(NR):
        for m in (1, 2, 3):
            heads_out(b, m).wait()
        for c in heads[b]:
            c.wait_send()
    saves.append(pltpu.make_async_copy(dots, dots_hbm, loc.at[10]))
    saves[-1].start()
    for c in saves:
        c.wait()
    for q in range(2):
        handing(q).wait_send()
    sends.drain()


def middle(weights, mix, *rest):
    sd = jax.ShapeDtypeStruct
    dma = pltpu.SemaphoreType.DMA
    with_w = len(weights) > 1
    vm = pltpu.VMEM
    tokens = (D, ROWS)
    extra = [vm((7, 16, D), f32), vm((4, 16, D), f32), dma((2,)), dma((2,)), dma((2, 5)), dma((2, 5)),
             dma((6,)), dma((6,))] if with_w else []
    return pl.pallas_call(
        functools.partial(middle_kernel, with_w),
        out_shape=(sd((ROWS, D), bf), sd((ROWS, D), f32), sd((4, QW, ROWS), bf),
                   *([sd((4, 96, PK), bf)] * 4), sd((16, D), f32)),
        in_specs=[HB] * len(weights) + [HB, HB, VM, HB] + [VM] * 4, out_specs=(HB, HB, HB, HB, HB, HB, HB, VM),
        scratch_shapes=[vm((ROWS, D), bf), vm((ROWS, D), bf), vm((ROWS, D), bf), vm((ROWS, D), f32),
                        vm((4, 4, 2, 96, PK), bf), vm((4, OU - AT, D), bf), vm((4, QW, ROWS), bf),
                        vm((4, QW, ROWS), bf), vm((4, QW, ROWS), bf), vm((4, QW, ROWS), bf),
                        vm((2, 4, 2, 96, PK), bf), vm(tokens, bf), vm(tokens, bf), vm(tokens, bf),
                        vm((4, ROWS, FQ), bf), vm((4, ROWS, FQ), bf), vm((4, RB, FQ), bf),
                        dma((23,)), dma((NR, 4)), dma((NR, 4)), dma((NR, 4)), dma((NR, 4)), dma((2,)), dma((2,))] + extra,
        compiler_params=pltpu.CompilerParams(collective_id=2, has_side_effects=True, vmem_limit_bytes=63 << 20),
        cost_estimate=pl.CostEstimate(flops=33_000_000_000, bytes_accessed=50_000_000, transcendentals=9_000_000),
        name="middle",
    )(*weights, mix, *rest)


def final_kernel(with_w, *refs):
    if with_w:
        (x_hbm, w_hbm, dqt_hbm, dkv_hbm, g1_hbm, m0_hbm, m1_hbm, m2_hbm, m3_hbm, out, pair, qo, mo,
         x_s, w_s, wr_s, dqt, dkv, grad1, part, crv, ysd, yrv, m0, m1, m2, m3, zsm, zrm, dwq, xrq, zsq, zrq,
         prv, psd, prs, loc, csend, crecv, ysend, yrecv, xsend, xrecv, zsend, zrecv) = refs
    else:
        (x_hbm, w_hbm, dqt_hbm, dkv_hbm, g1_hbm, out, pair, dw,
         x_s, w_s, wr_s, dqt, dkv, grad1, part, crv, ysd, yrv, loc, csend, crecv, ysend, yrecv) = refs
    pulls = [(w_hbm, w_s), (dqt_hbm, dqt), (dkv_hbm, dkv)]
    pulls += [(m0_hbm, m0), (m1_hbm, m1), (m2_hbm, m2), (m3_hbm, m3)] if with_w else []
    pulls += [(x_hbm, x_s), (g1_hbm, grad1)]
    loads = [pltpu.make_async_copy(a, b, loc.at[n]) for n, (a, b) in enumerate(pulls)]
    for c in loads[:-2]:
        c.start()
    r = lax.axis_index("tensor")
    d = lax.axis_index("dp")
    rc, ry = flip1(r), lax.rem(r + 2, 4)
    rd = 3 - r
    core, yy = {"tensor": rc}, {"tensor": ry}
    targets = [core, yy]
    if with_w:
        z, x = d // 2, lax.rem(d, 2)
        xo = 1 - x
        zs = [lax.rem(z + k, 4) for k in range(4)]
        xx = {"dp": flip1(d)}
        zdev = [{"dp": zs[k] * 2 + x} for k in range(4)]
        targets += [xx] + zdev[1:]
    meet(targets)
    sends = Sends()
    go = sends.go
    wait = lambda *which: [loads[n].wait() for n in which]
    rows = [pl.ds(i * CROWS, CROWS) for i in range(CH)]
    if with_w:
        wait(3, 4, 5, 6)
        zm = []
        for k in (1, 2, 3, 0):
            at = zs[k]
            zsm[k] = ((m0[at].astype(f32) + m1[at].astype(f32)) + (m2[at].astype(f32) + m3[at].astype(f32))).astype(bf)
            if k:
                zm.append(go(zsm.at[k], zrm.at[k - 1], zsend.at[1, k - 1], zrecv.at[1, k - 1], zdev[k]))
    wait(0, 1, 2)
    for c in loads[-2:]:
        c.start()
    w = w_s[...].reshape(D, 3 * QW)
    for h in range(HN):
        for c in (1, 2):
            wr_s[:, h * 128 + (c - 1) * HD:h * 128 + c * HD] = w[:, c * QW + h * HD:c * QW + (h + 1) * HD]
    wqs = w[:, :QW]

    def project_back(t, i):
        at = pl.ds(pl.multiple_of(t * ROWS + i * CROWS, CROWS), CROWS)
        part[t, rows[i]] = (mm(dqt[:, at], wqs, (((0,), (1,)), ((), ()))) + mm(dkv[at], wr_s[...], NT)).astype(bf)

    first, second, third = [], [], []
    for i in range(CH):
        project_back(rd, i)
        second.append(go(part.at[rd, rows[i]], crv.at[1, rows[i]], csend.at[1, i], crecv.at[1, i], core))
        project_back(ry, i)
        if i:
            second[i - 1].wait_recv()
            prev = rows[i - 1]
            ysd[prev] = (part[ry, prev].astype(f32) + crv[1, prev].astype(f32)).astype(bf)
            third.append(go(ysd.at[prev], yrv.at[prev], ysend.at[i - 1], yrecv.at[i - 1], yy))
    prev = rows[CH - 1]
    second[CH - 1].wait_recv()
    ysd[prev] = (part[ry, prev].astype(f32) + crv[1, prev].astype(f32)).astype(bf)
    third.append(go(ysd.at[prev], yrv.at[prev], ysend.at[CH - 1], yrecv.at[CH - 1], yy))

    wait(len(loads) - 2)
    whole = x_s[...].reshape(SEQ, D)
    aq = mm(dqt[...], whole)
    akv = mm(dkv[...], whole, TN)
    blocks = [aq]
    for c in (0, 1):
        blocks += [akv[h * 128 + c * HD:h * 128 + (c + 1) * HD] for h in range(HN)]
    dwt = jnp.concatenate(blocks, 0).T.astype(bf)
    sum_q = jnp.sum(dqt[...].astype(f32), axis=1, keepdims=True)
    sum_q = jnp.transpose(jnp.broadcast_to(sum_q, (QW, 8)))
    sum_kv = jnp.sum(dkv[...].astype(f32), axis=0, keepdims=True)
    sum_v = jnp.concatenate([sum_kv[:, h * 128 + HD:(h + 1) * 128] for h in range(HN)], 1)
    pairs = jnp.concatenate([sum_q[0:1], sum_v, jnp.zeros((6, QW), f32)], 0)
    if with_w:
        dwq[...] = dwt.reshape(dwq.shape)
        xq = go(dwq.at[:, xo], xrq, xsend.at[0], xrecv.at[0], xx)
        prs[...] = pairs
        px = go(prs, prv, xsend.at[1], xrecv.at[1], xx)
    for i in range(CH):
        project_back(rc, i)
        first.append(go(part.at[rc, rows[i]], crv.at[0, rows[i]], csend.at[0, i], crecv.at[0, i], core))
        project_back(r, i)
    if with_w:
        px.wait_recv()
        psd[z] = prs[...] + prv[...]
        zp = [go(psd.at[z], psd.at[z], zsend.at[2, k - 1], zrecv.at[2, k - 1], zdev[k]) for k in (1, 2, 3)]
        xq.wait_recv()
        for k in range(4):
            zsq[k] = (dwq[zs[k], x].astype(f32) + xrq[zs[k]].astype(f32)).astype(bf)
        zq = [go(zsq.at[k], zrq.at[k - 1], zsend.at[0, k - 1], zrecv.at[0, k - 1], zdev[k]) for k in (1, 2, 3)]
    else:
        dw[...] = dwt
        pair[...] = pairs
    wait(len(loads) - 1)
    for i in range(CH):
        first[i].wait_recv()
        third[i].wait_recv()
        out[rows[i]] = (part[r, rows[i]].astype(f32) + crv[0, rows[i]].astype(f32)
                        + yrv[rows[i]].astype(f32) + grad1[rows[i]]).astype(bf)
    if with_w:
        for c in zq:
            c.wait_recv()
        whole_q = (zsq[0].astype(f32) + zrq[0].astype(f32)) + (zrq[1].astype(f32) + zrq[2].astype(f32))
        qo[...] = whole_q
        for c in zp:
            c.wait_recv()
        pair[...] = ((psd[0] + psd[1]) + psd[2]) + psd[3]
        for c in zm:
            c.wait_recv()
        mo[...] = (zsm[0].astype(f32) + zrm[0].astype(f32)) + (zrm[1].astype(f32) + zrm[2].astype(f32))
    sends.drain()


def final(whole, w, dqt, dkv, grad1, *more):
    with_w = len(more) > 0
    dma = pltpu.SemaphoreType.DMA
    sd = jax.ShapeDtypeStruct
    vm = pltpu.VMEM
    rows = (ROWS, D)
    like = lambda a: vm(a.shape, a.dtype)
    shapes = [sd(rows, bf), sd((8, QW), f32)]
    args = [whole, w, dqt, dkv, grad1, *more]
    scratch = [like(whole), like(w), vm((D, 2 * QW), bf), like(dqt), like(dkv), like(grad1), vm((4,) + rows, bf),
               vm((2,) + rows, bf), vm(rows, bf), vm(rows, bf)]
    sems = [dma((9,)), dma((2, CH)), dma((2, CH)), dma((CH,)), dma((CH,))]
    if with_w:
        n = w.shape[1]
        shapes += [sd((n, 3 * QW), f32), sd((n, PK), f32)]
        scratch += [like(m) for m in more] + [vm((4, n, PK), bf), vm((3, n, PK), bf),
                    vm((4, 2, n, 3 * QW), bf), vm((4, n, 3 * QW), bf), vm((4, n, 3 * QW), bf), vm((3, n, 3 * QW), bf),
                    vm((8, QW), f32), vm((4, 8, QW), f32), vm((8, QW), f32)]
        sems += [dma((2,)), dma((2,)), dma((3, 3)), dma((3, 3))]
    else:
        shapes += [sd((D, 3 * QW), bf)]
    return pl.pallas_call(
        functools.partial(final_kernel, with_w),
        out_shape=shapes,
        in_specs=[HB] * len(args), out_specs=[VM] * len(shapes),
        scratch_shapes=scratch + sems,
        compiler_params=pltpu.CompilerParams(
            collective_id=1, has_side_effects=True, vmem_limit_bytes=60 << 20),
        name="final",
    )(*args)


def emit_kernel(*refs):
    sources, outs, kept, sem = refs[:5], refs[5:16], refs[16:21], refs[21]
    loads = [pltpu.make_async_copy(a, b, sem.at[n]) for n, (a, b) in enumerate(zip(sources, kept))]
    for c in loads:
        c.start()
    input_grad, qkv_o, pair_o, out_o, out_b, inner_o, inner_b, outer_o, outer_b, gain_o, shift_o = outs
    save = pltpu.make_async_copy(kept[0], input_grad, sem.at[5])
    loads[0].wait()
    save.start()
    for c in loads[1:]:
        c.wait()
    pair, qkv, share, sums = kept[1:]
    for c in range(3):
        qkv_o[c] = qkv[:, c * QW:(c + 1) * QW]
    pair_o[...] = pair[0:2]
    inner_o[...] = share[:, 0:FQ]
    outer_o[...] = share[:, OU:]
    out_o[...] = share[:, AT:OU].T[:QW]
    out_b[...] = sums[5]
    inner_b[...] = sums[6 + lax.axis_index("tensor")]
    outer_b[...] = sums[2]
    gain_o[...] = jnp.concatenate([sums[3:4], sums[0:1]], 0)
    shift_o[...] = jnp.concatenate([sums[4:5], sums[1:2]], 0)
    save.wait()


def emit(*arrays):
    sd = jax.ShapeDtypeStruct
    n = arrays[3].shape[0]
    rows = sd((ROWS, D), bf)
    vec = sd((D,), f32)
    shapes = (rows, sd((3, n, QW), f32), sd((2, QW), f32), sd((QW, n), f32), vec, sd((n, FQ), f32), vec,
              sd((n, FQ), f32), vec, sd((2, D), f32), sd((2, D), f32))
    return pl.pallas_call(
        emit_kernel, out_shape=shapes, in_specs=[HB] * 5, out_specs=(HB,) + (VM,) * 10,
        scratch_shapes=[pltpu.VMEM(a.shape, a.dtype) for a in arrays] + [pltpu.SemaphoreType.DMA((6,))],
        compiler_params=pltpu.CompilerParams(vmem_limit_bytes=60 << 20),
        name="emit",
    )(*arrays)


def add_low(a, b):
    return (a.astype(f32) + b.astype(f32)).astype(bf)


def on_device(
    ring, input_rows, time_embed, parents, qkv_weight, qv_bias, out_weight, out_bias, inner_weight,
    inner_bias, outer_weight, outer_bias, norm_gain, norm_shift, cotangent,
):
    rank = lax.axis_index("tensor")
    dpos = lax.axis_index("dp")
    part = qkv_weight.shape[0]
    own_ring = ring == 8

    if own_ring:
        whole, w_all, gz, half = gather_start(
            input_rows, time_embed, jnp.transpose(qkv_weight, (1, 0, 2)), inner_weight, outer_weight.T, out_weight,
            inner_bias)
        diagonal = [(i * 4 + j, (i ^ 1) * 4 + (j ^ 2)) for i in range(8) for j in range(4)]
        cross = lambda a: lax.ppermute(a, ("dp", "tensor"), diagonal)
        weights = [gz, across_x(gz), partner(gz, 2), cross(half)]
    else:
        whole = gather_start(input_rows, time_embed)[0]
        w_all = lax.all_gather(qkv_weight.reshape(part, 3 * QW), "dp", axis=0, tiled=True).reshape(8, 96, 3 * QW)
        bias_part = lax.dynamic_slice_in_dim(inner_bias, dpos * part, part, 0)
        packed = jnp.concatenate([inner_weight, out_weight.T, bias_part[:, None],
                                  jnp.zeros((part, OU - AT - QW - 1), bf), outer_weight.T], axis=1)
        packed = lax.all_gather(packed, "dp", axis=0, tiled=True)
        weights = [lax.all_gather(packed, "tensor", axis=0, tiled=False).reshape(4, 4, 2, 96, PK)]

    qt, kv, kt, ot, mix, lse, pairs = attn_fwd(parents, whole, w_all, qv_bias)
    block_out, grad1, dots, *parts, sums = middle(
        weights, mix, input_rows, time_embed, cotangent, out_bias, outer_bias, norm_gain, norm_shift)
    if own_ring:
        parts = [parts[0], across_x(parts[1]), partner(parts[2], 2), cross(parts[3])]
    else:
        far = [partner(parts[2], 2), partner(parts[3], 2)]
    dqt, dkv, block_out = attn_bwd((0, 1, 2), pairs, qt, kv, kt, dots, ot, lse, block_out)
    if own_ring:
        input_grad, pair, qkv_share, share = final(whole, w_all, dqt, dkv, grad1, *parts)
        (input_grad, qkv_share, pair, out_share, out_sum, inner_share, inner_sum, outer_share, outer_sum,
         gains, shifts) = emit(input_grad, pair, qkv_share, share, sums)
        return (block_out, input_grad, jnp.transpose(qkv_share, (1, 0, 2)), pair, out_share, out_sum,
                inner_share, inner_sum, outer_share.T, outer_sum, gains, shifts)
    else:
        input_grad, pair, dwq = final(whole, w_all, dqt, dkv, grad1)
        own, other = add_low(parts[0], far[0]), add_low(parts[1], far[1])
        even = dpos % 2 == 0
        mine = jnp.stack([jnp.where(even, own, other), jnp.where(even, other, own)], axis=1).reshape(D, PK)
        share = lax.psum_scatter(mine, "dp", scatter_dimension=0, tiled=True).astype(f32)
        qkv_share = lax.psum_scatter(dwq, "dp", scatter_dimension=0, tiled=True).astype(f32).reshape(part, 3, QW)
        pair = lax.psum(pair, "dp")
        sums = jnp.sum(lax.all_gather(sums, ("dp", "tensor"), axis=0, tiled=False), axis=0)
    return (
        block_out,
        input_grad,
        qkv_share,
        pair[:2],
        share[:, AT:AT + QW].T,
        sums[5],
        share[:, :FQ],
        lax.dynamic_index_in_dim(sums[6:10], rank, 0, keepdims=False),
        share[:, OU:].T,
        sums[2],
        jnp.stack([sums[3], sums[0]]),
        jnp.stack([sums[4], sums[1]]),
    )


def solution(mesh):
    both = P(("dp", "tensor"), None)
    return jax.shard_map(
        functools.partial(on_device, mesh.shape["dp"]),
        mesh=mesh,
        in_specs=(
            both, P("dp", None), P("dp", None), P("dp", None, "tensor"), P(None, "tensor"),
            P("tensor", "dp"), P(), P("dp", "tensor"), P("tensor"), P("tensor", "dp"), P(), P(), P(), both,
        ),
        out_specs=(
            both, both, P("dp", None, "tensor"), P(None, "tensor"), P("tensor", "dp"), P(),
            P("dp", "tensor"), P("tensor"), P("tensor", "dp"), P(), P(), P(),
        ),
        check_vma=False,
    )
```

```python
import functools
import jax, jax.numpy as jnp
from jax import lax
from jax.experimental import pallas as pl
from jax.experimental.pallas import tpu as pltpu
from jax.sharding import PartitionSpec as P
bf = jnp.bfloat16
f32 = jnp.float32
BLK = 256
TRUNK = 1024
NB = 16
HD = 64
HN = 3
SEGS = 13
PAD = 4
LIST = 192
TQ = 512
TK = 1024
FP = 4
BP = 4
BTQ = 1024
BTK = 256
FQT = 1024
FKT = 512
VM = pl.BlockSpec(memory_space=pltpu.VMEM)
SM = pl.BlockSpec(memory_space=pltpu.SMEM)
HB = pl.BlockSpec(memory_space=pltpu.HBM)
NT = (((1,), (1,)), ((), ()))


def mm(a, b, dims=(((1,), (0,)), ((), ()))):
    return lax.dot_general(a, b, dims, preferred_element_type=f32)


def aligned(i, n):
    return pl.ds(pl.multiple_of(i * n, n), n)


def list_pairs(parents, cur, pairs):
    for s in range(1, SEGS):
        cur[s] = jnp.int32(s)

    def level(_, n):
        for s in range(1, SEGS):
            c = cur[s]
            pairs[0, n] = jnp.int32(s + 3)
            pairs[1, n] = c + 3
            cur[s] = jnp.where(c > 0, parents[0, c], 0)
            n = n + jnp.where(c > 0, 1, 0)
        for i in range(PAD - 1):
            pairs[0, n + i] = jnp.int32(NB)
            pairs[1, n + i] = jnp.int32(NB)
        return (n + PAD - 1) // PAD * PAD

    pairs[2, 0] = lax.fori_loop(0, SEGS - 1, level, jnp.int32(0))


PR = 1024


def fwd_kernel(parents, x_hbm, w_hbm, b_ref, qt_hbm, kv_hbm, kt_hbm, o_hbm, mix_hbm, lse_ref, pairs,
               cur, m_s, acc_s, xs, w_s, wt_s, wr_s, br_s, qt_ref, kv_ref, kt_ref, vt_ref, o_ref, mix_ref, sem):
    def fetch(i, slot):
        return pltpu.make_async_copy(x_hbm.at[i], xs.at[slot], sem.at[slot])

    load_w = pltpu.make_async_copy(w_hbm, w_s, sem.at[2])
    load_w.start()
    fetch(0, 0).start()
    list_pairs(parents, cur, pairs)
    load_w.wait()
    bias = b_ref[...].astype(f32)
    bias = jnp.concatenate([bias[0:1], bias[1:2]], 1)
    w = w_s[...].reshape(w_s.shape[0] * w_s.shape[1], w_s.shape[2])
    wt_s[...] = w[:, :HN * HD].T
    for h in range(HN):
        for c in (1, 2):
            to = slice(h * 128 + (c - 1) * HD, h * 128 + c * HD)
            wr_s[:, to] = w[:, c * HN * HD + h * HD:c * HN * HD + (h + 1) * HD]
            part = bias[:, HN * HD + h * HD:HN * HD + (h + 1) * HD] if c == 2 else jnp.zeros((1, HD), f32)
            br_s[:, to] = jnp.broadcast_to(part, (8, HD))
    bias_col = jnp.transpose(jnp.broadcast_to(bias[:, :HN * HD], (8, HN * HD)))
    ones = (lax.broadcasted_iota(jnp.int32, (16, PR), 0) == 0).astype(f32).astype(bf)

    def rows(i, _):
        slot = lax.rem(i, 2)

        @pl.when(i + 1 < NB * BLK // PR)
        def _():
            fetch(i + 1, 1 - slot).start()

        fetch(i, slot).wait()
        cols = aligned(i, PR)
        x = xs[slot]
        kv = (mm(x, wr_s[...]) + br_s[0:1]).astype(bf)
        kv_ref[cols] = kv
        q = (mm(wt_s[...], x, NT) + bias_col[:, 0:1]).astype(bf)
        qt_ref[:, cols] = (q.astype(f32) * 0.125).astype(bf)
        turned = kv.T
        for h in range(HN):
            kt_ref[h * HD:(h + 1) * HD, cols] = turned[h * 128:h * 128 + HD]
            vt_ref[h, :HD, cols] = turned[h * 128 + HD:(h + 1) * 128]
            vt_ref[h, HD:, cols] = ones
        return 0

    lax.fori_loop(0, NB * BLK // PR, rows, 0)
    saves = [pltpu.make_async_copy(a, b, sem.at[3 + n])
             for n, (a, b) in enumerate(((qt_ref, qt_hbm), (kv_ref, kv_hbm), (kt_ref, kt_hbm)))]
    for c in saves:
        c.start()
    zero = jnp.zeros((HD, TQ), bf)

    square = lambda ref, h, cols: jnp.sum(jnp.square(ref[h * HD:(h + 1) * HD, cols].astype(f32)), axis=0, keepdims=True)

    def norms(i, best):
        cols = aligned(i, BLK)
        for h in range(HN):
            m_s[i, h:h + 1] = square(qt_ref, h, cols)
        return tuple(jnp.maximum(best[h], square(kt_ref, h, cols)) for h in range(HN))

    best = lax.fori_loop(0, NB, norms, tuple(jnp.zeros((1, BLK), f32) for h in range(HN)))
    most = [jnp.max(x, axis=1, keepdims=True) for x in best]

    def bounds(i, _):
        for h in range(HN):
            m_s[i, h:h + 1] = jnp.sqrt(m_s[i, h:h + 1] * most[h]) * 1.001
        return 0

    lax.fori_loop(0, NB, bounds, 0)
    m_s[NB] = jnp.zeros((8, BLK), f32)
    wide_zero = jnp.zeros((HD, FQT), bf)

    def fast_tile(i, _):
        per = FQT // BLK
        qz = [jnp.concatenate([qt_ref[h * HD:(h + 1) * HD, aligned(i, FQT)], wide_zero], 0) for h in range(HN)]
        m = [jnp.concatenate([m_s[i * per + j, h:h + 1] for j in range(per)], 1) for h in range(HN)]
        acc = [None] * HN
        for c in range(TRUNK // FKT):
            ks = slice(c * FKT, (c + 1) * FKT)
            p = [jnp.exp(mm(kv_ref[ks, h * 128:(h + 1) * 128], qz[h]) - m[h]).astype(bf) for h in range(HN)]
            a = [mm(vt_ref[h, :, ks], p[h]) for h in range(HN)]
            acc = [x + y for x, y in zip(acc, a)] if c else a
        for h in range(HN):
            for j in range(per):
                acc_s[i * per + j, h] = acc[h][:, j * BLK:(j + 1) * BLK]
        return 0

    lax.fori_loop(0, NB * BLK // FQT, fast_tile, 0)

    def pick(g):
        work = []
        for p in range(FP):
            q, kb = pairs[0, g * FP + p], jnp.minimum(pairs[1, g * FP + p], NB - 1)
            work += [(q, aligned(jnp.minimum(q, NB - 1), BLK), aligned(kb, BLK), h) for h in range(HN)]
        return work

    def scores(work):
        return [mm(kv_ref[ks, h * 128:(h + 1) * 128],
                   jnp.concatenate([qt_ref[h * HD:(h + 1) * HD, qs], zero[:, :BLK]], 0)) for q, qs, ks, h in work]

    def fast_step(g, _):
        work = pick(g)
        p = [jnp.exp(x - m_s[q, h:h + 1]).astype(bf) for x, (q, qs, ks, h) in zip(scores(work), work)]
        a = [acc_s[q, h] + mm(vt_ref[h, :, ks], x) for x, (q, qs, ks, h) in zip(p, work)]
        for y, (q, qs, ks, h) in zip(a, work):
            acc_s[q, h] = y
        return 0

    lax.fori_loop(0, pairs[2, 0] // FP, fast_step, 0)

    def small(i, bad):
        for h in range(HN):
            bad = jnp.where(acc_s[i, h, HD:HD + 1, :] > 1e-18, bad, 1.0)
        return bad

    bad = jnp.max(lax.fori_loop(0, NB, small, jnp.zeros((1, BLK), f32)))

    @pl.when(bad > 0)
    def _():
        def tile(i, _):
            qz = [jnp.concatenate([qt_ref[h * HD:(h + 1) * HD, aligned(i, TQ)], zero], 0) for h in range(HN)]
            m, acc = [None] * HN, [None] * HN
            for c in range(TRUNK // TK):
                ks = slice(c * TK, (c + 1) * TK)
                s = [mm(kv_ref[ks, h * 128:(h + 1) * 128], qz[h]) for h in range(HN)]
                new = [jnp.max(x, axis=0, keepdims=True) for x in s]
                if c:
                    new = [jnp.maximum(x, y) for x, y in zip(m, new)]
                p = [jnp.exp(x - y).astype(bf) for x, y in zip(s, new)]
                a = [mm(vt_ref[h, :, ks], p[h]) for h in range(HN)]
                if c:
                    a = [x * jnp.exp(y - z) + w for x, y, z, w in zip(acc, m, new, a)]
                m, acc = new, a
            for h in range(HN):
                for j in range(TQ // BLK):
                    acc_s[i * (TQ // BLK) + j, h] = acc[h][:, j * BLK:(j + 1) * BLK]
                    m_s[i * (TQ // BLK) + j, h:h + 1] = m[h][:, j * BLK:(j + 1) * BLK]
            return 0

        lax.fori_loop(0, NB * BLK // TQ, tile, 0)

        def step(g, _):
            work = pick(g)
            s = scores(work)
            m = [m_s[q, h:h + 1] for q, qs, ks, h in work]
            new = [jnp.maximum(y, jnp.max(x, axis=0, keepdims=True)) for x, y in zip(s, m)]
            p = [jnp.exp(x - y).astype(bf) for x, y in zip(s, new)]
            a = [mm(vt_ref[h, :, ks], x) for x, (q, qs, ks, h) in zip(p, work)]
            a = [acc_s[q, h] * jnp.exp(x - y) + z for x, y, z, (q, qs, ks, h) in zip(m, new, a, work)]
            for x, y, (q, qs, ks, h) in zip(new, a, work):
                m_s[q, h:h + 1] = x
                acc_s[q, h] = y
            return 0

        lax.fori_loop(0, pairs[2, 0] // FP, step, 0)

    rank = lax.axis_index("tensor")

    def finish(i, _):
        qs = aligned(i, BLK)
        slot = jnp.bitwise_xor(rank, i // 4)
        for h in range(HN):
            total = acc_s[i, h, HD:HD + 1, :]
            out = acc_s[i, h, 0:HD, :] / total
            o_ref[h * HD:(h + 1) * HD, qs] = out
            mix_ref[slot, h * HD:(h + 1) * HD, aligned(lax.rem(i, 4), BLK)] = out.astype(bf)
            lse_ref[h:h + 1, qs] = m_s[i, h:h + 1] + jnp.log(total)
        return 0

    lax.fori_loop(0, NB, finish, 0)
    saves += [pltpu.make_async_copy(mix_ref, mix_hbm, sem.at[6]), pltpu.make_async_copy(o_ref, o_hbm, sem.at[7])]
    for c in saves[3:]:
        c.start()
    for c in saves:
        c.wait()


def attn_fwd(parents, whole, w, bias):
    S = NB * BLK
    sd = jax.ShapeDtypeStruct
    vm = pltpu.VMEM
    n = HN * HD
    d = whole.shape[2]
    return pl.pallas_call(
        fwd_kernel,
        out_shape=(sd((n, S), bf), sd((S, 2 * n), bf), sd((n, S), bf), sd((n, S), f32), sd((4, n, S // 4), bf),
                   sd((8, S), f32), sd((3, LIST), jnp.int32)),
        in_specs=[SM, HB, HB, VM], out_specs=(HB,) * 5 + (VM, SM),
        scratch_shapes=[pltpu.SMEM((16,), jnp.int32), vm((NB + 1, 8, BLK), f32), vm((NB + 1, HN, 80, BLK), f32),
                        vm((2, PR, d), bf), vm(w.shape, bf), vm((n, d), bf), vm((d, 2 * n), bf), vm((8, 2 * n), f32),
                        vm((n, S), bf), vm((S, 2 * n), bf), vm((n, S), bf), vm((HN, 80, S), bf),
                        vm((n, S), f32), vm((4, n, S // 4), bf), pltpu.SemaphoreType.DMA((8,))],
        compiler_params=pltpu.CompilerParams(vmem_limit_bytes=63 << 20),
        cost_estimate=pl.CostEstimate(flops=40_000_000_000, bytes_accessed=12_000_000, transcendentals=18_000_000),
        name="tree_attention",
    )(parents, whole, w, bias)


def bwd_kernel(heads, pairs, qt_hbm, kv_hbm, kt_hbm, dots_hbm, o_hbm, lse_ref, rows_in, dqt_hbm, dkv_hbm, rows_out,
               rows_s, dkv_s, dq_s, st_s, dot_ref, qt_ref, kv_ref, kt_ref, dots, o_ref, dqt_ref, dkv_ref, sem):
    loads = [pltpu.make_async_copy(a, b, sem.at[n]) for n, (a, b) in enumerate((
        (dots_hbm, dots), (o_hbm, o_ref), (qt_hbm, qt_ref), (kv_hbm, kv_ref), (kt_hbm, kt_ref)))]
    for c in loads:
        c.start()
    through = [pltpu.make_async_copy(rows_in, rows_s, sem.at[7]), pltpu.make_async_copy(rows_s, rows_out, sem.at[8])]
    through[0].start()
    dkv_s[...] = jnp.zeros_like(dkv_s)
    dq_s[...] = jnp.zeros_like(dq_s)
    rank = lax.axis_index("tensor")
    loads[0].wait()
    for m in range(4):
        dot_ref[:, aligned(jnp.bitwise_xor(rank, m), NB * BLK // 4)] = dots[m]
    loads[1].wait()

    def stats(i, _):
        qs = aligned(i, BLK)
        for n, h in enumerate(heads):
            rows = slice(h * HD, (h + 1) * HD)
            st_s[i, n:n + 1] = jnp.sum(dot_ref[rows, qs].astype(f32) * o_ref[rows, qs], axis=0, keepdims=True)
            st_s[i, 4 + n:5 + n] = lse_ref[h:h + 1, qs]
        return 0

    lax.fori_loop(0, NB, stats, 0)
    for c in loads[2:]:
        c.wait()
    through[0].wait()
    through[1].start()

    def chains(work, width):
        zero = jnp.zeros((HD, width), bf)
        rows = lambda h: slice(h * HD, (h + 1) * HD)
        qz = [jnp.concatenate([qt_ref[rows(h), qs], zero], 0) for h, qs, ks, lse, delta in work]
        dz = [jnp.concatenate([zero, dot_ref[rows(h), qs]], 0) for h, qs, ks, lse, delta in work]
        kv = [kv_ref[ks, h * 128:(h + 1) * 128] for h, qs, ks, lse, delta in work]
        p = [jnp.exp(mm(x, y) - w[3]) for x, y, w in zip(kv, qz, work)]
        ds = [(x * (mm(y, z) - w[4])).astype(bf) for x, y, z, w in zip(p, kv, dz, work)]
        g = [mm(jnp.concatenate([x, y.astype(bf)], 1), jnp.concatenate([z, u], 1), NT)
             for x, y, z, u in zip(ds, p, qz, dz)]
        return g, [mm(kt_ref[rows(h), ks], x) for x, (h, qs, ks, lse, delta) in zip(ds, work)]

    per = BTQ // BLK

    def tile(i, _):
        row = lambda k: jnp.concatenate([st_s[i * per + j, k:k + 1] for j in range(per)], 1)
        dq = [None] * len(heads)
        for c in range(TRUNK // BTK):
            ks = slice(c * BTK, (c + 1) * BTK)
            g, d = chains([(h, aligned(i, BTQ), ks, row(4 + n), row(n)) for n, h in enumerate(heads)], BTQ)
            for n in range(len(heads)):
                dkv_s[ks, n * 128:(n + 1) * 128] += g[n]
                dq[n] = d[n] if c == 0 else dq[n] + d[n]
        for n in range(len(heads)):
            for j in range(per):
                dq_s[i * per + j, n] += dq[n][:, j * BLK:(j + 1) * BLK]
        return 0

    lax.fori_loop(0, NB * BLK // BTQ, tile, 0)

    def step(s, _):
        work, where = [], []
        for p in range(BP):
            q, kb = pairs[0, s * BP + p], pairs[1, s * BP + p]
            qr = jnp.minimum(q, NB - 1)
            for n, h in enumerate(heads):
                work.append((h, aligned(qr, BLK), aligned(jnp.minimum(kb, NB - 1), BLK),
                             st_s[qr, 4 + n:5 + n], st_s[qr, n:n + 1]))
                where.append((q, kb, n))
        for g, d, (q, kb, n) in zip(*chains(work, BLK), where):
            dkv_s[aligned(kb, BLK), n * 128:(n + 1) * 128] += g
            dq_s[q, n] += d
        return 0

    lax.fori_loop(0, pairs[2, 0] // BP, step, 0)

    def finish(i, _):
        for n in range(len(heads)):
            dqt_ref[n * HD:(n + 1) * HD, aligned(i, BLK)] = (dq_s[i, n] * 0.125).astype(bf)
        dkv_ref[aligned(i, BLK)] = dkv_s[aligned(i, BLK)].astype(bf)
        save(i).start()
        return 0

    def save(i):
        return pltpu.make_async_copy(dkv_ref.at[aligned(i, BLK)], dkv_hbm.at[aligned(i, BLK)], sem.at[9 + i])

    lax.fori_loop(0, NB, finish, 0)
    last = pltpu.make_async_copy(dqt_ref, dqt_hbm, sem.at[5])
    last.start()
    for i in range(NB):
        save(i).wait()
    last.wait()
    through[1].wait()


def attn_bwd(heads, pairs, qt, kv, kt, dots, o, lse, rows):
    S = qt.shape[1]
    sd = jax.ShapeDtypeStruct
    n = len(heads)
    return pl.pallas_call(
        functools.partial(bwd_kernel, heads),
        out_shape=(sd((n * HD, S), bf), sd((S, n * 128), bf), sd(rows.shape, rows.dtype)),
        in_specs=[SM] + [HB] * 5 + [VM, HB], out_specs=(HB, HB, HB),
        scratch_shapes=[pltpu.VMEM(rows.shape, rows.dtype), pltpu.VMEM((S + BLK, n * 128), f32), pltpu.VMEM((NB + 1, n, HD, BLK), f32),
                        pltpu.VMEM((NB, 8, BLK), f32), pltpu.VMEM((HN * HD, S), bf)]
        + [pltpu.VMEM(a.shape, a.dtype) for a in (qt, kv, kt, dots, o)]
        + [pltpu.VMEM((n * HD, S), bf), pltpu.VMEM((S, n * 128), bf), pltpu.SemaphoreType.DMA((9 + NB,))],
        compiler_params=pltpu.CompilerParams(vmem_limit_bytes=63 << 20),
        cost_estimate=pl.CostEstimate(flops=20_000_000_000 * n, bytes_accessed=8_000_000 * n, transcendentals=6_000_000 * n),
        name="tree_attention_grad",
    )(pairs, qt, kv, kt, dots, o, lse, rows)


D = 768
SEQ = 4096
ROWS = SEQ // 4
QW = HN * HD
FQ = 768
AT = FQ
OU = FQ + 256
PK = OU + FQ
MESH = pl.DeviceIdType.MESH
HBM = pl.BlockSpec(memory_space=pl.ANY)
TN = (((0,), (0,)), ((), ()))
epsilon = 1e-05
root_half = 0.7071067811865476
inv_root_tau = 0.3989422804014327


def layer_norm(summed, gain_row, shift_row):
    centre = jnp.mean(summed, axis=-1, keepdims=True)
    offset = summed - centre
    inv_std = lax.rsqrt(jnp.mean(offset * offset, axis=-1, keepdims=True) + epsilon)
    normed = offset * inv_std
    return normed * gain_row + shift_row, normed, inv_std


def norm_back(grad_out, normed, inv_std, gain_row):
    scaled = grad_out * gain_row
    return inv_std * (
        scaled
        - jnp.mean(scaled, axis=-1, keepdims=True)
        - normed * jnp.mean(scaled * normed, axis=-1, keepdims=True)
    )


def gelu_parts(u):
    half = 0.5 * (1.0 + lax.erf(u * root_half))
    return u * half, half + u * inv_root_tau * jnp.exp(-0.5 * u * u)


def partner(x, mask):
    return lax.ppermute(x, "tensor", [(i, i ^ mask) for i in range(4)])


def across_x(x):
    return lax.ppermute(x, "dp", [(i, i ^ 1) for i in range(8)])


def flip1(r):
    return r + 1 - 2 * lax.rem(r, 2)


CH = 4
CROWS = ROWS // CH


def remote(src, dst, s, q, dev):
    return pltpu.make_async_remote_copy(
        src_ref=src, dst_ref=dst, send_sem=s, recv_sem=q, device_id=dev, device_id_type=MESH)


def meet(targets, meanwhile=None):
    barrier = pltpu.get_barrier_semaphore()
    for t in targets:
        pl.semaphore_signal(barrier, inc=1, device_id=t, device_id_type=MESH)
    if meanwhile is not None:
        meanwhile()
    pl.semaphore_wait(barrier, len(targets))


class Sends:
    def __init__(self):
        self.started = []

    def go(self, *args):
        c = remote(*args)
        c.start()
        self.started.append(c)
        return c

    def drain(self):
        for c in self.started:
            c.wait_send()


def gather_kernel(with_w, *refs):
    if with_w:
        (inp, te, wq, w1, w2, w3, bias, whole_hbm, wqg_hbm, gz_hbm, gl_hbm, whole, wqg, gz, bcol,
         ysend, yrecv, csend, crecv, out, zsend, zrecv, xsend, xrecv) = refs
    else:
        inp, te, whole_hbm, whole, ysend, yrecv, csend, crecv, out = refs
    r = lax.axis_index("tensor")
    d = lax.axis_index("dp")
    rc, ry = flip1(r), lax.rem(r + 2, 4)
    core, yy = {"tensor": rc}, {"tensor": ry}
    targets = [core, yy]
    if with_w:
        z, x = d // 2, lax.rem(d, 2)
        xx = {"dp": flip1(d)}
        up, down = {"dp": lax.rem(z + 1, 4) * 2 + x}, {"dp": lax.rem(z + 3, 4) * 2 + x}
        targets += [xx, up, down]

    def prepare():
        shift = te[...].astype(f32)
        whole[r] = (inp[...].astype(f32) + shift).astype(bf)
        if with_w:
            for c in range(3):
                wqg[d, :, c * QW:(c + 1) * QW] = wq[c]

    meet(targets, prepare)
    sends = Sends()
    if with_w:

        def line(a, s, slot, way):
            ref = wqg.at[slot * 2 + x] if a == 0 else gz.at[slot]
            k = 2 * (s - 1) + way
            return remote(ref, ref, zsend.at[a, k], zrecv.at[a, k], (up, down)[way])

        def side(i, slot):
            ref = wqg.at[slot * 2 + x]
            return remote(ref, ref, xsend.at[i], xrecv.at[i], xx)

        def can_send(s, way):
            return jnp.logical_and(z < 3, z - s + 1 >= 0) if way == 0 else jnp.logical_and(z > 0, z + s - 1 <= 3)

        def can_recv(s, way):
            return z - s >= 0 if way == 0 else z + s <= 3

        def own(a):
            for way in (0, 1):
                @pl.when(can_send(1, way))
                def _():
                    line(a, 1, z, way).start()

        own(0)
        side(0, z).start()
    rows = [pl.ds(i * CROWS, CROWS) for i in range(CH)]
    yc = []
    for i in range(CH):
        mine = whole.at[r, rows[i]]
        yc.append(sends.go(mine, mine, ysend.at[i], yrecv.at[i], yy))
    c0 = sends.go(whole.at[r], whole.at[r], csend.at[CH], crecv.at[CH], core)
    if with_w:
        part = wqg.shape[1]
        gz[z, :, 0:FQ] = w1[...]
        gz[z, :, OU:] = w2[...]
        bcol[...] = jnp.transpose(jnp.broadcast_to(bias[...].astype(f32).reshape(1, D), (8, D)))
        fill = OU - AT - QW
        column = bcol[pl.ds(pl.multiple_of(d * part, 32), part), 0:1]
        column = jnp.where(lax.broadcasted_iota(jnp.int32, (part, fill), 1) == 0, column, 0.0)
        gz[z, :, AT:OU] = jnp.concatenate([w3[...].astype(f32).T, column], 1).astype(bf)
        own(1)
        for s in (1, 2, 3):
            for way in (0, 1):
                slot = z - s if way == 0 else z + s

                @pl.when(can_recv(s, way))
                def _():
                    for a in (0, 1):
                        line(a, s, slot, way).wait_recv()
                        if s < 3:
                            @pl.when(can_send(s + 1, way))
                            def _():
                                line(a, s + 1, slot, way).start()
                        if a == 0:
                            side(slot_sem(s, way), slot).start()
    keeps = []

    def keep(src, dst):
        c = pltpu.make_async_copy(src, dst, out.at[len(keeps)])
        c.start()
        keeps.append(c)

    keep(whole.at[r], whole_hbm.at[r])
    cc = []
    for i in range(CH):
        yc[i].wait_recv()
        part = whole.at[ry, rows[i]]
        cc.append(sends.go(part, part, csend.at[i], crecv.at[i], core))
    keep(whole.at[ry], whole_hbm.at[ry])
    c0.wait_recv()
    keep(whole.at[rc], whole_hbm.at[rc])
    for c in cc:
        c.wait_recv()
    rd = 3 - r
    keep(whole.at[rd], whole_hbm.at[rd])
    if with_w:
        keep(gz, gz_hbm)
        keep(gz.at[pl.ds(0, 2), :, pl.ds(0, OU)], gl_hbm)
        side(0, z).wait()
        for s in (1, 2, 3):
            for way in (0, 1):
                slot = z - s if way == 0 else z + s

                @pl.when(can_recv(s, way))
                def _():
                    side(slot_sem(s, way), slot).wait()

                @pl.when(can_send(s, way))
                def _():
                    for a in (0, 1):
                        line(a, s, slot_of_send(z, s, way), way).wait_send()
        keep(wqg, wqg_hbm)
    for c in keeps:
        c.wait()
    sends.drain()


def slot_of_send(z, s, way):
    return z - s + 1 if way == 0 else z + s - 1


def slot_sem(s, way):
    return 2 * s - 1 + way


def gather_start(inp, te, *weights):
    with_w = len(weights) > 0
    dma = pltpu.SemaphoreType.DMA
    shapes = [jax.ShapeDtypeStruct((4, ROWS, D), bf)]
    args = [inp, te, *weights]
    scratch = []
    sems = [dma((CH,)), dma((CH,)), dma((CH + 1,)), dma((CH + 1,)), dma((8,))]
    if with_w:
        part = weights[0].shape[1]
        line = jax.ShapeDtypeStruct((4, part, PK), bf)
        shapes += [jax.ShapeDtypeStruct((8, part, 3 * QW), bf), line, jax.ShapeDtypeStruct((2, part, OU), bf)]
        scratch = [pltpu.VMEM((D, 8), f32)]
        sems += [dma((2, 6)), dma((2, 6)), dma((7,)), dma((7,))]
    return pl.pallas_call(
        functools.partial(gather_kernel, with_w),
        out_shape=shapes, in_specs=[VM] * len(args), out_specs=[HB] * len(shapes),
        scratch_shapes=[pltpu.VMEM(a.shape, bf) for a in shapes[:3]] + scratch + sems,
        compiler_params=pltpu.CompilerParams(collective_id=0, has_side_effects=True, vmem_limit_bytes=60 << 20),
        name="gather_start",
    )(*args)


RB = 512
NR = ROWS // RB


def middle_kernel(with_w, *refs):
    if with_w:
        wa, wb, wc, wd = refs[:4]
        step, line_s, xsend, xrecv, wsend, wrecv, ssend, srecv = refs[-8:]
        refs = refs[4:-8]
    else:
        wfull, refs = refs[0], refs[1:]
    (mix_hbm, inp_hbm, te, cot_hbm, ob, fb, ng, ns, block_hbm, grad1_hbm, dots_hbm, p00, p01, p10, p11, sums_o,
     inp, cot, block_out, grad1_o, w, wt_s, mix, mixr, gmix, dots, both, ht, gmt, gat, act, gp, slope_s,
     loc, asend, arecv, bsend, brecv, gsend, grecv) = refs
    r = lax.axis_index("tensor")
    d = lax.axis_index("dp")
    x = lax.rem(d, 2)
    ranks = [r, flip1(r), lax.rem(r + 2, 4), 3 - r]
    devices = [{"tensor": k} for k in ranks]
    xx = {"dp": flip1(d)}
    load = pltpu.make_async_copy(mix_hbm, mix, loc.at[5])
    load.start()
    rows_in = [pltpu.make_async_copy(inp_hbm, inp, loc.at[19]), pltpu.make_async_copy(cot_hbm, cot, loc.at[20])]
    for c in rows_in:
        c.start()
    if with_w:
        z = d // 2
        zdev = [{"dp": lax.rem(z + k, 4) * 2 + x} for k in range(4)]
        meet(devices[1:] + [xx] + zdev[1:])
    else:
        meet(devices[1:])
    sends = Sends()
    core = devices[1]
    load.wait()

    def heads_in(b, m):
        cols = pl.ds(b * RB, RB)
        k = lax.axis_index("tensor")
        peer = {"tensor": (k, flip1(k), lax.rem(k + 2, 4), 3 - k)[m]}
        return remote(mix.at[m, :, cols], mixr.at[m, :, cols], asend.at[b, m], arecv.at[b, m], peer)

    def heads_out(b, m):
        cols = aligned(b, RB)
        return remote(gmix.at[m, :, cols], dots.at[m, :, cols], bsend.at[b, m], brecv.at[b, m], devices[m])

    heads = [[heads_in(b, m) for m in (3, 2, 1)] for b in range(NR)]
    for c in heads[0]:
        c.start()
    fill = pltpu.make_async_copy(mix.at[0], mixr.at[0], loc.at[0])
    fill.start()

    def weight_moves(j, relay, hand, place):
        rank, side = lax.axis_index("tensor"), lax.rem(lax.axis_index("dp"), 2)
        span = (pl.ds(0, OU), pl.ds(OU, FQ))[j]
        other = lax.rem(rank + 2, 4)
        four, two, end = pl.ds(0, 4), pl.ds(0, 2), pl.ds(2, 2)
        near = {"tensor": flip1(rank)}
        if relay is not None:
            relay(remote(wc.at[end, :, span], w.at[other, end, side, :, span], xsend.at[j], xrecv.at[j],
                         {"dp": flip1(lax.axis_index("dp"))}))
            if j:
                relay(remote(wb.at[two, :, span], w.at[rank, two, 1 - side, :, span], xsend.at[2], xrecv.at[2],
                             {"tensor": other}))
        pieces = ((wa, rank, four, side), (wb, rank, four, 1 - side), (wc, other, four, side), (wd, other, two, 1 - side))
        for i, (ref, t, zz, at) in enumerate(pieces[:4 - j]):
            src, dst = ref.at[:, :, span], w.at[t, zz, at, :, span]
            if hand is not None:
                hand(remote(src, dst, wsend.at[j, i], wrecv.at[j, i], near))
            if place is not None:
                place(pltpu.make_async_copy(src, dst, loc.at[11 + 4 * j + i]))

    def whole_fill(j):
        span = (pl.ds(0, OU), pl.ds(OU, FQ))[j]
        return pltpu.make_async_copy(wfull.at[:, :, :, :, span], w.at[:, :, :, :, span], loc.at[1 + j])

    def weight_tail(j):
        rank, side = lax.axis_index("tensor"), lax.rem(lax.axis_index("dp"), 2)
        tail = w.at[lax.rem(rank + 2, 4), (pl.ds(2, 2), pl.ds(0, 4))[j], 1 - side, :, (pl.ds(0, OU), pl.ds(OU, FQ))[j]]
        return remote(tail, tail, wsend.at[j, 4], wrecv.at[j, 4], {"tensor": flip1(rank)})

    if with_w:
        weight_moves(0, lambda c: c.start(), lambda c: c.start(), lambda c: c.start())
    else:
        for j in (0, 1):
            whole_fill(j).start()
    sums_o[...] = jnp.zeros_like(sums_o)
    out_bias, outer_bias = (v[...].astype(f32).reshape(1, D) for v in (ob, fb))
    gains, shifts = ng[...].astype(f32), ns[...].astype(f32)
    gain1, gain2, shift1, shift2 = gains[0:1], gains[1:2], shifts[0:1], shifts[1:2]
    def weights_here(j):
        if with_w:
            weight_moves(j, lambda c: c.wait_recv(), None, None)
            weight_tail(j).start()
            weight_moves(j, None, lambda c: c.wait_recv(), lambda c: c.wait())
            weight_tail(j).wait_recv()
        else:
            whole_fill(j).wait()

    weights_here(0)
    for c in heads[0]:
        c.wait_recv()
    if with_w:
        weight_moves(1, lambda c: c.start(), lambda c: c.start(), lambda c: c.start())
    fill.wait()
    for c in rows_in:
        c.wait()
    for t in range(4):
        wt_s[t] = jnp.transpose(w[t, :, :, :, AT:OU].reshape(D, OU - AT))
    bias_in = [wt_s[t, QW:QW + 16].astype(f32)[0:1] for t in range(4)]
    w_in = lambda t: w[t, :, :, :, 0:FQ].reshape(D, FQ)
    w_ou = lambda t: w[t, :, :, :, OU:].reshape(D, FQ)

    def add_sum(i, rows):
        sums_o[i:i + 1] += jnp.sum(rows, axis=0, keepdims=True)

    def block(b, _):
        for i in range(1, NR):
            @pl.when(b == i)
            def _():
                for c in heads[i]:
                    c.wait_recv()
        rows = aligned(b, RB)
        start = inp[rows].astype(f32) + te[...].astype(f32)
        attn = out_bias
        for m in range(4):
            attn = attn + mm(mixr[m, :, rows], wt_s[ranks[m], :QW], TN)
        hidden, normed1, inv1 = layer_norm(start + attn, gain1, shift1)
        low = hidden.astype(bf)
        ht[:, rows] = low.T
        for t in range(4):
            u = mm(low, w_in(t)) + bias_in[t]
            value, slope = gelu_parts(u)
            act[t, rows] = value.astype(bf)
            slope_s[t] = slope.astype(bf)

        @pl.when(b == 0)
        def _():
            weights_here(1)
            for i in range(1, NR):
                for m in (3, 2, 1):
                    heads_in(i, m).start()

        mlp = outer_bias
        for t in range(4):
            mlp = mlp + mm(act[t, rows], w_ou(t), NT)
        final, normed2, inv2 = layer_norm(hidden + mlp, gain2, shift2)
        block_out[rows] = final.astype(bf)
        e = cot[rows].astype(f32)
        add_sum(0, e * normed2)
        add_sum(1, e)
        grad2 = norm_back(e, normed2, inv2, gain2)
        gm = grad2.astype(bf)
        gmt[:, rows] = gm.T
        add_sum(2, gm.astype(f32))
        gin = grad2
        for t in range(4):
            g = (mm(gm, w_ou(t)) * slope_s[t].astype(f32)).astype(bf)
            gp[t, rows] = g
            add_sum(6 + t, g.astype(f32))
            gin = gin + mm(g, w_in(t), NT)
        add_sum(3, gin * normed1)
        add_sum(4, gin)
        grad1 = norm_back(gin, normed1, inv1, gain1)
        grad1_o[rows] = grad1
        ga = grad1.astype(bf)
        gat_rows = ga.T
        gat[:, rows] = gat_rows
        add_sum(5, ga.astype(f32))
        for m in (3, 2, 1):
            gmix[m, :, rows] = mm(wt_s[ranks[m], :QW], gat_rows).astype(bf)
            heads_out(b, m).start()
        dots[0, :, rows] = mm(wt_s[r, :QW], gat_rows).astype(bf)
        return 0

    lax.fori_loop(0, NR, block, 0)

    if with_w:
        for j in (0, 1):
            weight_moves(j, lambda c: c.wait_send(), lambda c: c.wait_send(), None)
            weight_tail(j).wait_send()

    def grads(t, m):
        return (lambda: mm(ht[...], gp[t]), lambda: mm(gmt[...], act[t]), lambda: mm(gat[...], mixr[m], NT))

    cols = (slice(0, FQ), slice(OU, PK), slice(AT, AT + QW))
    blank = jnp.zeros((4, 2, 96, OU - AT - QW), bf)
    cut = lambda g: g.reshape(4, 2, 96, g.shape[1])

    def handing(q):
        return remote(w.at[q], both.at[q], gsend.at[q], grecv.at[q], core)

    hops = []

    def hop(n):
        if not with_w:
            return
        if n:
            hops[-1].wait_recv()
        step[n] = step[n - 1] + step[n + 3] if n else sums_o[...]
        hops.append(sends.go(step.at[n], step.at[n + 4], ssend.at[n], srecv.at[n], (core, devices[2], xx)[n]))

    hop(0)
    saves = [pltpu.make_async_copy(grad1_o, grad1_hbm, loc.at[21]), pltpu.make_async_copy(block_out, block_hbm, loc.at[22])]
    for c in saves:
        c.start()
    for q in (1, 0):
        for c, g in zip(cols, grads(ranks[2 * q + 1], 2 * q + 1)):
            w[q, :, :, :, c] = cut(g().astype(bf))
        w[q, :, :, :, AT + QW:OU] = blank
        handing(q).start()
        hop(2 - q)
    for q in (1, 0):
        mine = grads(ranks[2 * q], 2 * q)
        handing(q).wait_recv()
        for c, g in zip(cols, mine):
            both[q, :, :, :, c] = (both[q, :, :, :, c].astype(f32) + cut(g())).astype(bf)
        for n, side in ((0, x), (1, 1 - x)):
            to = ((p00, p01), (p10, p11))[q][n]
            saves.append(pltpu.make_async_copy(both.at[q, :, side], to, loc.at[6 + 2 * q + n]))
            saves[-1].start()
        if with_w and q:
            hops[-1].wait_recv()
            line_s[z] = step[2] + step[6]
            ends = [sends.go(line_s.at[z], line_s.at[z], ssend.at[2 + k], srecv.at[2 + k], zdev[k]) for k in (1, 2, 3)]
    if with_w:
        for c in ends:
            c.wait_recv()
        sums_o[...] = ((line_s[0] + line_s[1]) + line_s[2]) + line_s[3]
    for b in range(NR):
        for m in (1, 2, 3):
            heads_out(b, m).wait()
        for c in heads[b]:
            c.wait_send()
    saves.append(pltpu.make_async_copy(dots, dots_hbm, loc.at[10]))
    saves[-1].start()
    for c in saves:
        c.wait()
    for q in range(2):
        handing(q).wait_send()
    sends.drain()


def middle(weights, mix, *rest):
    sd = jax.ShapeDtypeStruct
    dma = pltpu.SemaphoreType.DMA
    with_w = len(weights) > 1
    vm = pltpu.VMEM
    tokens = (D, ROWS)
    extra = [vm((7, 16, D), f32), vm((4, 16, D), f32), dma((3,)), dma((3,)), dma((2, 5)), dma((2, 5)),
             dma((6,)), dma((6,))] if with_w else []
    return pl.pallas_call(
        functools.partial(middle_kernel, with_w),
        out_shape=(sd((ROWS, D), bf), sd((ROWS, D), f32), sd((4, QW, ROWS), bf),
                   *([sd((4, 96, PK), bf)] * 4), sd((16, D), f32)),
        in_specs=[HB] * len(weights) + [HB, HB, VM, HB] + [VM] * 4, out_specs=(HB, HB, HB, HB, HB, HB, HB, VM),
        scratch_shapes=[vm((ROWS, D), bf), vm((ROWS, D), bf), vm((ROWS, D), bf), vm((ROWS, D), f32),
                        vm((4, 4, 2, 96, PK), bf), vm((4, OU - AT, D), bf), vm((4, QW, ROWS), bf),
                        vm((4, QW, ROWS), bf), vm((4, QW, ROWS), bf), vm((4, QW, ROWS), bf),
                        vm((2, 4, 2, 96, PK), bf), vm(tokens, bf), vm(tokens, bf), vm(tokens, bf),
                        vm((4, ROWS, FQ), bf), vm((4, ROWS, FQ), bf), vm((4, RB, FQ), bf),
                        dma((23,)), dma((NR, 4)), dma((NR, 4)), dma((NR, 4)), dma((NR, 4)), dma((2,)), dma((2,))] + extra,
        compiler_params=pltpu.CompilerParams(collective_id=2, has_side_effects=True, vmem_limit_bytes=63 << 20),
        cost_estimate=pl.CostEstimate(flops=33_000_000_000, bytes_accessed=50_000_000, transcendentals=9_000_000),
        name="middle",
    )(*weights, mix, *rest)


def final_kernel(with_w, *refs):
    if with_w:
        (x_hbm, w_hbm, dqt_hbm, dkv_hbm, g1_hbm, m0_hbm, m1_hbm, m2_hbm, m3_hbm, out, pair, qo, mo,
         x_s, w_s, wr_s, dqt, dkv, grad1, part, crv, ysd, yrv, m0, m1, m2, m3, zsm, zrm, dwq, xrq, zsq, zrq,
         prv, psd, prs, loc, csend, crecv, ysend, yrecv, xsend, xrecv, zsend, zrecv) = refs
    else:
        (x_hbm, w_hbm, dqt_hbm, dkv_hbm, g1_hbm, out, pair, dw,
         x_s, w_s, wr_s, dqt, dkv, grad1, part, crv, ysd, yrv, loc, csend, crecv, ysend, yrecv) = refs
    pulls = [(w_hbm, w_s), (dqt_hbm, dqt), (dkv_hbm, dkv)]
    pulls += [(m0_hbm, m0), (m1_hbm, m1), (m2_hbm, m2), (m3_hbm, m3)] if with_w else []
    pulls += [(x_hbm, x_s), (g1_hbm, grad1)]
    loads = [pltpu.make_async_copy(a, b, loc.at[n]) for n, (a, b) in enumerate(pulls)]
    for c in loads[:-2]:
        c.start()
    r = lax.axis_index("tensor")
    d = lax.axis_index("dp")
    rc, ry = flip1(r), lax.rem(r + 2, 4)
    rd = 3 - r
    core, yy = {"tensor": rc}, {"tensor": ry}
    targets = [core, yy]
    if with_w:
        z, x = d // 2, lax.rem(d, 2)
        xo = 1 - x
        zs = [lax.rem(z + k, 4) for k in range(4)]
        xx = {"dp": flip1(d)}
        zdev = [{"dp": zs[k] * 2 + x} for k in range(4)]
        targets += [xx] + zdev[1:]
    meet(targets)
    sends = Sends()
    go = sends.go
    wait = lambda *which: [loads[n].wait() for n in which]
    rows = [pl.ds(i * CROWS, CROWS) for i in range(CH)]
    if with_w:
        wait(3, 4, 5, 6)
        zm = []
        for k in (1, 2, 3, 0):
            at = zs[k]
            zsm[k] = ((m0[at].astype(f32) + m1[at].astype(f32)) + (m2[at].astype(f32) + m3[at].astype(f32))).astype(bf)
            if k:
                zm.append(go(zsm.at[k], zrm.at[k - 1], zsend.at[1, k - 1], zrecv.at[1, k - 1], zdev[k]))
    wait(0, 1, 2)
    for c in loads[-2:]:
        c.start()
    w = w_s[...].reshape(D, 3 * QW)
    for h in range(HN):
        for c in (1, 2):
            wr_s[:, h * 128 + (c - 1) * HD:h * 128 + c * HD] = w[:, c * QW + h * HD:c * QW + (h + 1) * HD]
    wqs = w[:, :QW]

    def project_back(t, i):
        at = pl.ds(pl.multiple_of(t * ROWS + i * CROWS, CROWS), CROWS)
        part[t, rows[i]] = (mm(dqt[:, at], wqs, (((0,), (1,)), ((), ()))) + mm(dkv[at], wr_s[...], NT)).astype(bf)

    first, second, third = [], [], []
    for i in range(CH):
        project_back(rd, i)
        second.append(go(part.at[rd, rows[i]], crv.at[1, rows[i]], csend.at[1, i], crecv.at[1, i], core))
        project_back(ry, i)
        if i:
            second[i - 1].wait_recv()
            prev = rows[i - 1]
            ysd[prev] = (part[ry, prev].astype(f32) + crv[1, prev].astype(f32)).astype(bf)
            third.append(go(ysd.at[prev], yrv.at[prev], ysend.at[i - 1], yrecv.at[i - 1], yy))
    prev = rows[CH - 1]
    second[CH - 1].wait_recv()
    ysd[prev] = (part[ry, prev].astype(f32) + crv[1, prev].astype(f32)).astype(bf)
    third.append(go(ysd.at[prev], yrv.at[prev], ysend.at[CH - 1], yrecv.at[CH - 1], yy))

    wait(len(loads) - 2)
    whole = x_s[...].reshape(SEQ, D)
    aq = mm(dqt[...], whole)
    akv = mm(dkv[...], whole, TN)
    blocks = [aq]
    for c in (0, 1):
        blocks += [akv[h * 128 + c * HD:h * 128 + (c + 1) * HD] for h in range(HN)]
    dwt = jnp.concatenate(blocks, 0).T.astype(bf)
    sum_q = jnp.sum(dqt[...].astype(f32), axis=1, keepdims=True)
    sum_q = jnp.transpose(jnp.broadcast_to(sum_q, (QW, 8)))
    sum_kv = jnp.sum(dkv[...].astype(f32), axis=0, keepdims=True)
    sum_v = jnp.concatenate([sum_kv[:, h * 128 + HD:(h + 1) * 128] for h in range(HN)], 1)
    pairs = jnp.concatenate([sum_q[0:1], sum_v, jnp.zeros((6, QW), f32)], 0)
    if with_w:
        dwq[...] = dwt.reshape(dwq.shape)
        xq = go(dwq.at[:, xo], xrq, xsend.at[0], xrecv.at[0], xx)
        prs[...] = pairs
        px = go(prs, prv, xsend.at[1], xrecv.at[1], xx)
    for i in range(CH):
        project_back(rc, i)
        first.append(go(part.at[rc, rows[i]], crv.at[0, rows[i]], csend.at[0, i], crecv.at[0, i], core))
        project_back(r, i)
    if with_w:
        px.wait_recv()
        psd[z] = prs[...] + prv[...]
        zp = [go(psd.at[z], psd.at[z], zsend.at[2, k - 1], zrecv.at[2, k - 1], zdev[k]) for k in (1, 2, 3)]
        xq.wait_recv()
        for k in range(4):
            zsq[k] = (dwq[zs[k], x].astype(f32) + xrq[zs[k]].astype(f32)).astype(bf)
        zq = [go(zsq.at[k], zrq.at[k - 1], zsend.at[0, k - 1], zrecv.at[0, k - 1], zdev[k]) for k in (1, 2, 3)]
    else:
        dw[...] = dwt
        pair[...] = pairs
    wait(len(loads) - 1)
    for i in range(CH):
        first[i].wait_recv()
        third[i].wait_recv()
        out[rows[i]] = (part[r, rows[i]].astype(f32) + crv[0, rows[i]].astype(f32)
                        + yrv[rows[i]].astype(f32) + grad1[rows[i]]).astype(bf)
    if with_w:
        for c in zq:
            c.wait_recv()
        whole_q = (zsq[0].astype(f32) + zrq[0].astype(f32)) + (zrq[1].astype(f32) + zrq[2].astype(f32))
        qo[...] = whole_q
        for c in zp:
            c.wait_recv()
        pair[...] = ((psd[0] + psd[1]) + psd[2]) + psd[3]
        for c in zm:
            c.wait_recv()
        mo[...] = (zsm[0].astype(f32) + zrm[0].astype(f32)) + (zrm[1].astype(f32) + zrm[2].astype(f32))
    sends.drain()


def final(whole, w, dqt, dkv, grad1, *more):
    with_w = len(more) > 0
    dma = pltpu.SemaphoreType.DMA
    sd = jax.ShapeDtypeStruct
    vm = pltpu.VMEM
    rows = (ROWS, D)
    like = lambda a: vm(a.shape, a.dtype)
    shapes = [sd(rows, bf), sd((8, QW), f32)]
    args = [whole, w, dqt, dkv, grad1, *more]
    scratch = [like(whole), like(w), vm((D, 2 * QW), bf), like(dqt), like(dkv), like(grad1), vm((4,) + rows, bf),
               vm((2,) + rows, bf), vm(rows, bf), vm(rows, bf)]
    sems = [dma((9,)), dma((2, CH)), dma((2, CH)), dma((CH,)), dma((CH,))]
    if with_w:
        n = w.shape[1]
        shapes += [sd((n, 3 * QW), f32), sd((n, PK), f32)]
        scratch += [like(m) for m in more] + [vm((4, n, PK), bf), vm((3, n, PK), bf),
                    vm((4, 2, n, 3 * QW), bf), vm((4, n, 3 * QW), bf), vm((4, n, 3 * QW), bf), vm((3, n, 3 * QW), bf),
                    vm((8, QW), f32), vm((4, 8, QW), f32), vm((8, QW), f32)]
        sems += [dma((2,)), dma((2,)), dma((3, 3)), dma((3, 3))]
    else:
        shapes += [sd((D, 3 * QW), bf)]
    return pl.pallas_call(
        functools.partial(final_kernel, with_w),
        out_shape=shapes,
        in_specs=[HB] * len(args), out_specs=[VM] * len(shapes),
        scratch_shapes=scratch + sems,
        compiler_params=pltpu.CompilerParams(
            collective_id=1, has_side_effects=True, vmem_limit_bytes=60 << 20),
        name="final",
    )(*args)


def emit_kernel(*refs):
    sources, outs, kept, sem = refs[:5], refs[5:16], refs[16:21], refs[21]
    loads = [pltpu.make_async_copy(a, b, sem.at[n]) for n, (a, b) in enumerate(zip(sources, kept))]
    for c in loads:
        c.start()
    input_grad, qkv_o, pair_o, out_o, out_b, inner_o, inner_b, outer_o, outer_b, gain_o, shift_o = outs
    save = pltpu.make_async_copy(kept[0], input_grad, sem.at[5])
    loads[0].wait()
    save.start()
    for c in loads[1:]:
        c.wait()
    pair, qkv, share, sums = kept[1:]
    for c in range(3):
        qkv_o[c] = qkv[:, c * QW:(c + 1) * QW]
    pair_o[...] = pair[0:2]
    inner_o[...] = share[:, 0:FQ]
    outer_o[...] = share[:, OU:]
    out_o[...] = share[:, AT:OU].T[:QW]
    out_b[...] = sums[5]
    inner_b[...] = sums[6 + lax.axis_index("tensor")]
    outer_b[...] = sums[2]
    gain_o[...] = jnp.concatenate([sums[3:4], sums[0:1]], 0)
    shift_o[...] = jnp.concatenate([sums[4:5], sums[1:2]], 0)
    save.wait()


def emit(*arrays):
    sd = jax.ShapeDtypeStruct
    n = arrays[3].shape[0]
    rows = sd((ROWS, D), bf)
    vec = sd((D,), f32)
    shapes = (rows, sd((3, n, QW), f32), sd((2, QW), f32), sd((QW, n), f32), vec, sd((n, FQ), f32), vec,
              sd((n, FQ), f32), vec, sd((2, D), f32), sd((2, D), f32))
    return pl.pallas_call(
        emit_kernel, out_shape=shapes, in_specs=[HB] * 5, out_specs=(HB,) + (VM,) * 10,
        scratch_shapes=[pltpu.VMEM(a.shape, a.dtype) for a in arrays] + [pltpu.SemaphoreType.DMA((6,))],
        compiler_params=pltpu.CompilerParams(vmem_limit_bytes=60 << 20),
        name="emit",
    )(*arrays)


def add_low(a, b):
    return (a.astype(f32) + b.astype(f32)).astype(bf)


def on_device(
    ring, input_rows, time_embed, parents, qkv_weight, qv_bias, out_weight, out_bias, inner_weight,
    inner_bias, outer_weight, outer_bias, norm_gain, norm_shift, cotangent,
):
    rank = lax.axis_index("tensor")
    dpos = lax.axis_index("dp")
    part = qkv_weight.shape[0]
    own_ring = ring == 8

    if own_ring:
        whole, w_all, gz, half = gather_start(
            input_rows, time_embed, jnp.transpose(qkv_weight, (1, 0, 2)), inner_weight, outer_weight.T, out_weight,
            inner_bias)
        diagonal = [(i * 4 + j, (i ^ 1) * 4 + (j ^ 2)) for i in range(8) for j in range(4)]
        cross = lambda a: lax.ppermute(a, ("dp", "tensor"), diagonal)
        weights = [gz, across_x(gz), partner(gz, 2), cross(half)]
    else:
        whole = gather_start(input_rows, time_embed)[0]
        w_all = lax.all_gather(qkv_weight.reshape(part, 3 * QW), "dp", axis=0, tiled=True).reshape(8, 96, 3 * QW)
        bias_part = lax.dynamic_slice_in_dim(inner_bias, dpos * part, part, 0)
        packed = jnp.concatenate([inner_weight, out_weight.T, bias_part[:, None],
                                  jnp.zeros((part, OU - AT - QW - 1), bf), outer_weight.T], axis=1)
        packed = lax.all_gather(packed, "dp", axis=0, tiled=True)
        weights = [lax.all_gather(packed, "tensor", axis=0, tiled=False).reshape(4, 4, 2, 96, PK)]

    qt, kv, kt, ot, mix, lse, pairs = attn_fwd(parents, whole, w_all, qv_bias)
    block_out, grad1, dots, *parts, sums = middle(
        weights, mix, input_rows, time_embed, cotangent, out_bias, outer_bias, norm_gain, norm_shift)
    if own_ring:
        parts = [parts[0], across_x(parts[1]), partner(parts[2], 2), cross(parts[3])]
    else:
        far = [partner(parts[2], 2), partner(parts[3], 2)]
    dqt, dkv, block_out = attn_bwd((0, 1, 2), pairs, qt, kv, kt, dots, ot, lse, block_out)
    if own_ring:
        input_grad, pair, qkv_share, share = final(whole, w_all, dqt, dkv, grad1, *parts)
        (input_grad, qkv_share, pair, out_share, out_sum, inner_share, inner_sum, outer_share, outer_sum,
         gains, shifts) = emit(input_grad, pair, qkv_share, share, sums)
        return (block_out, input_grad, jnp.transpose(qkv_share, (1, 0, 2)), pair, out_share, out_sum,
                inner_share, inner_sum, outer_share.T, outer_sum, gains, shifts)
    else:
        input_grad, pair, dwq = final(whole, w_all, dqt, dkv, grad1)
        own, other = add_low(parts[0], far[0]), add_low(parts[1], far[1])
        even = dpos % 2 == 0
        mine = jnp.stack([jnp.where(even, own, other), jnp.where(even, other, own)], axis=1).reshape(D, PK)
        share = lax.psum_scatter(mine, "dp", scatter_dimension=0, tiled=True).astype(f32)
        qkv_share = lax.psum_scatter(dwq, "dp", scatter_dimension=0, tiled=True).astype(f32).reshape(part, 3, QW)
        pair = lax.psum(pair, "dp")
        sums = jnp.sum(lax.all_gather(sums, ("dp", "tensor"), axis=0, tiled=False), axis=0)
    return (
        block_out,
        input_grad,
        qkv_share,
        pair[:2],
        share[:, AT:AT + QW].T,
        sums[5],
        share[:, :FQ],
        lax.dynamic_index_in_dim(sums[6:10], rank, 0, keepdims=False),
        share[:, OU:].T,
        sums[2],
        jnp.stack([sums[3], sums[0]]),
        jnp.stack([sums[4], sums[1]]),
    )


def solution(mesh):
    both = P(("dp", "tensor"), None)
    return jax.shard_map(
        functools.partial(on_device, mesh.shape["dp"]),
        mesh=mesh,
        in_specs=(
            both, P("dp", None), P("dp", None), P("dp", None, "tensor"), P(None, "tensor"),
            P("tensor", "dp"), P(), P("dp", "tensor"), P("tensor"), P("tensor", "dp"), P(), P(), P(), both,
        ),
        out_specs=(
            both, both, P("dp", None, "tensor"), P(None, "tensor"), P("tensor", "dp"), P(),
            P("dp", "tensor"), P("tensor"), P("tensor", "dp"), P(), P(), P(),
        ),
        check_vma=False,
    )
```

```python
import functools
import jax, jax.numpy as jnp
from jax import lax
from jax.experimental import pallas as pl
from jax.experimental.pallas import tpu as pltpu
from jax.sharding import PartitionSpec as P
bf = jnp.bfloat16
f32 = jnp.float32
BLK = 256
TRUNK = 1024
NB = 16
HD = 64
HN = 3
SEGS = 13
PAD = 4
LIST = 192
TQ = 512
TK = 1024
FP = 4
BP = 4
BTQ = 1024
BTK = 256
FQT = 1024
FKT = 512
VM = pl.BlockSpec(memory_space=pltpu.VMEM)
SM = pl.BlockSpec(memory_space=pltpu.SMEM)
HB = pl.BlockSpec(memory_space=pltpu.HBM)
NT = (((1,), (1,)), ((), ()))


def mm(a, b, dims=(((1,), (0,)), ((), ()))):
    return lax.dot_general(a, b, dims, preferred_element_type=f32)


def aligned(i, n):
    return pl.ds(pl.multiple_of(i * n, n), n)


def list_pairs(parents, cur, pairs):
    for s in range(1, SEGS):
        cur[s] = jnp.int32(s)

    def level(_, n):
        for s in range(1, SEGS):
            c = cur[s]
            pairs[0, n] = jnp.int32(s + 3)
            pairs[1, n] = c + 3
            cur[s] = jnp.where(c > 0, parents[0, c], 0)
            n = n + jnp.where(c > 0, 1, 0)
        return n

    n = lax.fori_loop(0, SEGS - 1, level, jnp.int32(0))
    for i in range(PAD - 1):
        pairs[0, n + i] = jnp.int32(NB)
        pairs[1, n + i] = jnp.int32(NB)
    pairs[2, 0] = (n + PAD - 1) // PAD * PAD


PR = 1024


def fwd_kernel(parents, x_hbm, w_hbm, b_ref, qt_hbm, kv_hbm, kt_hbm, o_hbm, mix_hbm, lse_ref, pairs,
               cur, m_s, acc_s, xs, w_s, wt_s, wr_s, br_s, qt_ref, kv_ref, kt_ref, vt_ref, o_ref, mix_ref, sem):
    def fetch(i, slot):
        return pltpu.make_async_copy(x_hbm.at[i], xs.at[slot], sem.at[slot])

    load_w = pltpu.make_async_copy(w_hbm, w_s, sem.at[2])
    load_w.start()
    fetch(0, 0).start()
    list_pairs(parents, cur, pairs)
    load_w.wait()
    bias = b_ref[...].astype(f32)
    bias = jnp.concatenate([bias[0:1], bias[1:2]], 1)
    w = w_s[...].reshape(w_s.shape[0] * w_s.shape[1], w_s.shape[2])
    wt_s[...] = w[:, :HN * HD].T
    for h in range(HN):
        for c in (1, 2):
            to = slice(h * 128 + (c - 1) * HD, h * 128 + c * HD)
            wr_s[:, to] = w[:, c * HN * HD + h * HD:c * HN * HD + (h + 1) * HD]
            part = bias[:, HN * HD + h * HD:HN * HD + (h + 1) * HD] if c == 2 else jnp.zeros((1, HD), f32)
            br_s[:, to] = jnp.broadcast_to(part, (8, HD))
    bias_col = jnp.transpose(jnp.broadcast_to(bias[:, :HN * HD], (8, HN * HD)))
    ones = (lax.broadcasted_iota(jnp.int32, (16, PR), 0) == 0).astype(f32).astype(bf)

    def rows(i, _):
        slot = lax.rem(i, 2)

        @pl.when(i + 1 < NB * BLK // PR)
        def _():
            fetch(i + 1, 1 - slot).start()

        fetch(i, slot).wait()
        cols = aligned(i, PR)
        x = xs[slot]
        kv = (mm(x, wr_s[...]) + br_s[0:1]).astype(bf)
        kv_ref[cols] = kv
        q = (mm(wt_s[...], x, NT) + bias_col[:, 0:1]).astype(bf)
        qt_ref[:, cols] = (q.astype(f32) * 0.125).astype(bf)
        turned = kv.T
        for h in range(HN):
            kt_ref[h * HD:(h + 1) * HD, cols] = turned[h * 128:h * 128 + HD]
            vt_ref[h, :HD, cols] = turned[h * 128 + HD:(h + 1) * 128]
            vt_ref[h, HD:, cols] = ones
        return 0

    lax.fori_loop(0, NB * BLK // PR, rows, 0)
    saves = [pltpu.make_async_copy(a, b, sem.at[3 + n])
             for n, (a, b) in enumerate(((qt_ref, qt_hbm), (kv_ref, kv_hbm), (kt_ref, kt_hbm)))]
    for c in saves:
        c.start()
    zero = jnp.zeros((HD, TQ), bf)

    square = lambda ref, h, cols: jnp.sum(jnp.square(ref[h * HD:(h + 1) * HD, cols].astype(f32)), axis=0, keepdims=True)

    def norms(i, best):
        cols = aligned(i, BLK)
        for h in range(HN):
            m_s[i, h:h + 1] = square(qt_ref, h, cols)
        return tuple(jnp.maximum(best[h], square(kt_ref, h, cols)) for h in range(HN))

    best = lax.fori_loop(0, NB, norms, tuple(jnp.zeros((1, BLK), f32) for h in range(HN)))
    most = [jnp.max(x, axis=1, keepdims=True) for x in best]

    def bounds(i, _):
        for h in range(HN):
            m_s[i, h:h + 1] = jnp.sqrt(m_s[i, h:h + 1] * most[h]) * 1.001
        return 0

    lax.fori_loop(0, NB, bounds, 0)
    m_s[NB] = jnp.zeros((8, BLK), f32)
    wide_zero = jnp.zeros((HD, FQT), bf)

    def fast_tile(i, _):
        per = FQT // BLK
        qz = [jnp.concatenate([qt_ref[h * HD:(h + 1) * HD, aligned(i, FQT)], wide_zero], 0) for h in range(HN)]
        m = [jnp.concatenate([m_s[i * per + j, h:h + 1] for j in range(per)], 1) for h in range(HN)]
        acc = [None] * HN
        for c in range(TRUNK // FKT):
            ks = slice(c * FKT, (c + 1) * FKT)
            p = [jnp.exp(mm(kv_ref[ks, h * 128:(h + 1) * 128], qz[h]) - m[h]).astype(bf) for h in range(HN)]
            a = [mm(vt_ref[h, :, ks], p[h]) for h in range(HN)]
            acc = [x + y for x, y in zip(acc, a)] if c else a
        for h in range(HN):
            for j in range(per):
                acc_s[i * per + j, h] = acc[h][:, j * BLK:(j + 1) * BLK]
        return 0

    lax.fori_loop(0, NB * BLK // FQT, fast_tile, 0)

    def pick(g, count):
        work = []
        for p in range(count):
            q, kb = pairs[0, g * count + p], jnp.minimum(pairs[1, g * count + p], NB - 1)
            work += [(q, aligned(jnp.minimum(q, NB - 1), BLK), aligned(kb, BLK), h) for h in range(HN)]
        return work

    def scores(work):
        return [mm(kv_ref[ks, h * 128:(h + 1) * 128],
                   jnp.concatenate([qt_ref[h * HD:(h + 1) * HD, qs], zero[:, :BLK]], 0)) for q, qs, ks, h in work]

    def fast_step(g, _):
        work = pick(g, FP)
        p = [jnp.exp(x - m_s[q, h:h + 1]).astype(bf) for x, (q, qs, ks, h) in zip(scores(work), work)]
        a = [mm(vt_ref[h, :, ks], x) for x, (q, qs, ks, h) in zip(p, work)]
        for y, (q, qs, ks, h) in zip(a, work):
            acc_s[q, h] += y
        return 0

    lax.fori_loop(0, pairs[2, 0] // FP, fast_step, 0)

    def small(i, bad):
        for h in range(HN):
            bad = jnp.where(acc_s[i, h, HD:HD + 1, :] > 1e-18, bad, 1.0)
        return bad

    bad = jnp.max(lax.fori_loop(0, NB, small, jnp.zeros((1, BLK), f32)))

    @pl.when(bad > 0)
    def _():
        def tile(i, _):
            qz = [jnp.concatenate([qt_ref[h * HD:(h + 1) * HD, aligned(i, TQ)], zero], 0) for h in range(HN)]
            m, acc = [None] * HN, [None] * HN
            for c in range(TRUNK // TK):
                ks = slice(c * TK, (c + 1) * TK)
                s = [mm(kv_ref[ks, h * 128:(h + 1) * 128], qz[h]) for h in range(HN)]
                new = [jnp.max(x, axis=0, keepdims=True) for x in s]
                if c:
                    new = [jnp.maximum(x, y) for x, y in zip(m, new)]
                p = [jnp.exp(x - y).astype(bf) for x, y in zip(s, new)]
                a = [mm(vt_ref[h, :, ks], p[h]) for h in range(HN)]
                if c:
                    a = [x * jnp.exp(y - z) + w for x, y, z, w in zip(acc, m, new, a)]
                m, acc = new, a
            for h in range(HN):
                for j in range(TQ // BLK):
                    acc_s[i * (TQ // BLK) + j, h] = acc[h][:, j * BLK:(j + 1) * BLK]
                    m_s[i * (TQ // BLK) + j, h:h + 1] = m[h][:, j * BLK:(j + 1) * BLK]
            return 0

        lax.fori_loop(0, NB * BLK // TQ, tile, 0)

        def step(g, _):
            work = pick(g, 1)
            s = scores(work)
            m = [m_s[q, h:h + 1] for q, qs, ks, h in work]
            new = [jnp.maximum(y, jnp.max(x, axis=0, keepdims=True)) for x, y in zip(s, m)]
            p = [jnp.exp(x - y).astype(bf) for x, y in zip(s, new)]
            a = [mm(vt_ref[h, :, ks], x) for x, (q, qs, ks, h) in zip(p, work)]
            a = [acc_s[q, h] * jnp.exp(x - y) + z for x, y, z, (q, qs, ks, h) in zip(m, new, a, work)]
            for x, y, (q, qs, ks, h) in zip(new, a, work):
                m_s[q, h:h + 1] = x
                acc_s[q, h] = y
            return 0

        lax.fori_loop(0, pairs[2, 0], step, 0)

    rank = lax.axis_index("tensor")

    def finish(i, _):
        qs = aligned(i, BLK)
        slot = jnp.bitwise_xor(rank, i // 4)
        for h in range(HN):
            total = acc_s[i, h, HD:HD + 1, :]
            out = acc_s[i, h, 0:HD, :] / total
            o_ref[h * HD:(h + 1) * HD, qs] = out
            mix_ref[slot, h * HD:(h + 1) * HD, aligned(lax.rem(i, 4), BLK)] = out.astype(bf)
            lse_ref[h:h + 1, qs] = m_s[i, h:h + 1] + jnp.log(total)
        return 0

    lax.fori_loop(0, NB, finish, 0)
    saves += [pltpu.make_async_copy(mix_ref, mix_hbm, sem.at[6]), pltpu.make_async_copy(o_ref, o_hbm, sem.at[7])]
    for c in saves[3:]:
        c.start()
    for c in saves:
        c.wait()


def attn_fwd(parents, whole, w, bias):
    S = NB * BLK
    sd = jax.ShapeDtypeStruct
    vm = pltpu.VMEM
    n = HN * HD
    d = whole.shape[2]
    return pl.pallas_call(
        fwd_kernel,
        out_shape=(sd((n, S), bf), sd((S, 2 * n), bf), sd((n, S), bf), sd((n, S), f32), sd((4, n, S // 4), bf),
                   sd((8, S), f32), sd((3, LIST), jnp.int32)),
        in_specs=[SM, HB, HB, VM], out_specs=(HB,) * 5 + (VM, SM),
        scratch_shapes=[pltpu.SMEM((16,), jnp.int32), vm((NB + 1, 8, BLK), f32), vm((NB + 1, HN, 80, BLK), f32),
                        vm((2, PR, d), bf), vm(w.shape, bf), vm((n, d), bf), vm((d, 2 * n), bf), vm((8, 2 * n), f32),
                        vm((n, S), bf), vm((S, 2 * n), bf), vm((n, S), bf), vm((HN, 80, S), bf),
                        vm((n, S), f32), vm((4, n, S // 4), bf), pltpu.SemaphoreType.DMA((8,))],
        compiler_params=pltpu.CompilerParams(vmem_limit_bytes=63 << 20),
        cost_estimate=pl.CostEstimate(flops=40_000_000_000, bytes_accessed=12_000_000, transcendentals=18_000_000),
        name="tree_attention",
    )(parents, whole, w, bias)


def bwd_kernel(heads, pairs, qt_hbm, kv_hbm, kt_hbm, dots_hbm, o_hbm, lse_ref, rows_in, dqt_hbm, dkv_hbm, rows_out,
               rows_s, dkv_s, dq_s, st_s, dot_ref, qt_ref, kv_ref, kt_ref, dots, o_ref, dqt_ref, dkv_ref, sem):
    loads = [pltpu.make_async_copy(a, b, sem.at[n]) for n, (a, b) in enumerate((
        (dots_hbm, dots), (o_hbm, o_ref), (qt_hbm, qt_ref), (kv_hbm, kv_ref), (kt_hbm, kt_ref)))]
    for c in loads:
        c.start()
    through = [pltpu.make_async_copy(rows_in, rows_s, sem.at[7]), pltpu.make_async_copy(rows_s, rows_out, sem.at[8])]
    through[0].start()
    dkv_s[...] = jnp.zeros_like(dkv_s)
    dq_s[...] = jnp.zeros_like(dq_s)
    rank = lax.axis_index("tensor")
    loads[0].wait()
    for m in range(4):
        dot_ref[:, aligned(jnp.bitwise_xor(rank, m), NB * BLK // 4)] = dots[m]
    loads[1].wait()

    def stats(i, _):
        qs = aligned(i, BLK)
        for n, h in enumerate(heads):
            rows = slice(h * HD, (h + 1) * HD)
            st_s[i, n:n + 1] = jnp.sum(dot_ref[rows, qs].astype(f32) * o_ref[rows, qs], axis=0, keepdims=True)
            st_s[i, 4 + n:5 + n] = lse_ref[h:h + 1, qs]
        return 0

    lax.fori_loop(0, NB, stats, 0)
    for c in loads[2:]:
        c.wait()
    through[0].wait()
    through[1].start()

    def chains(work, width):
        zero = jnp.zeros((HD, width), bf)
        rows = lambda h: slice(h * HD, (h + 1) * HD)
        qz = [jnp.concatenate([qt_ref[rows(h), qs], zero], 0) for h, qs, ks, lse, delta in work]
        dz = [jnp.concatenate([zero, dot_ref[rows(h), qs]], 0) for h, qs, ks, lse, delta in work]
        kv = [kv_ref[ks, h * 128:(h + 1) * 128] for h, qs, ks, lse, delta in work]
        p = [jnp.exp(mm(x, y) - w[3]) for x, y, w in zip(kv, qz, work)]
        ds = [(x * (mm(y, z) - w[4])).astype(bf) for x, y, z, w in zip(p, kv, dz, work)]
        g = [mm(jnp.concatenate([x, y.astype(bf)], 1), jnp.concatenate([z, u], 1), NT)
             for x, y, z, u in zip(ds, p, qz, dz)]
        return g, [mm(kt_ref[rows(h), ks], x) for x, (h, qs, ks, lse, delta) in zip(ds, work)]

    per = BTQ // BLK

    def tile(i, _):
        row = lambda k: jnp.concatenate([st_s[i * per + j, k:k + 1] for j in range(per)], 1)
        dq = [None] * len(heads)
        for c in range(TRUNK // BTK):
            ks = slice(c * BTK, (c + 1) * BTK)
            g, d = chains([(h, aligned(i, BTQ), ks, row(4 + n), row(n)) for n, h in enumerate(heads)], BTQ)
            for n in range(len(heads)):
                dkv_s[ks, n * 128:(n + 1) * 128] += g[n]
                dq[n] = d[n] if c == 0 else dq[n] + d[n]
        for n in range(len(heads)):
            for j in range(per):
                dq_s[i * per + j, n] += dq[n][:, j * BLK:(j + 1) * BLK]
        return 0

    lax.fori_loop(0, NB * BLK // BTQ, tile, 0)

    def step(s, _):
        work, where = [], []
        for p in range(BP):
            q, kb = pairs[0, s * BP + p], pairs[1, s * BP + p]
            qr = jnp.minimum(q, NB - 1)
            for n, h in enumerate(heads):
                work.append((h, aligned(qr, BLK), aligned(jnp.minimum(kb, NB - 1), BLK),
                             st_s[qr, 4 + n:5 + n], st_s[qr, n:n + 1]))
                where.append((q, kb, n))
        for g, d, (q, kb, n) in zip(*chains(work, BLK), where):
            dkv_s[aligned(kb, BLK), n * 128:(n + 1) * 128] += g
            dq_s[q, n] += d
        return 0

    lax.fori_loop(0, pairs[2, 0] // BP, step, 0)

    def finish(i, _):
        for n in range(len(heads)):
            dqt_ref[n * HD:(n + 1) * HD, aligned(i, BLK)] = (dq_s[i, n] * 0.125).astype(bf)
        dkv_ref[aligned(i, BLK)] = dkv_s[aligned(i, BLK)].astype(bf)
        save(i).start()
        return 0

    def save(i):
        return pltpu.make_async_copy(dkv_ref.at[aligned(i, BLK)], dkv_hbm.at[aligned(i, BLK)], sem.at[9 + i])

    lax.fori_loop(0, NB, finish, 0)
    last = pltpu.make_async_copy(dqt_ref, dqt_hbm, sem.at[5])
    last.start()
    for i in range(NB):
        save(i).wait()
    last.wait()
    through[1].wait()


def attn_bwd(heads, pairs, qt, kv, kt, dots, o, lse, rows):
    S = qt.shape[1]
    sd = jax.ShapeDtypeStruct
    n = len(heads)
    return pl.pallas_call(
        functools.partial(bwd_kernel, heads),
        out_shape=(sd((n * HD, S), bf), sd((S, n * 128), bf), sd(rows.shape, rows.dtype)),
        in_specs=[SM] + [HB] * 5 + [VM, HB], out_specs=(HB, HB, HB),
        scratch_shapes=[pltpu.VMEM(rows.shape, rows.dtype), pltpu.VMEM((S + BLK, n * 128), f32), pltpu.VMEM((NB + 1, n, HD, BLK), f32),
                        pltpu.VMEM((NB, 8, BLK), f32), pltpu.VMEM((HN * HD, S), bf)]
        + [pltpu.VMEM(a.shape, a.dtype) for a in (qt, kv, kt, dots, o)]
        + [pltpu.VMEM((n * HD, S), bf), pltpu.VMEM((S, n * 128), bf), pltpu.SemaphoreType.DMA((9 + NB,))],
        compiler_params=pltpu.CompilerParams(vmem_limit_bytes=63 << 20),
        cost_estimate=pl.CostEstimate(flops=20_000_000_000 * n, bytes_accessed=8_000_000 * n, transcendentals=6_000_000 * n),
        name="tree_attention_grad",
    )(pairs, qt, kv, kt, dots, o, lse, rows)


D = 768
SEQ = 4096
ROWS = SEQ // 4
QW = HN * HD
FQ = 768
AT = FQ
OU = FQ + 256
PK = OU + FQ
MESH = pl.DeviceIdType.MESH
HBM = pl.BlockSpec(memory_space=pl.ANY)
TN = (((0,), (0,)), ((), ()))
epsilon = 1e-05
root_half = 0.7071067811865476
inv_root_tau = 0.3989422804014327


def layer_norm(summed, gain_row, shift_row):
    centre = jnp.mean(summed, axis=-1, keepdims=True)
    offset = summed - centre
    inv_std = lax.rsqrt(jnp.mean(offset * offset, axis=-1, keepdims=True) + epsilon)
    normed = offset * inv_std
    return normed * gain_row + shift_row, normed, inv_std


def norm_back(grad_out, normed, inv_std, gain_row):
    scaled = grad_out * gain_row
    return inv_std * (
        scaled
        - jnp.mean(scaled, axis=-1, keepdims=True)
        - normed * jnp.mean(scaled * normed, axis=-1, keepdims=True)
    )


def gelu_parts(u):
    half = 0.5 * (1.0 + lax.erf(u * root_half))
    return u * half, half + u * inv_root_tau * jnp.exp(-0.5 * u * u)


def partner(x, mask):
    return lax.ppermute(x, "tensor", [(i, i ^ mask) for i in range(4)])


def across_x(x):
    return lax.ppermute(x, "dp", [(i, i ^ 1) for i in range(8)])


def flip1(r):
    return r + 1 - 2 * lax.rem(r, 2)


CH = 4
CROWS = ROWS // CH


def remote(src, dst, s, q, dev):
    return pltpu.make_async_remote_copy(
        src_ref=src, dst_ref=dst, send_sem=s, recv_sem=q, device_id=dev, device_id_type=MESH)


def meet(targets, meanwhile=None):
    barrier = pltpu.get_barrier_semaphore()
    for t in targets:
        pl.semaphore_signal(barrier, inc=1, device_id=t, device_id_type=MESH)
    if meanwhile is not None:
        meanwhile()
    pl.semaphore_wait(barrier, len(targets))


class Sends:
    def __init__(self):
        self.started = []

    def go(self, *args):
        c = remote(*args)
        c.start()
        self.started.append(c)
        return c

    def drain(self):
        for c in self.started:
            c.wait_send()


def gather_kernel(with_w, *refs):
    if with_w:
        (inp, te, wq, w1, w2, w3, bias, whole_hbm, wqg_hbm, gz_hbm, gl_hbm, whole, wqg, gz, bcol,
         ysend, yrecv, csend, crecv, out, zsend, zrecv, xsend, xrecv) = refs
    else:
        inp, te, whole_hbm, whole, ysend, yrecv, csend, crecv, out = refs
    r = lax.axis_index("tensor")
    d = lax.axis_index("dp")
    rc, ry = flip1(r), lax.rem(r + 2, 4)
    core, yy = {"tensor": rc}, {"tensor": ry}
    targets = [core, yy]
    if with_w:
        z, x = d // 2, lax.rem(d, 2)
        xx = {"dp": flip1(d)}
        up, down = {"dp": lax.rem(z + 1, 4) * 2 + x}, {"dp": lax.rem(z + 3, 4) * 2 + x}
        targets += [xx, up, down]

    def prepare():
        shift = te[...].astype(f32)
        whole[r] = (inp[...].astype(f32) + shift).astype(bf)
        if with_w:
            for c in range(3):
                wqg[d, :, c * QW:(c + 1) * QW] = wq[c]

    meet(targets, prepare)
    sends = Sends()
    if with_w:

        def line(a, s, slot, way):
            ref = wqg.at[slot * 2 + x] if a == 0 else gz.at[slot]
            k = 2 * (s - 1) + way
            return remote(ref, ref, zsend.at[a, k], zrecv.at[a, k], (up, down)[way])

        def side(i, slot):
            ref = wqg.at[slot * 2 + x]
            return remote(ref, ref, xsend.at[i], xrecv.at[i], xx)

        def can_send(s, way):
            return jnp.logical_and(z < 3, z - s + 1 >= 0) if way == 0 else jnp.logical_and(z > 0, z + s - 1 <= 3)

        def can_recv(s, way):
            return z - s >= 0 if way == 0 else z + s <= 3

        def own(a):
            for way in (0, 1):
                @pl.when(can_send(1, way))
                def _():
                    line(a, 1, z, way).start()

        own(0)
        side(0, z).start()
    rows = [pl.ds(i * CROWS, CROWS) for i in range(CH)]
    yc = []
    for i in range(CH):
        mine = whole.at[r, rows[i]]
        yc.append(sends.go(mine, mine, ysend.at[i], yrecv.at[i], yy))
    c0 = sends.go(whole.at[r], whole.at[r], csend.at[CH], crecv.at[CH], core)
    if with_w:
        part = wqg.shape[1]
        gz[z, :, 0:FQ] = w1[...]
        gz[z, :, OU:] = w2[...]
        bcol[...] = jnp.transpose(jnp.broadcast_to(bias[...].astype(f32).reshape(1, D), (8, D)))
        fill = OU - AT - QW
        column = bcol[pl.ds(pl.multiple_of(d * part, 32), part), 0:1]
        column = jnp.where(lax.broadcasted_iota(jnp.int32, (part, fill), 1) == 0, column, 0.0)
        gz[z, :, AT:OU] = jnp.concatenate([w3[...].astype(f32).T, column], 1).astype(bf)
        own(1)
        for s in (1, 2, 3):
            for way in (0, 1):
                slot = z - s if way == 0 else z + s

                @pl.when(can_recv(s, way))
                def _():
                    for a in (0, 1):
                        line(a, s, slot, way).wait_recv()
                        if s < 3:
                            @pl.when(can_send(s + 1, way))
                            def _():
                                line(a, s + 1, slot, way).start()
                        if a == 0:
                            side(slot_sem(s, way), slot).start()
    keeps = []

    def keep(src, dst):
        c = pltpu.make_async_copy(src, dst, out.at[len(keeps)])
        c.start()
        keeps.append(c)

    keep(whole.at[r], whole_hbm.at[r])
    cc = []
    for i in range(CH):
        yc[i].wait_recv()
        part = whole.at[ry, rows[i]]
        cc.append(sends.go(part, part, csend.at[i], crecv.at[i], core))
    keep(whole.at[ry], whole_hbm.at[ry])
    c0.wait_recv()
    keep(whole.at[rc], whole_hbm.at[rc])
    for c in cc:
        c.wait_recv()
    rd = 3 - r
    keep(whole.at[rd], whole_hbm.at[rd])
    if with_w:
        keep(gz, gz_hbm)
        keep(gz.at[pl.ds(0, 2), :, pl.ds(0, OU)], gl_hbm)
        side(0, z).wait()
        for s in (1, 2, 3):
            for way in (0, 1):
                slot = z - s if way == 0 else z + s

                @pl.when(can_recv(s, way))
                def _():
                    side(slot_sem(s, way), slot).wait()

                @pl.when(can_send(s, way))
                def _():
                    for a in (0, 1):
                        line(a, s, slot_of_send(z, s, way), way).wait_send()
        keep(wqg, wqg_hbm)
    for c in keeps:
        c.wait()
    sends.drain()


def slot_of_send(z, s, way):
    return z - s + 1 if way == 0 else z + s - 1


def slot_sem(s, way):
    return 2 * s - 1 + way


def gather_start(inp, te, *weights):
    with_w = len(weights) > 0
    dma = pltpu.SemaphoreType.DMA
    shapes = [jax.ShapeDtypeStruct((4, ROWS, D), bf)]
    args = [inp, te, *weights]
    scratch = []
    sems = [dma((CH,)), dma((CH,)), dma((CH + 1,)), dma((CH + 1,)), dma((8,))]
    if with_w:
        part = weights[0].shape[1]
        line = jax.ShapeDtypeStruct((4, part, PK), bf)
        shapes += [jax.ShapeDtypeStruct((8, part, 3 * QW), bf), line, jax.ShapeDtypeStruct((2, part, OU), bf)]
        scratch = [pltpu.VMEM((D, 8), f32)]
        sems += [dma((2, 6)), dma((2, 6)), dma((7,)), dma((7,))]
    return pl.pallas_call(
        functools.partial(gather_kernel, with_w),
        out_shape=shapes, in_specs=[VM] * len(args), out_specs=[HB] * len(shapes),
        scratch_shapes=[pltpu.VMEM(a.shape, bf) for a in shapes[:3]] + scratch + sems,
        compiler_params=pltpu.CompilerParams(collective_id=0, has_side_effects=True, vmem_limit_bytes=60 << 20),
        name="gather_start",
    )(*args)


RB = 512
NR = ROWS // RB


def middle_kernel(with_w, *refs):
    if with_w:
        wa, wb, wc, wd = refs[:4]
        step, line_s, xsend, xrecv, wsend, wrecv, ssend, srecv = refs[-8:]
        refs = refs[4:-8]
    else:
        wfull, refs = refs[0], refs[1:]
    (mix_hbm, inp_hbm, te, cot_hbm, ob, fb, ng, ns, block_hbm, grad1_hbm, dots_hbm, p00, p01, p10, p11, sums_o,
     inp, cot, block_out, grad1_o, w, wt_s, mix, mixr, gmix, dots, both, ht, gmt, gat, act, gp, slope_s,
     loc, asend, arecv, bsend, brecv, gsend, grecv) = refs
    r = lax.axis_index("tensor")
    d = lax.axis_index("dp")
    x = lax.rem(d, 2)
    ranks = [r, flip1(r), lax.rem(r + 2, 4), 3 - r]
    devices = [{"tensor": k} for k in ranks]
    xx = {"dp": flip1(d)}
    load = pltpu.make_async_copy(mix_hbm, mix, loc.at[5])
    load.start()
    rows_in = [pltpu.make_async_copy(inp_hbm, inp, loc.at[19]), pltpu.make_async_copy(cot_hbm, cot, loc.at[20])]
    for c in rows_in:
        c.start()
    if with_w:
        z = d // 2
        zdev = [{"dp": lax.rem(z + k, 4) * 2 + x} for k in range(4)]
        meet(devices[1:] + [xx] + zdev[1:])
    else:
        meet(devices[1:])
    sends = Sends()
    core = devices[1]
    load.wait()

    def heads_in(b, m):
        cols = pl.ds(b * RB, RB)
        k = lax.axis_index("tensor")
        peer = {"tensor": (k, flip1(k), lax.rem(k + 2, 4), 3 - k)[m]}
        return remote(mix.at[m, :, cols], mixr.at[m, :, cols], asend.at[b, m], arecv.at[b, m], peer)

    def heads_out(b, m):
        cols = aligned(b, RB)
        return remote(gmix.at[m, :, cols], dots.at[m, :, cols], bsend.at[b, m], brecv.at[b, m], devices[m])

    heads = [[heads_in(b, m) for m in (3, 2, 1)] for b in range(NR)]
    for c in heads[0]:
        c.start()
    fill = pltpu.make_async_copy(mix.at[0], mixr.at[0], loc.at[0])
    fill.start()

    def weight_moves(j, relay, hand, place):
        rank, side = lax.axis_index("tensor"), lax.rem(lax.axis_index("dp"), 2)
        span = (pl.ds(0, OU), pl.ds(OU, FQ))[j]
        other = lax.rem(rank + 2, 4)
        four, two, end = pl.ds(0, 4), pl.ds(0, 2), pl.ds(2, 2)
        near = {"tensor": flip1(rank)}
        if relay is not None:
            relay(remote(wc.at[end, :, span], w.at[other, end, side, :, span], xsend.at[j], xrecv.at[j],
                         {"dp": flip1(lax.axis_index("dp"))}))
            if j:
                relay(remote(wb.at[two, :, span], w.at[rank, two, 1 - side, :, span], xsend.at[2], xrecv.at[2],
                             {"tensor": other}))
        pieces = ((wa, rank, four, side), (wb, rank, four, 1 - side), (wc, other, four, side), (wd, other, two, 1 - side))
        for i, (ref, t, zz, at) in enumerate(pieces[:4 - j]):
            src, dst = ref.at[:, :, span], w.at[t, zz, at, :, span]
            if hand is not None:
                hand(remote(src, dst, wsend.at[j, i], wrecv.at[j, i], near))
            if place is not None:
                place(pltpu.make_async_copy(src, dst, loc.at[11 + 4 * j + i]))

    def whole_fill(j):
        span = (pl.ds(0, OU), pl.ds(OU, FQ))[j]
        return pltpu.make_async_copy(wfull.at[:, :, :, :, span], w.at[:, :, :, :, span], loc.at[1 + j])

    def weight_tail(j):
        rank, side = lax.axis_index("tensor"), lax.rem(lax.axis_index("dp"), 2)
        tail = w.at[lax.rem(rank + 2, 4), (pl.ds(2, 2), pl.ds(0, 4))[j], 1 - side, :, (pl.ds(0, OU), pl.ds(OU, FQ))[j]]
        return remote(tail, tail, wsend.at[j, 4], wrecv.at[j, 4], {"tensor": flip1(rank)})

    if with_w:
        weight_moves(0, lambda c: c.start(), lambda c: c.start(), lambda c: c.start())
    else:
        for j in (0, 1):
            whole_fill(j).start()
    sums_o[...] = jnp.zeros_like(sums_o)
    out_bias, outer_bias = (v[...].astype(f32).reshape(1, D) for v in (ob, fb))
    gains, shifts = ng[...].astype(f32), ns[...].astype(f32)
    gain1, gain2, shift1, shift2 = gains[0:1], gains[1:2], shifts[0:1], shifts[1:2]
    def weights_here(j):
        if with_w:
            weight_moves(j, lambda c: c.wait_recv(), None, None)
            weight_tail(j).start()
            weight_moves(j, None, lambda c: c.wait_recv(), lambda c: c.wait())
            weight_tail(j).wait_recv()
        else:
            whole_fill(j).wait()

    weights_here(0)
    for c in heads[0]:
        c.wait_recv()
    if with_w:
        weight_moves(1, lambda c: c.start(), lambda c: c.start(), lambda c: c.start())
    fill.wait()
    for c in rows_in:
        c.wait()
    for t in range(4):
        wt_s[t] = jnp.transpose(w[t, :, :, :, AT:OU].reshape(D, OU - AT))
    bias_in = [wt_s[t, QW:QW + 16].astype(f32)[0:1] for t in range(4)]
    w_in = lambda t: w[t, :, :, :, 0:FQ].reshape(D, FQ)
    w_ou = lambda t: w[t, :, :, :, OU:].reshape(D, FQ)

    def add_sum(i, rows):
        sums_o[i:i + 1] += jnp.sum(rows, axis=0, keepdims=True)

    def block(b, _):
        for i in range(1, NR):
            @pl.when(b == i)
            def _():
                for c in heads[i]:
                    c.wait_recv()
        rows = aligned(b, RB)
        start = inp[rows].astype(f32) + te[...].astype(f32)
        attn = out_bias
        for m in range(4):
            attn = attn + mm(mixr[m, :, rows], wt_s[ranks[m], :QW], TN)
        hidden, normed1, inv1 = layer_norm(start + attn, gain1, shift1)
        low = hidden.astype(bf)
        ht[:, rows] = low.T
        for t in range(4):
            u = mm(low, w_in(t)) + bias_in[t]
            value, slope = gelu_parts(u)
            act[t, rows] = value.astype(bf)
            slope_s[t] = slope.astype(bf)

        @pl.when(b == 0)
        def _():
            weights_here(1)
            for i in range(1, NR):
                for m in (3, 2, 1):
                    heads_in(i, m).start()

        mlp = outer_bias
        for t in range(4):
            mlp = mlp + mm(act[t, rows], w_ou(t), NT)
        final, normed2, inv2 = layer_norm(hidden + mlp, gain2, shift2)
        block_out[rows] = final.astype(bf)
        e = cot[rows].astype(f32)
        add_sum(0, e * normed2)
        add_sum(1, e)
        grad2 = norm_back(e, normed2, inv2, gain2)
        gm = grad2.astype(bf)
        gmt[:, rows] = gm.T
        add_sum(2, gm.astype(f32))
        gin = grad2
        for t in range(4):
            g = (mm(gm, w_ou(t)) * slope_s[t].astype(f32)).astype(bf)
            gp[t, rows] = g
            add_sum(6 + t, g.astype(f32))
            gin = gin + mm(g, w_in(t), NT)
        add_sum(3, gin * normed1)
        add_sum(4, gin)
        grad1 = norm_back(gin, normed1, inv1, gain1)
        grad1_o[rows] = grad1
        ga = grad1.astype(bf)
        gat_rows = ga.T
        gat[:, rows] = gat_rows
        add_sum(5, ga.astype(f32))
        for m in (3, 2, 1):
            gmix[m, :, rows] = mm(wt_s[ranks[m], :QW], gat_rows).astype(bf)
            heads_out(b, m).start()
        dots[0, :, rows] = mm(wt_s[r, :QW], gat_rows).astype(bf)
        return 0

    lax.fori_loop(0, NR, block, 0)

    if with_w:
        for j in (0, 1):
            weight_moves(j, lambda c: c.wait_send(), lambda c: c.wait_send(), None)
            weight_tail(j).wait_send()

    def grads(t, m):
        return (lambda: mm(ht[...], gp[t]), lambda: mm(gmt[...], act[t]), lambda: mm(gat[...], mixr[m], NT))

    cols = (slice(0, FQ), slice(OU, PK), slice(AT, AT + QW))
    blank = jnp.zeros((4, 2, 96, OU - AT - QW), bf)
    cut = lambda g: g.reshape(4, 2, 96, g.shape[1])

    def handing(q):
        return remote(w.at[q], both.at[q], gsend.at[q], grecv.at[q], core)

    hops = []

    def hop(n):
        if not with_w:
            return
        if n:
            hops[-1].wait_recv()
        step[n] = step[n - 1] + step[n + 3] if n else sums_o[...]
        hops.append(sends.go(step.at[n], step.at[n + 4], ssend.at[n], srecv.at[n], (core, devices[2], xx)[n]))

    hop(0)
    saves = [pltpu.make_async_copy(grad1_o, grad1_hbm, loc.at[21]), pltpu.make_async_copy(block_out, block_hbm, loc.at[22])]
    for c in saves:
        c.start()
    for q in (1, 0):
        for c, g in zip(cols, grads(ranks[2 * q + 1], 2 * q + 1)):
            w[q, :, :, :, c] = cut(g().astype(bf))
        w[q, :, :, :, AT + QW:OU] = blank
        handing(q).start()
        hop(2 - q)
    for q in (1, 0):
        mine = grads(ranks[2 * q], 2 * q)
        handing(q).wait_recv()
        for c, g in zip(cols, mine):
            both[q, :, :, :, c] = (both[q, :, :, :, c].astype(f32) + cut(g())).astype(bf)
        for n, side in ((0, x), (1, 1 - x)):
            to = ((p00, p01), (p10, p11))[q][n]
            saves.append(pltpu.make_async_copy(both.at[q, :, side], to, loc.at[6 + 2 * q + n]))
            saves[-1].start()
        if with_w and q:
            hops[-1].wait_recv()
            line_s[z] = step[2] + step[6]
            ends = [sends.go(line_s.at[z], line_s.at[z], ssend.at[2 + k], srecv.at[2 + k], zdev[k]) for k in (1, 2, 3)]
    if with_w:
        for c in ends:
            c.wait_recv()
        sums_o[...] = ((line_s[0] + line_s[1]) + line_s[2]) + line_s[3]
    for b in range(NR):
        for m in (1, 2, 3):
            heads_out(b, m).wait()
        for c in heads[b]:
            c.wait_send()
    saves.append(pltpu.make_async_copy(dots, dots_hbm, loc.at[10]))
    saves[-1].start()
    for c in saves:
        c.wait()
    for q in range(2):
        handing(q).wait_send()
    sends.drain()


def middle(weights, mix, *rest):
    sd = jax.ShapeDtypeStruct
    dma = pltpu.SemaphoreType.DMA
    with_w = len(weights) > 1
    vm = pltpu.VMEM
    tokens = (D, ROWS)
    extra = [vm((7, 16, D), f32), vm((4, 16, D), f32), dma((3,)), dma((3,)), dma((2, 5)), dma((2, 5)),
             dma((6,)), dma((6,))] if with_w else []
    return pl.pallas_call(
        functools.partial(middle_kernel, with_w),
        out_shape=(sd((ROWS, D), bf), sd((ROWS, D), f32), sd((4, QW, ROWS), bf),
                   *([sd((4, 96, PK), bf)] * 4), sd((16, D), f32)),
        in_specs=[HB] * len(weights) + [HB, HB, VM, HB] + [VM] * 4, out_specs=(HB, HB, HB, HB, HB, HB, HB, VM),
        scratch_shapes=[vm((ROWS, D), bf), vm((ROWS, D), bf), vm((ROWS, D), bf), vm((ROWS, D), f32),
                        vm((4, 4, 2, 96, PK), bf), vm((4, OU - AT, D), bf), vm((4, QW, ROWS), bf),
                        vm((4, QW, ROWS), bf), vm((4, QW, ROWS), bf), vm((4, QW, ROWS), bf),
                        vm((2, 4, 2, 96, PK), bf), vm(tokens, bf), vm(tokens, bf), vm(tokens, bf),
                        vm((4, ROWS, FQ), bf), vm((4, ROWS, FQ), bf), vm((4, RB, FQ), bf),
                        dma((23,)), dma((NR, 4)), dma((NR, 4)), dma((NR, 4)), dma((NR, 4)), dma((2,)), dma((2,))] + extra,
        compiler_params=pltpu.CompilerParams(collective_id=2, has_side_effects=True, vmem_limit_bytes=63 << 20),
        cost_estimate=pl.CostEstimate(flops=33_000_000_000, bytes_accessed=50_000_000, transcendentals=9_000_000),
        name="middle",
    )(*weights, mix, *rest)


def final_kernel(with_w, *refs):
    if with_w:
        (x_hbm, w_hbm, dqt_hbm, dkv_hbm, g1_hbm, m0_hbm, m1_hbm, m2_hbm, m3_hbm, out, pair, qo, mo,
         x_s, w_s, wr_s, dqt, dkv, grad1, part, crv, ysd, yrv, m0, m1, m2, m3, zsm, zrm, dwq, xrq, zsq, zrq,
         prv, psd, prs, loc, csend, crecv, ysend, yrecv, xsend, xrecv, zsend, zrecv) = refs
    else:
        (x_hbm, w_hbm, dqt_hbm, dkv_hbm, g1_hbm, out, pair, dw,
         x_s, w_s, wr_s, dqt, dkv, grad1, part, crv, ysd, yrv, loc, csend, crecv, ysend, yrecv) = refs
    pulls = [(w_hbm, w_s), (dqt_hbm, dqt), (dkv_hbm, dkv)]
    pulls += [(m0_hbm, m0), (m1_hbm, m1), (m2_hbm, m2), (m3_hbm, m3)] if with_w else []
    pulls += [(x_hbm, x_s), (g1_hbm, grad1)]
    loads = [pltpu.make_async_copy(a, b, loc.at[n]) for n, (a, b) in enumerate(pulls)]
    for c in loads[:-2]:
        c.start()
    r = lax.axis_index("tensor")
    d = lax.axis_index("dp")
    rc, ry = flip1(r), lax.rem(r + 2, 4)
    rd = 3 - r
    core, yy = {"tensor": rc}, {"tensor": ry}
    targets = [core, yy]
    if with_w:
        z, x = d // 2, lax.rem(d, 2)
        xo = 1 - x
        zs = [lax.rem(z + k, 4) for k in range(4)]
        xx = {"dp": flip1(d)}
        zdev = [{"dp": zs[k] * 2 + x} for k in range(4)]
        targets += [xx] + zdev[1:]
    meet(targets)
    sends = Sends()
    go = sends.go
    wait = lambda *which: [loads[n].wait() for n in which]
    rows = [pl.ds(i * CROWS, CROWS) for i in range(CH)]
    if with_w:
        wait(3, 4, 5, 6)
        zm = []
        for k in (1, 2, 3, 0):
            at = zs[k]
            zsm[k] = ((m0[at].astype(f32) + m1[at].astype(f32)) + (m2[at].astype(f32) + m3[at].astype(f32))).astype(bf)
            if k:
                zm.append(go(zsm.at[k], zrm.at[k - 1], zsend.at[1, k - 1], zrecv.at[1, k - 1], zdev[k]))
    wait(0, 1, 2)
    for c in loads[-2:]:
        c.start()
    w = w_s[...].reshape(D, 3 * QW)
    for h in range(HN):
        for c in (1, 2):
            wr_s[:, h * 128 + (c - 1) * HD:h * 128 + c * HD] = w[:, c * QW + h * HD:c * QW + (h + 1) * HD]
    wqs = w[:, :QW]

    def project_back(t, i):
        at = pl.ds(pl.multiple_of(t * ROWS + i * CROWS, CROWS), CROWS)
        part[t, rows[i]] = (mm(dqt[:, at], wqs, (((0,), (1,)), ((), ()))) + mm(dkv[at], wr_s[...], NT)).astype(bf)

    first, second, third = [], [], []
    for i in range(CH):
        project_back(rd, i)
        second.append(go(part.at[rd, rows[i]], crv.at[1, rows[i]], csend.at[1, i], crecv.at[1, i], core))
        project_back(ry, i)
        if i:
            second[i - 1].wait_recv()
            prev = rows[i - 1]
            ysd[prev] = (part[ry, prev].astype(f32) + crv[1, prev].astype(f32)).astype(bf)
            third.append(go(ysd.at[prev], yrv.at[prev], ysend.at[i - 1], yrecv.at[i - 1], yy))
    prev = rows[CH - 1]
    second[CH - 1].wait_recv()
    ysd[prev] = (part[ry, prev].astype(f32) + crv[1, prev].astype(f32)).astype(bf)
    third.append(go(ysd.at[prev], yrv.at[prev], ysend.at[CH - 1], yrecv.at[CH - 1], yy))

    wait(len(loads) - 2)
    whole = x_s[...].reshape(SEQ, D)
    aq = mm(dqt[...], whole)
    akv = mm(dkv[...], whole, TN)
    blocks = [aq]
    for c in (0, 1):
        blocks += [akv[h * 128 + c * HD:h * 128 + (c + 1) * HD] for h in range(HN)]
    dwt = jnp.concatenate(blocks, 0).T.astype(bf)
    sum_q = jnp.sum(dqt[...].astype(f32), axis=1, keepdims=True)
    sum_q = jnp.transpose(jnp.broadcast_to(sum_q, (QW, 8)))
    sum_kv = jnp.sum(dkv[...].astype(f32), axis=0, keepdims=True)
    sum_v = jnp.concatenate([sum_kv[:, h * 128 + HD:(h + 1) * 128] for h in range(HN)], 1)
    pairs = jnp.concatenate([sum_q[0:1], sum_v, jnp.zeros((6, QW), f32)], 0)
    if with_w:
        dwq[...] = dwt.reshape(dwq.shape)
        xq = go(dwq.at[:, xo], xrq, xsend.at[0], xrecv.at[0], xx)
        prs[...] = pairs
        px = go(prs, prv, xsend.at[1], xrecv.at[1], xx)
    for i in range(CH):
        project_back(rc, i)
        first.append(go(part.at[rc, rows[i]], crv.at[0, rows[i]], csend.at[0, i], crecv.at[0, i], core))
        project_back(r, i)
    if with_w:
        px.wait_recv()
        psd[z] = prs[...] + prv[...]
        zp = [go(psd.at[z], psd.at[z], zsend.at[2, k - 1], zrecv.at[2, k - 1], zdev[k]) for k in (1, 2, 3)]
        xq.wait_recv()
        for k in range(4):
            zsq[k] = (dwq[zs[k], x].astype(f32) + xrq[zs[k]].astype(f32)).astype(bf)
        zq = [go(zsq.at[k], zrq.at[k - 1], zsend.at[0, k - 1], zrecv.at[0, k - 1], zdev[k]) for k in (1, 2, 3)]
    else:
        dw[...] = dwt
        pair[...] = pairs
    wait(len(loads) - 1)
    for i in range(CH):
        first[i].wait_recv()
        third[i].wait_recv()
        out[rows[i]] = (part[r, rows[i]].astype(f32) + crv[0, rows[i]].astype(f32)
                        + yrv[rows[i]].astype(f32) + grad1[rows[i]]).astype(bf)
    if with_w:
        for c in zq:
            c.wait_recv()
        whole_q = (zsq[0].astype(f32) + zrq[0].astype(f32)) + (zrq[1].astype(f32) + zrq[2].astype(f32))
        qo[...] = whole_q
        for c in zp:
            c.wait_recv()
        pair[...] = ((psd[0] + psd[1]) + psd[2]) + psd[3]
        for c in zm:
            c.wait_recv()
        mo[...] = (zsm[0].astype(f32) + zrm[0].astype(f32)) + (zrm[1].astype(f32) + zrm[2].astype(f32))
    sends.drain()


def final(whole, w, dqt, dkv, grad1, *more):
    with_w = len(more) > 0
    dma = pltpu.SemaphoreType.DMA
    sd = jax.ShapeDtypeStruct
    vm = pltpu.VMEM
    rows = (ROWS, D)
    like = lambda a: vm(a.shape, a.dtype)
    shapes = [sd(rows, bf), sd((8, QW), f32)]
    args = [whole, w, dqt, dkv, grad1, *more]
    scratch = [like(whole), like(w), vm((D, 2 * QW), bf), like(dqt), like(dkv), like(grad1), vm((4,) + rows, bf),
               vm((2,) + rows, bf), vm(rows, bf), vm(rows, bf)]
    sems = [dma((9,)), dma((2, CH)), dma((2, CH)), dma((CH,)), dma((CH,))]
    if with_w:
        n = w.shape[1]
        shapes += [sd((n, 3 * QW), f32), sd((n, PK), f32)]
        scratch += [like(m) for m in more] + [vm((4, n, PK), bf), vm((3, n, PK), bf),
                    vm((4, 2, n, 3 * QW), bf), vm((4, n, 3 * QW), bf), vm((4, n, 3 * QW), bf), vm((3, n, 3 * QW), bf),
                    vm((8, QW), f32), vm((4, 8, QW), f32), vm((8, QW), f32)]
        sems += [dma((2,)), dma((2,)), dma((3, 3)), dma((3, 3))]
    else:
        shapes += [sd((D, 3 * QW), bf)]
    return pl.pallas_call(
        functools.partial(final_kernel, with_w),
        out_shape=shapes,
        in_specs=[HB] * len(args), out_specs=[VM] * len(shapes),
        scratch_shapes=scratch + sems,
        compiler_params=pltpu.CompilerParams(
            collective_id=1, has_side_effects=True, vmem_limit_bytes=60 << 20),
        name="final",
    )(*args)


def emit_kernel(*refs):
    sources, outs, kept, sem = refs[:5], refs[5:16], refs[16:21], refs[21]
    loads = [pltpu.make_async_copy(a, b, sem.at[n]) for n, (a, b) in enumerate(zip(sources, kept))]
    for c in loads:
        c.start()
    input_grad, qkv_o, pair_o, out_o, out_b, inner_o, inner_b, outer_o, outer_b, gain_o, shift_o = outs
    save = pltpu.make_async_copy(kept[0], input_grad, sem.at[5])
    loads[0].wait()
    save.start()
    for c in loads[1:]:
        c.wait()
    pair, qkv, share, sums = kept[1:]
    for c in range(3):
        qkv_o[c] = qkv[:, c * QW:(c + 1) * QW]
    pair_o[...] = pair[0:2]
    inner_o[...] = share[:, 0:FQ]
    outer_o[...] = share[:, OU:]
    out_o[...] = share[:, AT:OU].T[:QW]
    out_b[...] = sums[5]
    inner_b[...] = sums[6 + lax.axis_index("tensor")]
    outer_b[...] = sums[2]
    gain_o[...] = jnp.concatenate([sums[3:4], sums[0:1]], 0)
    shift_o[...] = jnp.concatenate([sums[4:5], sums[1:2]], 0)
    save.wait()


def emit(*arrays):
    sd = jax.ShapeDtypeStruct
    n = arrays[3].shape[0]
    rows = sd((ROWS, D), bf)
    vec = sd((D,), f32)
    shapes = (rows, sd((3, n, QW), f32), sd((2, QW), f32), sd((QW, n), f32), vec, sd((n, FQ), f32), vec,
              sd((n, FQ), f32), vec, sd((2, D), f32), sd((2, D), f32))
    return pl.pallas_call(
        emit_kernel, out_shape=shapes, in_specs=[HB] * 5, out_specs=(HB,) + (VM,) * 10,
        scratch_shapes=[pltpu.VMEM(a.shape, a.dtype) for a in arrays] + [pltpu.SemaphoreType.DMA((6,))],
        compiler_params=pltpu.CompilerParams(vmem_limit_bytes=60 << 20),
        name="emit",
    )(*arrays)


def add_low(a, b):
    return (a.astype(f32) + b.astype(f32)).astype(bf)


def on_device(
    ring, input_rows, time_embed, parents, qkv_weight, qv_bias, out_weight, out_bias, inner_weight,
    inner_bias, outer_weight, outer_bias, norm_gain, norm_shift, cotangent,
):
    rank = lax.axis_index("tensor")
    dpos = lax.axis_index("dp")
    part = qkv_weight.shape[0]
    own_ring = ring == 8

    if own_ring:
        whole, w_all, gz, half = gather_start(
            input_rows, time_embed, jnp.transpose(qkv_weight, (1, 0, 2)), inner_weight, outer_weight.T, out_weight,
            inner_bias)
        diagonal = [(i * 4 + j, (i ^ 1) * 4 + (j ^ 2)) for i in range(8) for j in range(4)]
        cross = lambda a: lax.ppermute(a, ("dp", "tensor"), diagonal)
        weights = [gz, across_x(gz), partner(gz, 2), cross(half)]
    else:
        whole = gather_start(input_rows, time_embed)[0]
        w_all = lax.all_gather(qkv_weight.reshape(part, 3 * QW), "dp", axis=0, tiled=True).reshape(8, 96, 3 * QW)
        bias_part = lax.dynamic_slice_in_dim(inner_bias, dpos * part, part, 0)
        packed = jnp.concatenate([inner_weight, out_weight.T, bias_part[:, None],
                                  jnp.zeros((part, OU - AT - QW - 1), bf), outer_weight.T], axis=1)
        packed = lax.all_gather(packed, "dp", axis=0, tiled=True)
        weights = [lax.all_gather(packed, "tensor", axis=0, tiled=False).reshape(4, 4, 2, 96, PK)]

    qt, kv, kt, ot, mix, lse, pairs = attn_fwd(parents, whole, w_all, qv_bias)
    block_out, grad1, dots, *parts, sums = middle(
        weights, mix, input_rows, time_embed, cotangent, out_bias, outer_bias, norm_gain, norm_shift)
    if own_ring:
        parts = [parts[0], across_x(parts[1]), partner(parts[2], 2), cross(parts[3])]
    else:
        far = [partner(parts[2], 2), partner(parts[3], 2)]
    dqt, dkv, block_out = attn_bwd((0, 1, 2), pairs, qt, kv, kt, dots, ot, lse, block_out)
    if own_ring:
        input_grad, pair, qkv_share, share = final(whole, w_all, dqt, dkv, grad1, *parts)
        (input_grad, qkv_share, pair, out_share, out_sum, inner_share, inner_sum, outer_share, outer_sum,
         gains, shifts) = emit(input_grad, pair, qkv_share, share, sums)
        return (block_out, input_grad, jnp.transpose(qkv_share, (1, 0, 2)), pair, out_share, out_sum,
                inner_share, inner_sum, outer_share.T, outer_sum, gains, shifts)
    else:
        input_grad, pair, dwq = final(whole, w_all, dqt, dkv, grad1)
        own, other = add_low(parts[0], far[0]), add_low(parts[1], far[1])
        even = dpos % 2 == 0
        mine = jnp.stack([jnp.where(even, own, other), jnp.where(even, other, own)], axis=1).reshape(D, PK)
        share = lax.psum_scatter(mine, "dp", scatter_dimension=0, tiled=True).astype(f32)
        qkv_share = lax.psum_scatter(dwq, "dp", scatter_dimension=0, tiled=True).astype(f32).reshape(part, 3, QW)
        pair = lax.psum(pair, "dp")
        sums = jnp.sum(lax.all_gather(sums, ("dp", "tensor"), axis=0, tiled=False), axis=0)
    return (
        block_out,
        input_grad,
        qkv_share,
        pair[:2],
        share[:, AT:AT + QW].T,
        sums[5],
        share[:, :FQ],
        lax.dynamic_index_in_dim(sums[6:10], rank, 0, keepdims=False),
        share[:, OU:].T,
        sums[2],
        jnp.stack([sums[3], sums[0]]),
        jnp.stack([sums[4], sums[1]]),
    )


def solution(mesh):
    both = P(("dp", "tensor"), None)
    return jax.shard_map(
        functools.partial(on_device, mesh.shape["dp"]),
        mesh=mesh,
        in_specs=(
            both, P("dp", None), P("dp", None), P("dp", None, "tensor"), P(None, "tensor"),
            P("tensor", "dp"), P(), P("dp", "tensor"), P("tensor"), P("tensor", "dp"), P(), P(), P(), both,
        ),
        out_specs=(
            both, both, P("dp", None, "tensor"), P(None, "tensor"), P("tensor", "dp"), P(),
            P("dp", "tensor"), P("tensor"), P("tensor", "dp"), P(), P(), P(),
        ),
        check_vma=False,
    )
```

```python
import functools
import jax, jax.numpy as jnp
from jax import lax
from jax.experimental import pallas as pl
from jax.experimental.pallas import tpu as pltpu
from jax.sharding import PartitionSpec as P
bf = jnp.bfloat16
f32 = jnp.float32
BLK = 256
TRUNK = 1024
NB = 16
HD = 64
HN = 3
SEGS = 13
PAD = 4
LIST = 192
TQ = 512
TK = 1024
FP = 4
BP = 4
BTQ = 1024
BTK = 256
FQT = 1024
FKT = 512
VM = pl.BlockSpec(memory_space=pltpu.VMEM)
SM = pl.BlockSpec(memory_space=pltpu.SMEM)
HB = pl.BlockSpec(memory_space=pltpu.HBM)
NT = (((1,), (1,)), ((), ()))


def mm(a, b, dims=(((1,), (0,)), ((), ()))):
    return lax.dot_general(a, b, dims, preferred_element_type=f32)


def aligned(i, n):
    return pl.ds(pl.multiple_of(i * n, n), n)


def list_pairs(parents, cur, pairs):
    for s in range(1, SEGS):
        cur[s] = jnp.int32(s)

    def level(_, n):
        for s in range(1, SEGS):
            c = cur[s]
            pairs[0, n] = jnp.int32(s + 3)
            pairs[1, n] = c + 3
            cur[s] = jnp.where(c > 0, parents[0, c], 0)
            n = n + jnp.where(c > 0, 1, 0)
        return n

    n = lax.fori_loop(0, SEGS - 1, level, jnp.int32(0))
    for i in range(PAD - 1):
        pairs[0, n + i] = jnp.int32(NB)
        pairs[1, n + i] = jnp.int32(NB)
    pairs[2, 0] = (n + PAD - 1) // PAD * PAD


PR = 1024


def fwd_kernel(parents, x_hbm, w_hbm, b_ref, qt_hbm, kv_hbm, kt_hbm, o_hbm, mix_hbm, lse_ref, pairs,
               cur, m_s, acc_s, xs, w_s, wt_s, wr_s, br_s, qt_ref, kv_ref, kt_ref, vt_ref, o_ref, mix_ref, sem):
    def fetch(i, slot):
        return pltpu.make_async_copy(x_hbm.at[i], xs.at[slot], sem.at[slot])

    load_w = pltpu.make_async_copy(w_hbm, w_s, sem.at[2])
    load_w.start()
    fetch(0, 0).start()
    list_pairs(parents, cur, pairs)
    load_w.wait()
    bias = b_ref[...].astype(f32)
    bias = jnp.concatenate([bias[0:1], bias[1:2]], 1)
    w = w_s[...].reshape(w_s.shape[0] * w_s.shape[1], w_s.shape[2])
    wt_s[...] = w[:, :HN * HD].T
    for h in range(HN):
        for c in (1, 2):
            to = slice(h * 128 + (c - 1) * HD, h * 128 + c * HD)
            wr_s[:, to] = w[:, c * HN * HD + h * HD:c * HN * HD + (h + 1) * HD]
            part = bias[:, HN * HD + h * HD:HN * HD + (h + 1) * HD] if c == 2 else jnp.zeros((1, HD), f32)
            br_s[:, to] = jnp.broadcast_to(part, (8, HD))
    bias_col = jnp.transpose(jnp.broadcast_to(bias[:, :HN * HD], (8, HN * HD)))
    ones = (lax.broadcasted_iota(jnp.int32, (16, PR), 0) == 0).astype(f32).astype(bf)

    def rows(i, _):
        slot = lax.rem(i, 2)

        @pl.when(i + 1 < NB * BLK // PR)
        def _():
            fetch(i + 1, 1 - slot).start()

        fetch(i, slot).wait()
        cols = aligned(i, PR)
        x = xs[slot]
        kv = (mm(x, wr_s[...]) + br_s[0:1]).astype(bf)
        kv_ref[cols] = kv
        q = (mm(wt_s[...], x, NT) + bias_col[:, 0:1]).astype(bf)
        qt_ref[:, cols] = (q.astype(f32) * 0.125).astype(bf)
        turned = kv.T
        for h in range(HN):
            kt_ref[h * HD:(h + 1) * HD, cols] = turned[h * 128:h * 128 + HD]
            vt_ref[h, :HD, cols] = turned[h * 128 + HD:(h + 1) * 128]
            vt_ref[h, HD:, cols] = ones
        return 0

    lax.fori_loop(0, NB * BLK // PR, rows, 0)
    saves = [pltpu.make_async_copy(a, b, sem.at[3 + n])
             for n, (a, b) in enumerate(((qt_ref, qt_hbm), (kv_ref, kv_hbm), (kt_ref, kt_hbm)))]
    for c in saves:
        c.start()
    zero = jnp.zeros((HD, TQ), bf)

    square = lambda ref, h, cols: jnp.sum(jnp.square(ref[h * HD:(h + 1) * HD, cols].astype(f32)), axis=0, keepdims=True)

    def norms(i, best):
        cols = aligned(i, BLK)
        for h in range(HN):
            m_s[i, h:h + 1] = square(qt_ref, h, cols)
        return tuple(jnp.maximum(best[h], square(kt_ref, h, cols)) for h in range(HN))

    best = lax.fori_loop(0, NB, norms, tuple(jnp.zeros((1, BLK), f32) for h in range(HN)))
    most = [jnp.max(x, axis=1, keepdims=True) for x in best]

    def bounds(i, _):
        for h in range(HN):
            m_s[i, h:h + 1] = jnp.sqrt(m_s[i, h:h + 1] * most[h]) * 1.001
        return 0

    lax.fori_loop(0, NB, bounds, 0)
    m_s[NB] = jnp.zeros((8, BLK), f32)
    wide_zero = jnp.zeros((HD, FQT), bf)

    def fast_tile(i, _):
        per = FQT // BLK
        qz = [jnp.concatenate([qt_ref[h * HD:(h + 1) * HD, aligned(i, FQT)], wide_zero], 0) for h in range(HN)]
        m = [jnp.concatenate([m_s[i * per + j, h:h + 1] for j in range(per)], 1) for h in range(HN)]
        acc = [None] * HN
        for c in range(TRUNK // FKT):
            ks = slice(c * FKT, (c + 1) * FKT)
            p = [jnp.exp(mm(kv_ref[ks, h * 128:(h + 1) * 128], qz[h]) - m[h]).astype(bf) for h in range(HN)]
            a = [mm(vt_ref[h, :, ks], p[h]) for h in range(HN)]
            acc = [x + y for x, y in zip(acc, a)] if c else a
        for h in range(HN):
            for j in range(per):
                acc_s[i * per + j, h] = acc[h][:, j * BLK:(j + 1) * BLK]
        return 0

    lax.fori_loop(0, NB * BLK // FQT, fast_tile, 0)

    def pick(g, count):
        work = []
        for p in range(count):
            q, kb = pairs[0, g * count + p], jnp.minimum(pairs[1, g * count + p], NB - 1)
            work += [(q, aligned(jnp.minimum(q, NB - 1), BLK), aligned(kb, BLK), h) for h in range(HN)]
        return work

    def scores(work):
        return [mm(kv_ref[ks, h * 128:(h + 1) * 128],
                   jnp.concatenate([qt_ref[h * HD:(h + 1) * HD, qs], zero[:, :BLK]], 0)) for q, qs, ks, h in work]

    def fast_step(g, _):
        work = pick(g, FP)
        p = [jnp.exp(x - m_s[q, h:h + 1]).astype(bf) for x, (q, qs, ks, h) in zip(scores(work), work)]
        a = [mm(vt_ref[h, :, ks], x) for x, (q, qs, ks, h) in zip(p, work)]
        for y, (q, qs, ks, h) in zip(a, work):
            acc_s[q, h] += y
        return 0

    lax.fori_loop(0, pairs[2, 0] // FP, fast_step, 0)

    def small(i, bad):
        for h in range(HN):
            bad = jnp.where(acc_s[i, h, HD:HD + 1, :] > 1e-18, bad, 1.0)
        return bad

    bad = jnp.max(lax.fori_loop(0, NB, small, jnp.zeros((1, BLK), f32)))

    @pl.when(bad > 0)
    def _():
        def tile(i, _):
            qz = [jnp.concatenate([qt_ref[h * HD:(h + 1) * HD, aligned(i, TQ)], zero], 0) for h in range(HN)]
            m, acc = [None] * HN, [None] * HN
            for c in range(TRUNK // TK):
                ks = slice(c * TK, (c + 1) * TK)
                s = [mm(kv_ref[ks, h * 128:(h + 1) * 128], qz[h]) for h in range(HN)]
                new = [jnp.max(x, axis=0, keepdims=True) for x in s]
                if c:
                    new = [jnp.maximum(x, y) for x, y in zip(m, new)]
                p = [jnp.exp(x - y).astype(bf) for x, y in zip(s, new)]
                a = [mm(vt_ref[h, :, ks], p[h]) for h in range(HN)]
                if c:
                    a = [x * jnp.exp(y - z) + w for x, y, z, w in zip(acc, m, new, a)]
                m, acc = new, a
            for h in range(HN):
                for j in range(TQ // BLK):
                    acc_s[i * (TQ // BLK) + j, h] = acc[h][:, j * BLK:(j + 1) * BLK]
                    m_s[i * (TQ // BLK) + j, h:h + 1] = m[h][:, j * BLK:(j + 1) * BLK]
            return 0

        lax.fori_loop(0, NB * BLK // TQ, tile, 0)

        def step(g, _):
            work = pick(g, 1)
            s = scores(work)
            m = [m_s[q, h:h + 1] for q, qs, ks, h in work]
            new = [jnp.maximum(y, jnp.max(x, axis=0, keepdims=True)) for x, y in zip(s, m)]
            p = [jnp.exp(x - y).astype(bf) for x, y in zip(s, new)]
            a = [mm(vt_ref[h, :, ks], x) for x, (q, qs, ks, h) in zip(p, work)]
            a = [acc_s[q, h] * jnp.exp(x - y) + z for x, y, z, (q, qs, ks, h) in zip(m, new, a, work)]
            for x, y, (q, qs, ks, h) in zip(new, a, work):
                m_s[q, h:h + 1] = x
                acc_s[q, h] = y
            return 0

        lax.fori_loop(0, pairs[2, 0], step, 0)

    rank = lax.axis_index("tensor")

    def finish(i, _):
        qs = aligned(i, BLK)
        slot = jnp.bitwise_xor(rank, i // 4)
        for h in range(HN):
            total = acc_s[i, h, HD:HD + 1, :]
            out = acc_s[i, h, 0:HD, :] / total
            o_ref[h * HD:(h + 1) * HD, qs] = out
            mix_ref[slot, h * HD:(h + 1) * HD, aligned(lax.rem(i, 4), BLK)] = out.astype(bf)
            lse_ref[h:h + 1, qs] = m_s[i, h:h + 1] + jnp.log(total)
        return 0

    lax.fori_loop(0, NB, finish, 0)
    saves += [pltpu.make_async_copy(mix_ref, mix_hbm, sem.at[6]), pltpu.make_async_copy(o_ref, o_hbm, sem.at[7])]
    for c in saves[3:]:
        c.start()
    for c in saves:
        c.wait()


def attn_fwd(parents, whole, w, bias):
    S = NB * BLK
    sd = jax.ShapeDtypeStruct
    vm = pltpu.VMEM
    n = HN * HD
    d = whole.shape[2]
    return pl.pallas_call(
        fwd_kernel,
        out_shape=(sd((n, S), bf), sd((S, 2 * n), bf), sd((n, S), bf), sd((n, S), f32), sd((4, n, S // 4), bf),
                   sd((8, S), f32), sd((3, LIST), jnp.int32)),
        in_specs=[SM, HB, HB, VM], out_specs=(HB,) * 5 + (VM, SM),
        scratch_shapes=[pltpu.SMEM((16,), jnp.int32), vm((NB + 1, 8, BLK), f32), vm((NB + 1, HN, 80, BLK), f32),
                        vm((2, PR, d), bf), vm(w.shape, bf), vm((n, d), bf), vm((d, 2 * n), bf), vm((8, 2 * n), f32),
                        vm((n, S), bf), vm((S, 2 * n), bf), vm((n, S), bf), vm((HN, 80, S), bf),
                        vm((n, S), f32), vm((4, n, S // 4), bf), pltpu.SemaphoreType.DMA((8,))],
        compiler_params=pltpu.CompilerParams(vmem_limit_bytes=63 << 20),
        cost_estimate=pl.CostEstimate(flops=40_000_000_000, bytes_accessed=12_000_000, transcendentals=18_000_000),
        name="tree_attention",
    )(parents, whole, w, bias)


def bwd_kernel(heads, pairs, qt_hbm, kv_hbm, kt_hbm, dots_hbm, o_hbm, lse_ref, rows_in, dqt_hbm, dkv_hbm, rows_out,
               rows_s, dkv_s, dq_s, st_s, dot_ref, qt_ref, kv_ref, kt_ref, dots, o_ref, dqt_ref, dkv_ref, sem):
    loads = [pltpu.make_async_copy(a, b, sem.at[n]) for n, (a, b) in enumerate((
        (dots_hbm, dots), (o_hbm, o_ref), (qt_hbm, qt_ref), (kv_hbm, kv_ref), (kt_hbm, kt_ref)))]
    for c in loads:
        c.start()
    through = [pltpu.make_async_copy(rows_in, rows_s, sem.at[7]), pltpu.make_async_copy(rows_s, rows_out, sem.at[8])]
    through[0].start()
    dkv_s[...] = jnp.zeros_like(dkv_s)
    dq_s[...] = jnp.zeros_like(dq_s)
    rank = lax.axis_index("tensor")
    loads[0].wait()
    for m in range(4):
        dot_ref[:, aligned(jnp.bitwise_xor(rank, m), NB * BLK // 4)] = dots[m]
    loads[1].wait()

    def stats(i, _):
        qs = aligned(i, BLK)
        for n, h in enumerate(heads):
            rows = slice(h * HD, (h + 1) * HD)
            st_s[i, n:n + 1] = jnp.sum(dot_ref[rows, qs].astype(f32) * o_ref[rows, qs], axis=0, keepdims=True)
            st_s[i, 4 + n:5 + n] = lse_ref[h:h + 1, qs]
        return 0

    lax.fori_loop(0, NB, stats, 0)
    for c in loads[2:]:
        c.wait()
    through[0].wait()
    through[1].start()

    def chains(work, width):
        zero = jnp.zeros((HD, width), bf)
        rows = lambda h: slice(h * HD, (h + 1) * HD)
        qz = [jnp.concatenate([qt_ref[rows(h), qs], zero], 0) for h, qs, ks, lse, delta in work]
        dz = [jnp.concatenate([zero, dot_ref[rows(h), qs]], 0) for h, qs, ks, lse, delta in work]
        kv = [kv_ref[ks, h * 128:(h + 1) * 128] for h, qs, ks, lse, delta in work]
        p = [jnp.exp(mm(x, y) - w[3]) for x, y, w in zip(kv, qz, work)]
        ds = [(x * (mm(y, z) - w[4])).astype(bf) for x, y, z, w in zip(p, kv, dz, work)]
        g = [mm(jnp.concatenate([x, y.astype(bf)], 1), jnp.concatenate([z, u], 1), NT)
             for x, y, z, u in zip(ds, p, qz, dz)]
        return g, [mm(kt_ref[rows(h), ks], x) for x, (h, qs, ks, lse, delta) in zip(ds, work)]

    per = BTQ // BLK

    def tile(i, _):
        row = lambda k: jnp.concatenate([st_s[i * per + j, k:k + 1] for j in range(per)], 1)
        dq = [None] * len(heads)
        for c in range(TRUNK // BTK):
            ks = slice(c * BTK, (c + 1) * BTK)
            g, d = chains([(h, aligned(i, BTQ), ks, row(4 + n), row(n)) for n, h in enumerate(heads)], BTQ)
            for n in range(len(heads)):
                dkv_s[ks, n * 128:(n + 1) * 128] += g[n]
                dq[n] = d[n] if c == 0 else dq[n] + d[n]
        for n in range(len(heads)):
            for j in range(per):
                dq_s[i * per + j, n] += dq[n][:, j * BLK:(j + 1) * BLK]
        return 0

    lax.fori_loop(0, NB * BLK // BTQ, tile, 0)

    def step(s, _):
        work, where = [], []
        for p in range(BP):
            q, kb = pairs[0, s * BP + p], pairs[1, s * BP + p]
            qr = jnp.minimum(q, NB - 1)
            for n, h in enumerate(heads):
                work.append((h, aligned(qr, BLK), aligned(jnp.minimum(kb, NB - 1), BLK),
                             st_s[qr, 4 + n:5 + n], st_s[qr, n:n + 1]))
                where.append((q, kb, n))
        for g, d, (q, kb, n) in zip(*chains(work, BLK), where):
            dkv_s[aligned(kb, BLK), n * 128:(n + 1) * 128] += g
            dq_s[q, n] += d
        return 0

    lax.fori_loop(0, pairs[2, 0] // BP, step, 0)

    def finish(i, _):
        for n in range(len(heads)):
            dqt_ref[n * HD:(n + 1) * HD, aligned(i, BLK)] = (dq_s[i, n] * 0.125).astype(bf)
        dkv_ref[aligned(i, BLK)] = dkv_s[aligned(i, BLK)].astype(bf)
        save(i).start()
        return 0

    def save(i):
        return pltpu.make_async_copy(dkv_ref.at[aligned(i, BLK)], dkv_hbm.at[aligned(i, BLK)], sem.at[9 + i])

    lax.fori_loop(0, NB, finish, 0)
    last = pltpu.make_async_copy(dqt_ref, dqt_hbm, sem.at[5])
    last.start()
    for i in range(NB):
        save(i).wait()
    last.wait()
    through[1].wait()


def attn_bwd(heads, pairs, qt, kv, kt, dots, o, lse, rows):
    S = qt.shape[1]
    sd = jax.ShapeDtypeStruct
    n = len(heads)
    return pl.pallas_call(
        functools.partial(bwd_kernel, heads),
        out_shape=(sd((n * HD, S), bf), sd((S, n * 128), bf), sd(rows.shape, rows.dtype)),
        in_specs=[SM] + [HB] * 5 + [VM, HB], out_specs=(HB, HB, HB),
        scratch_shapes=[pltpu.VMEM(rows.shape, rows.dtype), pltpu.VMEM((S + BLK, n * 128), f32), pltpu.VMEM((NB + 1, n, HD, BLK), f32),
                        pltpu.VMEM((NB, 8, BLK), f32), pltpu.VMEM((HN * HD, S), bf)]
        + [pltpu.VMEM(a.shape, a.dtype) for a in (qt, kv, kt, dots, o)]
        + [pltpu.VMEM((n * HD, S), bf), pltpu.VMEM((S, n * 128), bf), pltpu.SemaphoreType.DMA((9 + NB,))],
        compiler_params=pltpu.CompilerParams(vmem_limit_bytes=63 << 20),
        cost_estimate=pl.CostEstimate(flops=20_000_000_000 * n, bytes_accessed=8_000_000 * n, transcendentals=6_000_000 * n),
        name="tree_attention_grad",
    )(pairs, qt, kv, kt, dots, o, lse, rows)


D = 768
SEQ = 4096
ROWS = SEQ // 4
QW = HN * HD
FQ = 768
AT = FQ
OU = FQ + 256
PK = OU + FQ
MESH = pl.DeviceIdType.MESH
HBM = pl.BlockSpec(memory_space=pl.ANY)
TN = (((0,), (0,)), ((), ()))
epsilon = 1e-05
root_half = 0.7071067811865476
inv_root_tau = 0.3989422804014327


def layer_norm(summed, gain_row, shift_row):
    centre = jnp.mean(summed, axis=-1, keepdims=True)
    offset = summed - centre
    inv_std = lax.rsqrt(jnp.mean(offset * offset, axis=-1, keepdims=True) + epsilon)
    normed = offset * inv_std
    return normed * gain_row + shift_row, normed, inv_std


def norm_back(grad_out, normed, inv_std, gain_row):
    scaled = grad_out * gain_row
    return inv_std * (
        scaled
        - jnp.mean(scaled, axis=-1, keepdims=True)
        - normed * jnp.mean(scaled * normed, axis=-1, keepdims=True)
    )


def gelu_parts(u):
    half = 0.5 * (1.0 + lax.erf(u * root_half))
    return u * half, half + u * inv_root_tau * jnp.exp(-0.5 * u * u)


def partner(x, mask):
    return lax.ppermute(x, "tensor", [(i, i ^ mask) for i in range(4)])


def across_x(x):
    return lax.ppermute(x, "dp", [(i, i ^ 1) for i in range(8)])


def flip1(r):
    return r + 1 - 2 * lax.rem(r, 2)


CH = 4
CROWS = ROWS // CH
GH = 8
GROWS = ROWS // GH


def remote(src, dst, s, q, dev):
    return pltpu.make_async_remote_copy(
        src_ref=src, dst_ref=dst, send_sem=s, recv_sem=q, device_id=dev, device_id_type=MESH)


def meet(targets, meanwhile=None):
    barrier = pltpu.get_barrier_semaphore()
    for t in targets:
        pl.semaphore_signal(barrier, inc=1, device_id=t, device_id_type=MESH)
    if meanwhile is not None:
        meanwhile()
    pl.semaphore_wait(barrier, len(targets))


class Sends:
    def __init__(self):
        self.started = []

    def go(self, *args):
        c = remote(*args)
        c.start()
        self.started.append(c)
        return c

    def drain(self):
        for c in self.started:
            c.wait_send()


def gather_kernel(with_w, *refs):
    if with_w:
        (inp, te, wq, w1, w2, w3, bias, whole_hbm, wqg_hbm, gz_hbm, gl_hbm, whole, wqg, gz, bcol,
         ysend, yrecv, csend, crecv, out, zsend, zrecv, xsend, xrecv) = refs
    else:
        inp, te, whole_hbm, whole, ysend, yrecv, csend, crecv, out = refs
    r = lax.axis_index("tensor")
    d = lax.axis_index("dp")
    rc, ry = flip1(r), lax.rem(r + 2, 4)
    core, yy = {"tensor": rc}, {"tensor": ry}
    targets = [core, yy]
    if with_w:
        z, x = d // 2, lax.rem(d, 2)
        xx = {"dp": flip1(d)}
        up, down = {"dp": lax.rem(z + 1, 4) * 2 + x}, {"dp": lax.rem(z + 3, 4) * 2 + x}
        targets += [xx, up, down]

    def prepare():
        shift = te[...].astype(f32)
        whole[r] = (inp[...].astype(f32) + shift).astype(bf)
        if with_w:
            for c in range(3):
                wqg[d, :, c * QW:(c + 1) * QW] = wq[c]

    meet(targets, prepare)
    sends = Sends()
    if with_w:

        def line(a, s, slot, way):
            ref = wqg.at[slot * 2 + x] if a == 0 else gz.at[slot]
            k = 2 * (s - 1) + way
            return remote(ref, ref, zsend.at[a, k], zrecv.at[a, k], (up, down)[way])

        def side(i, slot):
            ref = wqg.at[slot * 2 + x]
            return remote(ref, ref, xsend.at[i], xrecv.at[i], xx)

        def can_send(s, way):
            return jnp.logical_and(z < 3, z - s + 1 >= 0) if way == 0 else jnp.logical_and(z > 0, z + s - 1 <= 3)

        def can_recv(s, way):
            return z - s >= 0 if way == 0 else z + s <= 3

        def own(a):
            for way in (0, 1):
                @pl.when(can_send(1, way))
                def _():
                    line(a, 1, z, way).start()

        own(0)
        side(0, z).start()
    rows = [pl.ds(i * GROWS, GROWS) for i in range(GH)]
    yc = []
    for i in range(GH):
        mine = whole.at[r, rows[i]]
        yc.append(sends.go(mine, mine, ysend.at[i], yrecv.at[i], yy))
    c0 = sends.go(whole.at[r], whole.at[r], csend.at[GH], crecv.at[GH], core)
    if with_w:
        part = wqg.shape[1]
        gz[z, :, 0:FQ] = w1[...]
        gz[z, :, OU:] = w2[...]
        bcol[...] = jnp.transpose(jnp.broadcast_to(bias[...].astype(f32).reshape(1, D), (8, D)))
        fill = OU - AT - QW
        column = bcol[pl.ds(pl.multiple_of(d * part, 32), part), 0:1]
        column = jnp.where(lax.broadcasted_iota(jnp.int32, (part, fill), 1) == 0, column, 0.0)
        gz[z, :, AT:OU] = jnp.concatenate([w3[...].astype(f32).T, column], 1).astype(bf)
        own(1)
        for s in (1, 2, 3):
            for way in (0, 1):
                slot = z - s if way == 0 else z + s

                @pl.when(can_recv(s, way))
                def _():
                    for a in (0, 1):
                        line(a, s, slot, way).wait_recv()
                        if s < 3:
                            @pl.when(can_send(s + 1, way))
                            def _():
                                line(a, s + 1, slot, way).start()
                        if a == 0:
                            side(slot_sem(s, way), slot).start()
    keeps = []

    def keep(src, dst):
        c = pltpu.make_async_copy(src, dst, out.at[len(keeps)])
        c.start()
        keeps.append(c)

    keep(whole.at[r], whole_hbm.at[r])
    cc = []
    for i in range(GH):
        yc[i].wait_recv()
        part = whole.at[ry, rows[i]]
        cc.append(sends.go(part, part, csend.at[i], crecv.at[i], core))
    keep(whole.at[ry], whole_hbm.at[ry])
    c0.wait_recv()
    keep(whole.at[rc], whole_hbm.at[rc])
    for c in cc:
        c.wait_recv()
    rd = 3 - r
    keep(whole.at[rd], whole_hbm.at[rd])
    if with_w:
        keep(gz, gz_hbm)
        keep(gz.at[pl.ds(0, 2), :, pl.ds(0, OU)], gl_hbm)
        side(0, z).wait()
        for s in (1, 2, 3):
            for way in (0, 1):
                slot = z - s if way == 0 else z + s

                @pl.when(can_recv(s, way))
                def _():
                    side(slot_sem(s, way), slot).wait()

                @pl.when(can_send(s, way))
                def _():
                    for a in (0, 1):
                        line(a, s, slot_of_send(z, s, way), way).wait_send()
        keep(wqg, wqg_hbm)
    for c in keeps:
        c.wait()
    sends.drain()


def slot_of_send(z, s, way):
    return z - s + 1 if way == 0 else z + s - 1


def slot_sem(s, way):
    return 2 * s - 1 + way


def gather_start(inp, te, *weights):
    with_w = len(weights) > 0
    dma = pltpu.SemaphoreType.DMA
    shapes = [jax.ShapeDtypeStruct((4, ROWS, D), bf)]
    args = [inp, te, *weights]
    scratch = []
    sems = [dma((GH,)), dma((GH,)), dma((GH + 1,)), dma((GH + 1,)), dma((8,))]
    if with_w:
        part = weights[0].shape[1]
        line = jax.ShapeDtypeStruct((4, part, PK), bf)
        shapes += [jax.ShapeDtypeStruct((8, part, 3 * QW), bf), line, jax.ShapeDtypeStruct((2, part, OU), bf)]
        scratch = [pltpu.VMEM((D, 8), f32)]
        sems += [dma((2, 6)), dma((2, 6)), dma((7,)), dma((7,))]
    return pl.pallas_call(
        functools.partial(gather_kernel, with_w),
        out_shape=shapes, in_specs=[VM] * len(args), out_specs=[HB] * len(shapes),
        scratch_shapes=[pltpu.VMEM(a.shape, bf) for a in shapes[:3]] + scratch + sems,
        compiler_params=pltpu.CompilerParams(collective_id=0, has_side_effects=True, vmem_limit_bytes=60 << 20),
        name="gather_start",
    )(*args)


RB = 512
NR = ROWS // RB


def middle_kernel(with_w, *refs):
    if with_w:
        wa, wb, wc, wd = refs[:4]
        step, line_s, xsend, xrecv, wsend, wrecv, ssend, srecv = refs[-8:]
        refs = refs[4:-8]
    else:
        wfull, refs = refs[0], refs[1:]
    (mix_hbm, inp_hbm, te, cot_hbm, ob, fb, ng, ns, block_hbm, grad1_hbm, dots_hbm, p00, p01, p10, p11, sums_o,
     inp, cot, block_out, grad1_o, w, wt_s, mix, mixr, gmix, dots, both, ht, gmt, gat, act, gp, slope_s,
     loc, asend, arecv, bsend, brecv, gsend, grecv) = refs
    r = lax.axis_index("tensor")
    d = lax.axis_index("dp")
    x = lax.rem(d, 2)
    ranks = [r, flip1(r), lax.rem(r + 2, 4), 3 - r]
    devices = [{"tensor": k} for k in ranks]
    xx = {"dp": flip1(d)}
    load = pltpu.make_async_copy(mix_hbm, mix, loc.at[5])
    load.start()
    rows_in = [pltpu.make_async_copy(inp_hbm, inp, loc.at[19]), pltpu.make_async_copy(cot_hbm, cot, loc.at[20])]
    for c in rows_in:
        c.start()
    if with_w:
        z = d // 2
        zdev = [{"dp": lax.rem(z + k, 4) * 2 + x} for k in range(4)]
        meet(devices[1:] + [xx] + zdev[1:])
    else:
        meet(devices[1:])
    sends = Sends()
    core = devices[1]
    load.wait()

    def heads_in(b, m):
        cols = pl.ds(b * RB, RB)
        k = lax.axis_index("tensor")
        peer = {"tensor": (k, flip1(k), lax.rem(k + 2, 4), 3 - k)[m]}
        return remote(mix.at[m, :, cols], mixr.at[m, :, cols], asend.at[b, m], arecv.at[b, m], peer)

    def heads_out(b, m):
        cols = aligned(b, RB)
        return remote(gmix.at[m, :, cols], dots.at[m, :, cols], bsend.at[b, m], brecv.at[b, m], devices[m])

    heads = [[heads_in(b, m) for m in (3, 2, 1)] for b in range(NR)]
    for c in heads[0]:
        c.start()
    fill = pltpu.make_async_copy(mix.at[0], mixr.at[0], loc.at[0])
    fill.start()

    def weight_moves(j, relay, hand, place):
        rank, side = lax.axis_index("tensor"), lax.rem(lax.axis_index("dp"), 2)
        span = (pl.ds(0, OU), pl.ds(OU, FQ))[j]
        other = lax.rem(rank + 2, 4)
        four, two, end = pl.ds(0, 4), pl.ds(0, 2), pl.ds(2, 2)
        near = {"tensor": flip1(rank)}
        if relay is not None:
            relay(remote(wc.at[end, :, span], w.at[other, end, side, :, span], xsend.at[j], xrecv.at[j],
                         {"dp": flip1(lax.axis_index("dp"))}))
            if j:
                relay(remote(wb.at[two, :, span], w.at[rank, two, 1 - side, :, span], xsend.at[2], xrecv.at[2],
                             {"tensor": other}))
        pieces = ((wa, rank, four, side), (wb, rank, four, 1 - side), (wc, other, four, side), (wd, other, two, 1 - side))
        for i, (ref, t, zz, at) in enumerate(pieces[:4 - j]):
            src, dst = ref.at[:, :, span], w.at[t, zz, at, :, span]
            if hand is not None:
                hand(remote(src, dst, wsend.at[j, i], wrecv.at[j, i], near))
            if place is not None:
                place(pltpu.make_async_copy(src, dst, loc.at[11 + 4 * j + i]))

    def whole_fill(j):
        span = (pl.ds(0, OU), pl.ds(OU, FQ))[j]
        return pltpu.make_async_copy(wfull.at[:, :, :, :, span], w.at[:, :, :, :, span], loc.at[1 + j])

    def weight_tail(j):
        rank, side = lax.axis_index("tensor"), lax.rem(lax.axis_index("dp"), 2)
        tail = w.at[lax.rem(rank + 2, 4), (pl.ds(2, 2), pl.ds(0, 4))[j], 1 - side, :, (pl.ds(0, OU), pl.ds(OU, FQ))[j]]
        return remote(tail, tail, wsend.at[j, 4], wrecv.at[j, 4], {"tensor": flip1(rank)})

    if with_w:
        weight_moves(0, lambda c: c.start(), lambda c: c.start(), lambda c: c.start())
    else:
        for j in (0, 1):
            whole_fill(j).start()
    sums_o[...] = jnp.zeros_like(sums_o)
    out_bias, outer_bias = (v[...].astype(f32).reshape(1, D) for v in (ob, fb))
    gains, shifts = ng[...].astype(f32), ns[...].astype(f32)
    gain1, gain2, shift1, shift2 = gains[0:1], gains[1:2], shifts[0:1], shifts[1:2]
    def weights_here(j):
        if with_w:
            weight_moves(j, lambda c: c.wait_recv(), None, None)
            weight_tail(j).start()
            weight_moves(j, None, lambda c: c.wait_recv(), lambda c: c.wait())
            weight_tail(j).wait_recv()
        else:
            whole_fill(j).wait()

    weights_here(0)
    for c in heads[0]:
        c.wait_recv()
    if with_w:
        weight_moves(1, lambda c: c.start(), lambda c: c.start(), lambda c: c.start())
    fill.wait()
    for c in rows_in:
        c.wait()
    for t in range(4):
        wt_s[t] = jnp.transpose(w[t, :, :, :, AT:OU].reshape(D, OU - AT))
    bias_in = [wt_s[t, QW:QW + 16].astype(f32)[0:1] for t in range(4)]
    w_in = lambda t: w[t, :, :, :, 0:FQ].reshape(D, FQ)
    w_ou = lambda t: w[t, :, :, :, OU:].reshape(D, FQ)

    def add_sum(i, rows):
        sums_o[i:i + 1] += jnp.sum(rows, axis=0, keepdims=True)

    def block(b, _):
        for i in range(1, NR):
            @pl.when(b == i)
            def _():
                for c in heads[i]:
                    c.wait_recv()
        rows = aligned(b, RB)
        start = inp[rows].astype(f32) + te[...].astype(f32)
        attn = out_bias
        for m in range(4):
            attn = attn + mm(mixr[m, :, rows], wt_s[ranks[m], :QW], TN)
        hidden, normed1, inv1 = layer_norm(start + attn, gain1, shift1)
        low = hidden.astype(bf)
        ht[:, rows] = low.T
        for t in range(4):
            u = mm(low, w_in(t)) + bias_in[t]
            value, slope = gelu_parts(u)
            act[t, rows] = value.astype(bf)
            slope_s[t] = slope.astype(bf)

        @pl.when(b == 0)
        def _():
            weights_here(1)
            for i in range(1, NR):
                for m in (3, 2, 1):
                    heads_in(i, m).start()

        mlp = outer_bias
        for t in range(4):
            mlp = mlp + mm(act[t, rows], w_ou(t), NT)
        final, normed2, inv2 = layer_norm(hidden + mlp, gain2, shift2)
        block_out[rows] = final.astype(bf)
        e = cot[rows].astype(f32)
        add_sum(0, e * normed2)
        add_sum(1, e)
        grad2 = norm_back(e, normed2, inv2, gain2)
        gm = grad2.astype(bf)
        gmt[:, rows] = gm.T
        add_sum(2, gm.astype(f32))
        gin = grad2
        for t in range(4):
            g = (mm(gm, w_ou(t)) * slope_s[t].astype(f32)).astype(bf)
            gp[t, rows] = g
            add_sum(6 + t, g.astype(f32))
            gin = gin + mm(g, w_in(t), NT)
        add_sum(3, gin * normed1)
        add_sum(4, gin)
        grad1 = norm_back(gin, normed1, inv1, gain1)
        grad1_o[rows] = grad1
        ga = grad1.astype(bf)
        gat_rows = ga.T
        gat[:, rows] = gat_rows
        add_sum(5, ga.astype(f32))
        for m in (3, 2, 1):
            gmix[m, :, rows] = mm(wt_s[ranks[m], :QW], gat_rows).astype(bf)
            heads_out(b, m).start()
        dots[0, :, rows] = mm(wt_s[r, :QW], gat_rows).astype(bf)
        return 0

    lax.fori_loop(0, NR, block, 0)

    if with_w:
        for j in (0, 1):
            weight_moves(j, lambda c: c.wait_send(), lambda c: c.wait_send(), None)
            weight_tail(j).wait_send()

    def grads(t, m):
        return (lambda: mm(ht[...], gp[t]), lambda: mm(gmt[...], act[t]), lambda: mm(gat[...], mixr[m], NT))

    cols = (slice(0, FQ), slice(OU, PK), slice(AT, AT + QW))
    blank = jnp.zeros((4, 2, 96, OU - AT - QW), bf)
    cut = lambda g: g.reshape(4, 2, 96, g.shape[1])

    def handing(q):
        return remote(w.at[q], both.at[q], gsend.at[q], grecv.at[q], core)

    hops = []

    def hop(n):
        if not with_w:
            return
        if n:
            hops[-1].wait_recv()
        step[n] = step[n - 1] + step[n + 3] if n else sums_o[...]
        hops.append(sends.go(step.at[n], step.at[n + 4], ssend.at[n], srecv.at[n], (core, devices[2], xx)[n]))

    hop(0)
    saves = [pltpu.make_async_copy(grad1_o, grad1_hbm, loc.at[21]), pltpu.make_async_copy(block_out, block_hbm, loc.at[22])]
    for c in saves:
        c.start()
    for q in (1, 0):
        for c, g in zip(cols, grads(ranks[2 * q + 1], 2 * q + 1)):
            w[q, :, :, :, c] = cut(g().astype(bf))
        w[q, :, :, :, AT + QW:OU] = blank
        handing(q).start()
        hop(2 - q)
    for q in (1, 0):
        mine = grads(ranks[2 * q], 2 * q)
        handing(q).wait_recv()
        for c, g in zip(cols, mine):
            both[q, :, :, :, c] = (both[q, :, :, :, c].astype(f32) + cut(g())).astype(bf)
        for n, side in ((0, x), (1, 1 - x)):
            to = ((p00, p01), (p10, p11))[q][n]
            saves.append(pltpu.make_async_copy(both.at[q, :, side], to, loc.at[6 + 2 * q + n]))
            saves[-1].start()
        if with_w and q:
            hops[-1].wait_recv()
            line_s[z] = step[2] + step[6]
            ends = [sends.go(line_s.at[z], line_s.at[z], ssend.at[2 + k], srecv.at[2 + k], zdev[k]) for k in (1, 2, 3)]
    if with_w:
        for c in ends:
            c.wait_recv()
        sums_o[...] = ((line_s[0] + line_s[1]) + line_s[2]) + line_s[3]
    for b in range(NR):
        for m in (1, 2, 3):
            heads_out(b, m).wait()
        for c in heads[b]:
            c.wait_send()
    saves.append(pltpu.make_async_copy(dots, dots_hbm, loc.at[10]))
    saves[-1].start()
    for c in saves:
        c.wait()
    for q in range(2):
        handing(q).wait_send()
    sends.drain()


def middle(weights, mix, *rest):
    sd = jax.ShapeDtypeStruct
    dma = pltpu.SemaphoreType.DMA
    with_w = len(weights) > 1
    vm = pltpu.VMEM
    tokens = (D, ROWS)
    extra = [vm((7, 16, D), f32), vm((4, 16, D), f32), dma((3,)), dma((3,)), dma((2, 5)), dma((2, 5)),
             dma((6,)), dma((6,))] if with_w else []
    return pl.pallas_call(
        functools.partial(middle_kernel, with_w),
        out_shape=(sd((ROWS, D), bf), sd((ROWS, D), f32), sd((4, QW, ROWS), bf),
                   *([sd((4, 96, PK), bf)] * 4), sd((16, D), f32)),
        in_specs=[HB] * len(weights) + [HB, HB, VM, HB] + [VM] * 4, out_specs=(HB, HB, HB, HB, HB, HB, HB, VM),
        scratch_shapes=[vm((ROWS, D), bf), vm((ROWS, D), bf), vm((ROWS, D), bf), vm((ROWS, D), f32),
                        vm((4, 4, 2, 96, PK), bf), vm((4, OU - AT, D), bf), vm((4, QW, ROWS), bf),
                        vm((4, QW, ROWS), bf), vm((4, QW, ROWS), bf), vm((4, QW, ROWS), bf),
                        vm((2, 4, 2, 96, PK), bf), vm(tokens, bf), vm(tokens, bf), vm(tokens, bf),
                        vm((4, ROWS, FQ), bf), vm((4, ROWS, FQ), bf), vm((4, RB, FQ), bf),
                        dma((23,)), dma((NR, 4)), dma((NR, 4)), dma((NR, 4)), dma((NR, 4)), dma((2,)), dma((2,))] + extra,
        compiler_params=pltpu.CompilerParams(collective_id=2, has_side_effects=True, vmem_limit_bytes=63 << 20),
        cost_estimate=pl.CostEstimate(flops=33_000_000_000, bytes_accessed=50_000_000, transcendentals=9_000_000),
        name="middle",
    )(*weights, mix, *rest)


def final_kernel(with_w, *refs):
    if with_w:
        (x_hbm, w_hbm, dqt_hbm, dkv_hbm, g1_hbm, m0_hbm, m1_hbm, m2_hbm, m3_hbm, out, pair, qo, mo,
         x_s, w_s, wr_s, dqt, dkv, grad1, part, crv, ysd, yrv, m0, m1, m2, m3, zsm, zrm, dwq, xrq, zsq, zrq,
         prv, psd, prs, loc, csend, crecv, ysend, yrecv, xsend, xrecv, zsend, zrecv) = refs
    else:
        (x_hbm, w_hbm, dqt_hbm, dkv_hbm, g1_hbm, out, pair, dw,
         x_s, w_s, wr_s, dqt, dkv, grad1, part, crv, ysd, yrv, loc, csend, crecv, ysend, yrecv) = refs
    pulls = [(w_hbm, w_s), (dqt_hbm, dqt), (dkv_hbm, dkv)]
    pulls += [(m0_hbm, m0), (m1_hbm, m1), (m2_hbm, m2), (m3_hbm, m3)] if with_w else []
    pulls += [(x_hbm, x_s), (g1_hbm, grad1)]
    loads = [pltpu.make_async_copy(a, b, loc.at[n]) for n, (a, b) in enumerate(pulls)]
    for c in loads[:-2]:
        c.start()
    r = lax.axis_index("tensor")
    d = lax.axis_index("dp")
    rc, ry = flip1(r), lax.rem(r + 2, 4)
    rd = 3 - r
    core, yy = {"tensor": rc}, {"tensor": ry}
    targets = [core, yy]
    if with_w:
        z, x = d // 2, lax.rem(d, 2)
        xo = 1 - x
        zs = [lax.rem(z + k, 4) for k in range(4)]
        xx = {"dp": flip1(d)}
        zdev = [{"dp": zs[k] * 2 + x} for k in range(4)]
        targets += [xx] + zdev[1:]
    meet(targets)
    sends = Sends()
    go = sends.go
    wait = lambda *which: [loads[n].wait() for n in which]
    rows = [pl.ds(i * CROWS, CROWS) for i in range(CH)]
    if with_w:
        wait(3, 4, 5, 6)
        zm = []
        for k in (1, 2, 3, 0):
            at = zs[k]
            zsm[k] = ((m0[at].astype(f32) + m1[at].astype(f32)) + (m2[at].astype(f32) + m3[at].astype(f32))).astype(bf)
            if k:
                zm.append(go(zsm.at[k], zrm.at[k - 1], zsend.at[1, k - 1], zrecv.at[1, k - 1], zdev[k]))
    wait(0, 1, 2)
    for c in loads[-2:]:
        c.start()
    w = w_s[...].reshape(D, 3 * QW)
    for h in range(HN):
        for c in (1, 2):
            wr_s[:, h * 128 + (c - 1) * HD:h * 128 + c * HD] = w[:, c * QW + h * HD:c * QW + (h + 1) * HD]
    wqs = w[:, :QW]

    def project_back(t, i):
        at = pl.ds(pl.multiple_of(t * ROWS + i * CROWS, CROWS), CROWS)
        part[t, rows[i]] = (mm(dqt[:, at], wqs, (((0,), (1,)), ((), ()))) + mm(dkv[at], wr_s[...], NT)).astype(bf)

    first, second, third = [], [], []
    for i in range(CH):
        project_back(rd, i)
        second.append(go(part.at[rd, rows[i]], crv.at[1, rows[i]], csend.at[1, i], crecv.at[1, i], core))
        project_back(ry, i)
        if i:
            second[i - 1].wait_recv()
            prev = rows[i - 1]
            ysd[prev] = (part[ry, prev].astype(f32) + crv[1, prev].astype(f32)).astype(bf)
            third.append(go(ysd.at[prev], yrv.at[prev], ysend.at[i - 1], yrecv.at[i - 1], yy))
    prev = rows[CH - 1]
    second[CH - 1].wait_recv()
    ysd[prev] = (part[ry, prev].astype(f32) + crv[1, prev].astype(f32)).astype(bf)
    third.append(go(ysd.at[prev], yrv.at[prev], ysend.at[CH - 1], yrecv.at[CH - 1], yy))

    wait(len(loads) - 2)
    whole = x_s[...].reshape(SEQ, D)
    aq = mm(dqt[...], whole)
    akv = mm(dkv[...], whole, TN)
    blocks = [aq]
    for c in (0, 1):
        blocks += [akv[h * 128 + c * HD:h * 128 + (c + 1) * HD] for h in range(HN)]
    dwt = jnp.concatenate(blocks, 0).T.astype(bf)
    sum_q = jnp.sum(dqt[...].astype(f32), axis=1, keepdims=True)
    sum_q = jnp.transpose(jnp.broadcast_to(sum_q, (QW, 8)))
    sum_kv = jnp.sum(dkv[...].astype(f32), axis=0, keepdims=True)
    sum_v = jnp.concatenate([sum_kv[:, h * 128 + HD:(h + 1) * 128] for h in range(HN)], 1)
    pairs = jnp.concatenate([sum_q[0:1], sum_v, jnp.zeros((6, QW), f32)], 0)
    if with_w:
        dwq[...] = dwt.reshape(dwq.shape)
        xq = go(dwq.at[:, xo], xrq, xsend.at[0], xrecv.at[0], xx)
        prs[...] = pairs
        px = go(prs, prv, xsend.at[1], xrecv.at[1], xx)
    for i in range(CH):
        project_back(rc, i)
        first.append(go(part.at[rc, rows[i]], crv.at[0, rows[i]], csend.at[0, i], crecv.at[0, i], core))
        project_back(r, i)
    if with_w:
        px.wait_recv()
        psd[z] = prs[...] + prv[...]
        zp = [go(psd.at[z], psd.at[z], zsend.at[2, k - 1], zrecv.at[2, k - 1], zdev[k]) for k in (1, 2, 3)]
        xq.wait_recv()
        for k in range(4):
            zsq[k] = (dwq[zs[k], x].astype(f32) + xrq[zs[k]].astype(f32)).astype(bf)
        zq = [go(zsq.at[k], zrq.at[k - 1], zsend.at[0, k - 1], zrecv.at[0, k - 1], zdev[k]) for k in (1, 2, 3)]
    else:
        dw[...] = dwt
        pair[...] = pairs
    wait(len(loads) - 1)
    for i in range(CH):
        first[i].wait_recv()
        third[i].wait_recv()
        out[rows[i]] = (part[r, rows[i]].astype(f32) + crv[0, rows[i]].astype(f32)
                        + yrv[rows[i]].astype(f32) + grad1[rows[i]]).astype(bf)
    if with_w:
        for c in zq:
            c.wait_recv()
        whole_q = (zsq[0].astype(f32) + zrq[0].astype(f32)) + (zrq[1].astype(f32) + zrq[2].astype(f32))
        qo[...] = whole_q
        for c in zp:
            c.wait_recv()
        pair[...] = ((psd[0] + psd[1]) + psd[2]) + psd[3]
        for c in zm:
            c.wait_recv()
        mo[...] = (zsm[0].astype(f32) + zrm[0].astype(f32)) + (zrm[1].astype(f32) + zrm[2].astype(f32))
    sends.drain()


def final(whole, w, dqt, dkv, grad1, *more):
    with_w = len(more) > 0
    dma = pltpu.SemaphoreType.DMA
    sd = jax.ShapeDtypeStruct
    vm = pltpu.VMEM
    rows = (ROWS, D)
    like = lambda a: vm(a.shape, a.dtype)
    shapes = [sd(rows, bf), sd((8, QW), f32)]
    args = [whole, w, dqt, dkv, grad1, *more]
    scratch = [like(whole), like(w), vm((D, 2 * QW), bf), like(dqt), like(dkv), like(grad1), vm((4,) + rows, bf),
               vm((2,) + rows, bf), vm(rows, bf), vm(rows, bf)]
    sems = [dma((9,)), dma((2, CH)), dma((2, CH)), dma((CH,)), dma((CH,))]
    if with_w:
        n = w.shape[1]
        shapes += [sd((n, 3 * QW), f32), sd((n, PK), f32)]
        scratch += [like(m) for m in more] + [vm((4, n, PK), bf), vm((3, n, PK), bf),
                    vm((4, 2, n, 3 * QW), bf), vm((4, n, 3 * QW), bf), vm((4, n, 3 * QW), bf), vm((3, n, 3 * QW), bf),
                    vm((8, QW), f32), vm((4, 8, QW), f32), vm((8, QW), f32)]
        sems += [dma((2,)), dma((2,)), dma((3, 3)), dma((3, 3))]
    else:
        shapes += [sd((D, 3 * QW), bf)]
    return pl.pallas_call(
        functools.partial(final_kernel, with_w),
        out_shape=shapes,
        in_specs=[HB] * len(args), out_specs=[VM] * len(shapes),
        scratch_shapes=scratch + sems,
        compiler_params=pltpu.CompilerParams(
            collective_id=1, has_side_effects=True, vmem_limit_bytes=60 << 20),
        name="final",
    )(*args)


def emit_kernel(*refs):
    sources, outs, kept, sem = refs[:5], refs[5:16], refs[16:21], refs[21]
    loads = [pltpu.make_async_copy(a, b, sem.at[n]) for n, (a, b) in enumerate(zip(sources, kept))]
    for c in loads:
        c.start()
    input_grad, qkv_o, pair_o, out_o, out_b, inner_o, inner_b, outer_o, outer_b, gain_o, shift_o = outs
    save = pltpu.make_async_copy(kept[0], input_grad, sem.at[5])
    loads[0].wait()
    save.start()
    for c in loads[1:]:
        c.wait()
    pair, qkv, share, sums = kept[1:]
    for c in range(3):
        qkv_o[c] = qkv[:, c * QW:(c + 1) * QW]
    pair_o[...] = pair[0:2]
    inner_o[...] = share[:, 0:FQ]
    outer_o[...] = share[:, OU:]
    out_o[...] = share[:, AT:OU].T[:QW]
    out_b[...] = sums[5]
    inner_b[...] = sums[6 + lax.axis_index("tensor")]
    outer_b[...] = sums[2]
    gain_o[...] = jnp.concatenate([sums[3:4], sums[0:1]], 0)
    shift_o[...] = jnp.concatenate([sums[4:5], sums[1:2]], 0)
    save.wait()


def emit(*arrays):
    sd = jax.ShapeDtypeStruct
    n = arrays[3].shape[0]
    rows = sd((ROWS, D), bf)
    vec = sd((D,), f32)
    shapes = (rows, sd((3, n, QW), f32), sd((2, QW), f32), sd((QW, n), f32), vec, sd((n, FQ), f32), vec,
              sd((n, FQ), f32), vec, sd((2, D), f32), sd((2, D), f32))
    return pl.pallas_call(
        emit_kernel, out_shape=shapes, in_specs=[HB] * 5, out_specs=(HB,) + (VM,) * 10,
        scratch_shapes=[pltpu.VMEM(a.shape, a.dtype) for a in arrays] + [pltpu.SemaphoreType.DMA((6,))],
        compiler_params=pltpu.CompilerParams(vmem_limit_bytes=60 << 20),
        name="emit",
    )(*arrays)


def add_low(a, b):
    return (a.astype(f32) + b.astype(f32)).astype(bf)


def on_device(
    ring, input_rows, time_embed, parents, qkv_weight, qv_bias, out_weight, out_bias, inner_weight,
    inner_bias, outer_weight, outer_bias, norm_gain, norm_shift, cotangent,
):
    rank = lax.axis_index("tensor")
    dpos = lax.axis_index("dp")
    part = qkv_weight.shape[0]
    own_ring = ring == 8

    if own_ring:
        whole, w_all, gz, half = gather_start(
            input_rows, time_embed, jnp.transpose(qkv_weight, (1, 0, 2)), inner_weight, outer_weight.T, out_weight,
            inner_bias)
        diagonal = [(i * 4 + j, (i ^ 1) * 4 + (j ^ 2)) for i in range(8) for j in range(4)]
        cross = lambda a: lax.ppermute(a, ("dp", "tensor"), diagonal)
        weights = [gz, across_x(gz), partner(gz, 2), cross(half)]
    else:
        whole = gather_start(input_rows, time_embed)[0]
        w_all = lax.all_gather(qkv_weight.reshape(part, 3 * QW), "dp", axis=0, tiled=True).reshape(8, 96, 3 * QW)
        bias_part = lax.dynamic_slice_in_dim(inner_bias, dpos * part, part, 0)
        packed = jnp.concatenate([inner_weight, out_weight.T, bias_part[:, None],
                                  jnp.zeros((part, OU - AT - QW - 1), bf), outer_weight.T], axis=1)
        packed = lax.all_gather(packed, "dp", axis=0, tiled=True)
        weights = [lax.all_gather(packed, "tensor", axis=0, tiled=False).reshape(4, 4, 2, 96, PK)]

    qt, kv, kt, ot, mix, lse, pairs = attn_fwd(parents, whole, w_all, qv_bias)
    block_out, grad1, dots, *parts, sums = middle(
        weights, mix, input_rows, time_embed, cotangent, out_bias, outer_bias, norm_gain, norm_shift)
    if own_ring:
        parts = [parts[0], across_x(parts[1]), partner(parts[2], 2), cross(parts[3])]
    else:
        far = [partner(parts[2], 2), partner(parts[3], 2)]
    dqt, dkv, block_out = attn_bwd((0, 1, 2), pairs, qt, kv, kt, dots, ot, lse, block_out)
    if own_ring:
        input_grad, pair, qkv_share, share = final(whole, w_all, dqt, dkv, grad1, *parts)
        (input_grad, qkv_share, pair, out_share, out_sum, inner_share, inner_sum, outer_share, outer_sum,
         gains, shifts) = emit(input_grad, pair, qkv_share, share, sums)
        return (block_out, input_grad, jnp.transpose(qkv_share, (1, 0, 2)), pair, out_share, out_sum,
                inner_share, inner_sum, outer_share.T, outer_sum, gains, shifts)
    else:
        input_grad, pair, dwq = final(whole, w_all, dqt, dkv, grad1)
        own, other = add_low(parts[0], far[0]), add_low(parts[1], far[1])
        even = dpos % 2 == 0
        mine = jnp.stack([jnp.where(even, own, other), jnp.where(even, other, own)], axis=1).reshape(D, PK)
        share = lax.psum_scatter(mine, "dp", scatter_dimension=0, tiled=True).astype(f32)
        qkv_share = lax.psum_scatter(dwq, "dp", scatter_dimension=0, tiled=True).astype(f32).reshape(part, 3, QW)
        pair = lax.psum(pair, "dp")
        sums = jnp.sum(lax.all_gather(sums, ("dp", "tensor"), axis=0, tiled=False), axis=0)
    return (
        block_out,
        input_grad,
        qkv_share,
        pair[:2],
        share[:, AT:AT + QW].T,
        sums[5],
        share[:, :FQ],
        lax.dynamic_index_in_dim(sums[6:10], rank, 0, keepdims=False),
        share[:, OU:].T,
        sums[2],
        jnp.stack([sums[3], sums[0]]),
        jnp.stack([sums[4], sums[1]]),
    )


def solution(mesh):
    both = P(("dp", "tensor"), None)
    return jax.shard_map(
        functools.partial(on_device, mesh.shape["dp"]),
        mesh=mesh,
        in_specs=(
            both, P("dp", None), P("dp", None), P("dp", None, "tensor"), P(None, "tensor"),
            P("tensor", "dp"), P(), P("dp", "tensor"), P("tensor"), P("tensor", "dp"), P(), P(), P(), both,
        ),
        out_specs=(
            both, both, P("dp", None, "tensor"), P(None, "tensor"), P("tensor", "dp"), P(),
            P("dp", "tensor"), P("tensor"), P("tensor", "dp"), P(), P(), P(),
        ),
        check_vma=False,
    )
```
